512 devices in a mesh: grid: 64 (over y_lo, z, core), dp: 8 (over y_hi, x).
Axes of the slice: x: 4, y: 4 (y_hi: 2, y_lo: 2; y = y_hi * 2 + y_lo), z: 16, core: 2. Of those that a mesh axis runs over, the one named last changes fastest.
Arguments:
- field: bfloat16 [65536, 1024], P('grid', 'dp'), may hold values from -6 to 6
- cotangent: bfloat16 [65536, 1024], P('grid', 'dp'), may hold values from -6 to 6
- mode_blocks: int32 [8], replicated, may hold values from 0 to 4095, as said below
- spectral: bfloat16 [2, 64, 64, 64], P(None, 'grid'), may hold values from -6 to 6
- w_in: bfloat16 [64, 256], replicated, may hold values from -0.75 to 0.75
- b_in: float32 [256], replicated, may hold values from -3 to 3
- w_out: bfloat16 [256, 64], replicated, may hold values from -0.375 to 0.375
- b_out: float32 [64], replicated, may hold values from -3 to 3
Outputs:
- output: bfloat16 [65536, 1024], P('grid', 'dp')
- field_grad: bfloat16 [65536, 1024], P('grid', 'dp')
- spectral_grad: float32 [2, 64, 64, 64], P(None, 'grid')
- w_in_grad: float32 [64, 256], replicated
- b_in_grad: float32 [256], replicated
- w_out_grad: float32 [256, 64], replicated
- b_out_grad: float32 [64], replicated
The draws below stay inside these ranges and needn't reach their ends.
Inputs may be any that keep to these rules, and one draw needn't show every extreme that they name: `mode_blocks`: distinct block numbers; 0 and 4095 are always among them.
All inputs are finite; a program needn't handle non-finite values.
Results may differ from the reference program's by a relative error of at most 0.013.
Values may be sent and summed in bfloat16 or wider, within the bound.
No kernel may reach another device: no remote copies, remote signals or barrier semaphores. Data moves between devices by JAX's collectives and lax.ppermute only.
A program may use at most 64 MiB of HBM per device.

```python
import math
import jax
import jax.numpy as jnp
from jax import lax

NX = 65536
C = 64
HID = 256
BLK = 8
KB = 8
KM = 64
NBLK = 4096
WIDE = 1024


def draw_mode_blocks(key, part):
    inner = jax.random.permutation(jax.random.fold_in(key, 11), NBLK - 2)[:KB - 2].astype(jnp.int32) + 1
    chosen = jnp.concatenate([jnp.zeros((1,), jnp.int32), inner, jnp.full((1,), NBLK - 1, jnp.int32)])
    return jax.random.permutation(jax.random.fold_in(key, 12), chosen).astype(jnp.int32)


def levels(rng, shape, cuts, least, top_value):
    factor_of, own = 1.0, jax.random.fold_in(rng, 6)
    for position, parts in cuts:
        draws = jnp.exp(jax.random.uniform(jax.random.fold_in(own, position), (parts,), jnp.float32, least / len(cuts), top_value / len(cuts)))
        factor_of = factor_of * jnp.repeat(draws, shape[position] // parts).reshape([-1 if axis == position else 1 for axis in range(len(shape))])
    return factor_of


def bell_draw(key, extent, spread, reach, split=(), kind=jnp.bfloat16):
    values = jax.random.normal(key, extent, jnp.float32) * spread
    if len(split) > 0:
        values = levels(key, extent, split, -0.22, 0.18) * values
    return jnp.clip(values, min=-reach, max=reach).astype(kind)


def setup_inputs(seed: int = 0) -> dict:
    splits = jax.random.split(jax.random.key(seed), 9)
    field = bell_draw(splits[0], (NX, WIDE), 1.0, 6.0, ((0, 64), (1, 8)))
    cotangent = bell_draw(splits[1], (NX, WIDE), 1.0, 6.0, ((0, 64), (1, 8)))
    mode_blocks = draw_mode_blocks(jax.random.fold_in(splits[8], 71), 0)
    spectral = bell_draw(splits[3], (2, KM, C, C), (max(1, 2 * KM * C // NX)) ** -0.5, 6.0, ((1, 64),))
    w_in = bell_draw(splits[4], (C, HID), C ** -0.5, 0.75)
    b_in = bell_draw(splits[5], (HID,), 0.5, 3.0, (), jnp.float32)
    w_out = bell_draw(splits[6], (HID, C), HID ** -0.5, 0.375)
    b_out = bell_draw(splits[7], (C,), 0.5, 3.0, (), jnp.float32)
    return {"field": field, "cotangent": cotangent, "mode_blocks": mode_blocks, "spectral": spectral, "w_in": w_in, "b_in": b_in, "w_out": w_out, "b_out": b_out}


def mode_list(mode_blocks, block_width):
    offsets = jnp.arange(block_width, dtype=jnp.int32)
    return (mode_blocks.astype(jnp.int32)[:, None] * block_width + offsets[None, :]).reshape(-1)

def forward_table(modes, first_row, count, length):
    rows_here = first_row + jnp.arange(count, dtype=jnp.int32)
    product = modes[:, None] * rows_here[None, :] % length
    phase = product.astype(jnp.float32) * (2.0 * math.pi / length)
    scale = 1.0 / math.sqrt(length)
    table = jnp.stack([jnp.cos(phase) * scale, -jnp.sin(phase) * scale], axis=1)
    return table.reshape(2 * modes.shape[0], count).astype(jnp.bfloat16)

def inverse_table(forward):
    return (forward.astype(jnp.float32) * 2.0).astype(jnp.bfloat16).T

def gelu_grad(pre):
    _, pull = jax.vjp(jax.nn.gelu, pre)
    return pull(jnp.ones_like(pre))[0]

def mix(real, imag, weight_re, weight_im):
    best = lax.Precision.HIGHEST
    out_re = jnp.einsum('kbi,kio->kbo', real, weight_re, precision=best) - jnp.einsum('kbi,kio->kbo', imag, weight_im, precision=best)
    out_im = jnp.einsum('kbi,kio->kbo', real, weight_im, precision=best) + jnp.einsum('kbi,kio->kbo', imag, weight_re, precision=best)
    return (out_re, out_im)

def mix_grads(real, imag, grad_re, grad_im, weight_re, weight_im):
    best = lax.Precision.HIGHEST
    w_re = jnp.einsum('kbi,kbo->kio', real, grad_re, precision=best) + jnp.einsum('kbi,kbo->kio', imag, grad_im, precision=best)
    w_im = jnp.einsum('kbi,kbo->kio', real, grad_im, precision=best) - jnp.einsum('kbi,kbo->kio', imag, grad_re, precision=best)
    in_re = jnp.einsum('kbo,kio->kbi', grad_re, weight_re, precision=best) + jnp.einsum('kbo,kio->kbi', grad_im, weight_im, precision=best)
    in_im = jnp.einsum('kbo,kio->kbi', grad_im, weight_re, precision=best) - jnp.einsum('kbo,kio->kbi', grad_re, weight_im, precision=best)
    return (w_re, w_im, in_re, in_im)

def pointwise_pass(field, spec, cotangent, w_in, b_in, w_out, b_out):
    chans = w_in.shape[0]
    shape = field.shape
    spec_rows = spec.reshape(-1, chans)
    pre = jnp.dot(spec_rows, w_in, preferred_element_type=jnp.float32) + b_in
    hidden = jax.nn.gelu(pre).astype(jnp.bfloat16)
    out = jnp.dot(hidden, w_out, preferred_element_type=jnp.float32) + b_out
    result = (field.reshape(-1, chans).astype(jnp.float32) + out).astype(jnp.bfloat16).reshape(shape)
    upstream = cotangent.reshape(-1, chans)
    grad_w_out = jnp.einsum('nh,nc->hc', hidden, upstream, preferred_element_type=jnp.float32)
    grad_b_out = lax.optimization_barrier(jnp.sum(upstream.astype(jnp.float32), axis=0))
    grad_hidden = jnp.einsum('nc,hc->nh', upstream, w_out, preferred_element_type=jnp.float32)
    grad_pre = (grad_hidden * gelu_grad(pre)).astype(jnp.bfloat16)
    grad_w_in = jnp.einsum('nc,nh->ch', spec_rows, grad_pre, preferred_element_type=jnp.float32)
    grad_b_in = lax.optimization_barrier(jnp.sum(grad_pre.astype(jnp.float32), axis=0))
    grad_spec = jnp.einsum('nh,ch->nc', grad_pre, w_in, preferred_element_type=jnp.float32).astype(jnp.bfloat16).reshape(shape)
    return (result, grad_spec, (grad_w_in, grad_b_in, grad_w_out, grad_b_out))

def layer_block(field, cotangent, forward, weight_re, weight_im, w_in, b_in, w_out, b_out):
    chans = w_in.shape[0]
    width = field.shape[1]
    ncol = width // chans
    kmodes = forward.shape[0] // 2
    modal = jnp.dot(forward, field, preferred_element_type=jnp.float32).reshape(kmodes, 2, ncol, chans)
    real = modal[:, 0]
    imag = modal[:, 1]
    out_re, out_im = mix(real, imag, weight_re, weight_im)
    mixed = jnp.stack([out_re, out_im], axis=1).reshape(2 * kmodes, width).astype(jnp.bfloat16)
    inverse = inverse_table(forward)
    spec = jnp.dot(inverse, mixed, preferred_element_type=jnp.float32).astype(jnp.bfloat16)
    result, grad_spec, sums = pointwise_pass(field, spec, cotangent, w_in, b_in, w_out, b_out)
    grad_modal = jnp.einsum('rm,rw->mw', inverse, grad_spec, preferred_element_type=jnp.float32).reshape(kmodes, 2, ncol, chans)
    w_re, w_im, in_re, in_im = mix_grads(real, imag, grad_modal[:, 0], grad_modal[:, 1], weight_re, weight_im)
    grad_in = jnp.stack([in_re, in_im], axis=1).reshape(2 * kmodes, width).astype(jnp.bfloat16)
    back = jnp.einsum('mr,mw->rw', forward, grad_in, preferred_element_type=jnp.float32)
    grad_field = (cotangent.astype(jnp.float32) + back).astype(jnp.bfloat16)
    return (result, grad_field, sums + (w_re, w_im))

def reference(field, cotangent, mode_blocks, spectral, w_in, b_in, w_out, b_out):
    chans = w_in.shape[0]
    hidden_units = w_in.shape[1]
    modes = mode_list(mode_blocks, BLK)
    kmodes = modes.shape[0]
    forward = forward_table(modes, jnp.int32(0), NX, NX)
    weight_re = spectral[0].astype(jnp.float32)
    weight_im = spectral[1].astype(jnp.float32)
    columns = field.shape[1] // chans
    group = 8
    nblocks = columns // group
    block_width = group * chans
    fields = field.reshape(NX, nblocks, block_width).transpose(1, 0, 2)
    cots = cotangent.reshape(NX, nblocks, block_width).transpose(1, 0, 2)
    init = (jnp.zeros((chans, hidden_units), jnp.float32), jnp.zeros((hidden_units,), jnp.float32), jnp.zeros((hidden_units, chans), jnp.float32), jnp.zeros((chans,), jnp.float32), jnp.zeros((kmodes, chans, chans), jnp.float32), jnp.zeros((kmodes, chans, chans), jnp.float32))

    def advance(carry, pair):
        result, grad_field, sums = layer_block(pair[0], pair[1], forward, weight_re, weight_im, w_in, b_in, w_out, b_out)
        return (tuple((a + b for a, b in zip(carry, sums))), (result, grad_field))
    sums, (results, grads) = lax.scan(advance, init, (fields, cots))
    output = results.transpose(1, 0, 2).reshape(NX, columns * chans)
    field_grad = grads.transpose(1, 0, 2).reshape(NX, columns * chans)
    inv_cols = 1.0 / columns
    spectral_grad = jnp.stack([sums[4], sums[5]], axis=0) * inv_cols
    return (output, field_grad, spectral_grad, sums[0] * inv_cols, sums[1] * inv_cols, sums[2] * inv_cols, sums[3] * inv_cols)
```

```python
import math

import jax
import jax.numpy as jnp
from jax import lax
from jax.sharding import PartitionSpec as P

NX = 65536
BLK = 8


def mode_list(mode_blocks, block_width):
    offsets = jnp.arange(block_width, dtype=jnp.int32)
    return (mode_blocks[:, None] * block_width + offsets[None, :]).reshape(-1)


def forward_table(modes, first_row, count, length):
    rows_here = first_row + jnp.arange(count, dtype=jnp.int32)
    product = modes[:, None] * rows_here[None, :] % length
    phase = product.astype(jnp.float32) * (2.0 * math.pi / length)
    scale = 1.0 / math.sqrt(length)
    table = jnp.stack([jnp.cos(phase) * scale, -jnp.sin(phase) * scale], axis=1)
    return table.reshape(2 * modes.shape[0], count).astype(jnp.bfloat16)


def gelu_grad(pre):
    _, pull = jax.vjp(jax.nn.gelu, pre)
    return pull(jnp.ones_like(pre))[0]


def exchange(x, axis):
    return lax.all_to_all(x, axis, 0, 0, tiled=True)


def complex_mix(real, imag, weight_re, weight_im):
    best = lax.Precision.HIGHEST
    left = jnp.concatenate([real, imag], axis=0)
    by_re = jnp.dot(left, weight_re, precision=best)
    by_im = jnp.dot(left, weight_im, precision=best)
    n = real.shape[0]
    return by_re[:n] - by_im[n:], by_im[:n] + by_re[n:]


def complex_outer(real, imag, grad_re, grad_im):
    best = lax.Precision.HIGHEST
    w_re = jnp.dot(real.T, grad_re, precision=best) + jnp.dot(imag.T, grad_im, precision=best)
    w_im = jnp.dot(real.T, grad_im, precision=best) - jnp.dot(imag.T, grad_re, precision=best)
    return w_re, w_im


def local(field, cotangent, mode_blocks, spectral, w_in, b_in, w_out, b_out):
    rows, width = field.shape
    chans, hid = w_in.shape
    ncol = width // chans
    grid = lax.axis_size("grid")
    dp = lax.axis_size("dp")
    modes = mode_list(mode_blocks, BLK)
    first = lax.axis_index("grid") * rows
    table = forward_table(modes, first, rows, NX)
    twice = (table.astype(jnp.float32) * 2.0).astype(jnp.bfloat16)
    weight_re = spectral[0, 0].astype(jnp.float32)
    weight_im = spectral[1, 0].astype(jnp.float32)

    modal = jnp.dot(table, field, preferred_element_type=jnp.float32)
    modal = jnp.sum(exchange(modal.reshape(grid, 2, width), "grid"), axis=0)
    real = modal[0].reshape(ncol, chans)
    imag = modal[1].reshape(ncol, chans)
    out_re, out_im = complex_mix(real, imag, weight_re, weight_im)
    mixed = jnp.stack([out_re.reshape(width), out_im.reshape(width)]).astype(jnp.bfloat16)
    piece = exchange(jnp.broadcast_to(mixed[None], (grid, 2, width)), "grid").reshape(2 * grid, width)

    spec = jnp.einsum("mr,mw->rw", twice, piece, preferred_element_type=jnp.float32).astype(jnp.bfloat16)
    spec_rows = spec.reshape(-1, chans)
    pre = jnp.dot(spec_rows, w_in, preferred_element_type=jnp.float32) + b_in
    hidden = jax.nn.gelu(pre).astype(jnp.bfloat16)
    out = jnp.dot(hidden, w_out, preferred_element_type=jnp.float32) + b_out
    output = (field.astype(jnp.float32) + out.reshape(field.shape)).astype(jnp.bfloat16)
    upstream = cotangent.reshape(-1, chans)
    grad_w_out = jnp.einsum("nh,nc->hc", hidden, upstream, preferred_element_type=jnp.float32)
    grad_b_out = jnp.sum(upstream.astype(jnp.float32), axis=0)
    grad_hidden = jnp.einsum("nc,hc->nh", upstream, w_out, preferred_element_type=jnp.float32)
    grad_pre = (grad_hidden * gelu_grad(pre)).astype(jnp.bfloat16)
    grad_w_in = jnp.einsum("nc,nh->ch", spec_rows, grad_pre, preferred_element_type=jnp.float32)
    grad_b_in = jnp.sum(grad_pre.astype(jnp.float32), axis=0)
    grad_spec = (
        jnp.einsum("nh,ch->nc", grad_pre, w_in, preferred_element_type=jnp.float32)
        .astype(jnp.bfloat16)
        .reshape(field.shape)
    )
    grad_modal = jnp.dot(twice, grad_spec, preferred_element_type=jnp.float32)

    biases = jnp.concatenate([grad_b_in, grad_b_out]).reshape(grid, 1, -1)
    biases = jnp.pad(biases, ((0, 0), (0, 0), (0, width - biases.shape[2])))
    parts = jnp.concatenate(
        [
            grad_modal.reshape(grid, 2, width),
            grad_w_in.reshape(grid, -1, width),
            grad_w_out.reshape(grid, -1, width),
            biases,
        ],
        axis=1,
    )
    sums = jnp.sum(exchange(parts, "grid"), axis=0)
    d_re = sums[0].reshape(ncol, chans)
    d_im = sums[1].reshape(ncol, chans)
    w_re, w_im = complex_outer(real, imag, d_re, d_im)
    in_re, in_im = complex_mix(d_re, d_im, weight_re.T, -weight_im.T)

    feed = sums[2:]
    high = lax.reduce_precision(feed, 8, 7)
    low = feed - high
    share = jnp.concatenate(
        [
            w_re.reshape(-1, width).astype(jnp.bfloat16),
            w_im.reshape(-1, width).astype(jnp.bfloat16),
            high.astype(jnp.bfloat16),
            low.astype(jnp.bfloat16),
        ],
        axis=0,
    )
    shares = exchange(jnp.broadcast_to(share[None], (dp,) + share.shape), "dp")
    total = jnp.sum(shares.astype(jnp.float32), axis=0)
    inv_cols = 1.0 / (ncol * dp)
    nspec = 2 * chans * chans // width
    spectral_grad = (total[:nspec] * inv_cols).reshape(2, 1, chans, chans)
    nfeed = feed.shape[0]
    feed = (total[nspec : nspec + nfeed] + total[nspec + nfeed :]) * inv_cols

    own = jnp.concatenate(
        [jnp.stack([in_re.reshape(width), in_im.reshape(width)]), feed], axis=0
    ).astype(jnp.bfloat16)
    every = exchange(jnp.broadcast_to(own[None], (grid,) + own.shape), "grid")
    grad_in = every[:, :2].reshape(2 * grid, width)
    back = jnp.einsum("mr,mw->rw", table, grad_in, preferred_element_type=jnp.float32)
    field_grad = (cotangent.astype(jnp.float32) + back).astype(jnp.bfloat16)
    nrow = chans * hid // (grid * width)
    feeds = every[:, 2:].astype(jnp.float32)
    w_in_grad = feeds[:, :nrow].reshape(chans, hid)
    w_out_grad = feeds[:, nrow : 2 * nrow].reshape(hid, chans)
    flat = feeds[:, 2 * nrow, : (hid + chans) // grid].reshape(-1)
    return (output, field_grad, spectral_grad, w_in_grad, flat[:hid], w_out_grad, flat[hid:])


def solution(mesh):
    in_specs = (
        P("grid", "dp"),
        P("grid", "dp"),
        P(),
        P(None, "grid", None, None),
        P(),
        P(),
        P(),
        P(),
    )
    out_specs = (P("grid", "dp"), P("grid", "dp"), P(None, "grid", None, None), P(), P(), P(), P())
    return jax.shard_map(local, mesh=mesh, in_specs=in_specs, out_specs=out_specs, check_vma=False)
```

```python
import functools
import math

import jax
import jax.numpy as jnp
from jax import lax
from jax.experimental import pallas as pl
from jax.experimental.pallas import tpu as pltpu
from jax.sharding import PartitionSpec as P

NX = 65536
BLK = 8
LANES = 128
TILE = 8
F32 = jnp.float32
BF16 = jnp.bfloat16
VMEM = pl.BlockSpec(memory_space=pltpu.VMEM)
SMEM = pl.BlockSpec(memory_space=pltpu.SMEM)


def call(kernel, name, outs, specs, scratch=()):
    return pl.pallas_call(
        kernel,
        name=name,
        out_shape=[jax.ShapeDtypeStruct(shape, dtype) for shape, dtype in outs],
        in_specs=specs,
        out_specs=[VMEM] * len(outs),
        scratch_shapes=list(scratch),
        compiler_params=pltpu.CompilerParams(vmem_limit_bytes=48 << 20),
    )


def dot(a, b):
    return jnp.dot(a, b, preferred_element_type=F32)


def row_id(shape):
    return lax.broadcasted_iota(jnp.int32, shape, 0)


def every(ref, start, count, step):
    return ref[pl.ds(start, count, stride=step), :]


def cos_sin(turn):
    quarter = NX // 4
    quad = (turn + quarter // 2) >> (quarter.bit_length() - 1)
    rest = (turn - quad * quarter).astype(F32) * (2.0 * math.pi / NX)
    sq = rest * rest
    sin = rest * (1.0 + sq * (-1 / 6 + sq * (1 / 120 + sq * (-1 / 5040 + sq * (1 / 362880)))))
    cos = 1.0 + sq * (
        -1 / 2 + sq * (1 / 24 + sq * (-1 / 720 + sq * (1 / 40320 + sq * (-1 / 3628800))))
    )
    odd = (quad & 1) == 1
    c = jnp.where(odd, sin, cos)
    s = jnp.where(odd, cos, sin)
    return jnp.where(((quad + 1) & 2) != 0, -c, c), jnp.where((quad & 2) != 0, -s, s)


def modal_kernel(blocks_ref, first_ref, field_ref, modal_ref, table_ref):
    kblocks = blocks_ref.shape[0]
    count = kblocks * BLK
    rows = field_ref.shape[0]
    base = jnp.concatenate(
        [jnp.full((BLK, LANES), blocks_ref[b] * BLK, jnp.int32) for b in range(kblocks)], axis=0
    )
    modes = base + row_id((count, LANES)) % BLK
    lane = lax.broadcasted_iota(jnp.int32, (count, LANES), 1)
    scale = 1.0 / math.sqrt(NX)
    near_c, near_s = cos_sin((modes * lane) & (NX - 1))
    near_c, near_s = near_c * scale, near_s * scale
    far_c, far_s = cos_sin((modes * (first_ref[0] + lane * LANES)) & (NX - 1))
    for a in range(rows // LANES):
        ca = jnp.broadcast_to(far_c[:, a : a + 1], (count, LANES))
        sa = jnp.broadcast_to(far_s[:, a : a + 1], (count, LANES))
        span = pl.ds(a * LANES, LANES)
        table_ref[:count, span] = (near_c * ca - near_s * sa).astype(BF16)
        table_ref[count:, span] = (-(near_s * ca + near_c * sa)).astype(BF16)
    modal = dot(table_ref[...], field_ref[...])
    modal_ref[pl.ds(0, count, stride=2), :] = modal[:count]
    modal_ref[pl.ds(1, count, stride=2), :] = modal[count:]


def complex_rows(x, weights, sign):
    high = x.astype(BF16).astype(F32)
    rest = x - high
    mid = rest.astype(BF16).astype(F32)
    low = rest - mid
    row = row_id(x.shape)
    left = jnp.where(row < 2, high, jnp.where(row < 4, mid, jnp.where(row < 6, low, 0.0)))
    y = dot(left.astype(BF16), weights)
    y = y + pltpu.roll(y, 4, 0)
    y = y + pltpu.roll(y, 2, 0)
    by_re = y[:, :LANES]
    by_im = pltpu.roll(y[:, LANES:], 1, 0)
    return by_re + jnp.where(row % 2 == 0, sign, -sign) * by_im


def mix_kernel(recv_ref, weights_ref, out_ref, sum_ref):
    x = jnp.sum(recv_ref[...].reshape(-1, TILE, LANES), axis=0)
    x = x + pltpu.roll(x, 4, 0)
    x = x + pltpu.roll(x, 2, 0)
    sum_ref[...] = x
    mixed = complex_rows(x, weights_ref[...], -1.0)
    out_ref[...] = jnp.concatenate([mixed] * (out_ref.shape[0] // TILE), axis=0).astype(BF16)


def gelu_pair(pre):
    k = math.sqrt(2.0 / math.pi)
    sq = pre * pre
    t = jnp.tanh(pre * (k + (0.044715 * k) * sq))
    half = 0.5 * pre
    up = 1.0 + t
    return half * up, up * (0.5 + half * (1.0 - t) * (k + (3 * 0.044715 * k) * sq))


def cells_kernel(
    chunk,
    piece_ref,
    table_ref,
    table_t_ref,
    field_ref,
    cot_ref,
    cot_t_ref,
    win_ref,
    win_t_ref,
    bin_ref,
    wout_ref,
    wout_t_ref,
    bout_ref,
    out_ref,
    parts_ref,
    wide_ref,
    hidden_ref,
    gpre_ref,
    gspec_ref,
):
    rows = field_ref.shape[0]
    count = table_ref.shape[0] // 2
    hid = bin_ref.shape[1] // 2
    chans = LANES // 2
    wide_ref[...] = piece_ref[...].astype(F32)
    mixed = jnp.concatenate([every(wide_ref, 0, count, 2), every(wide_ref, 1, count, 2)], axis=0)
    mixed_t = mixed.T.astype(BF16)
    mixed = mixed.astype(BF16)
    for i in range(rows // chunk):
        span = pl.ds(i * chunk, chunk)
        spec = (2.0 * dot(table_t_ref[span, :], mixed)).astype(BF16)
        pre = dot(spec, win_ref[...]) + bin_ref[...]
        gate, slope = gelu_pair(pre)
        hidden = gate.astype(BF16)
        hidden_ref[span, :] = hidden
        gpre = (dot(cot_ref[span, :], wout_t_ref[...]) * slope).astype(BF16)
        gpre_ref[span, :] = gpre
        gspec_ref[span, :] = dot(gpre, win_t_ref[...]).astype(BF16)
        out = dot(hidden, wout_ref[...]) + bout_ref[...]
        out_ref[span, :] = (field_ref[span, :].astype(F32) + out).astype(BF16)
    spec_t = (2.0 * dot(mixed_t, table_ref[...])).astype(BF16)
    ones = jnp.ones((2 * TILE, rows), BF16)
    by_in = dot(jnp.concatenate([spec_t, ones], axis=0), gpre_ref[...])
    by_out = dot(cot_t_ref[...], hidden_ref[...])
    grad_modal = 2.0 * dot(table_ref[...], gspec_ref[...])
    sums_out = dot(ones, cot_ref[...])
    g_in = by_in[:chans, :hid] + by_in[chans:LANES, hid:]
    g_out = by_out[:chans, :hid] + by_out[chans:, hid:]
    b_in = by_in[LANES : LANES + 1, :hid] + by_in[LANES : LANES + 1, hid:]
    b_out = (sums_out + pltpu.roll(sums_out, chans, 1))[:1]
    row = row_id((count, LANES))
    bias = jnp.where(
        row == 0,
        b_in[:, :LANES],
        jnp.where(row == 1, b_in[:, LANES:], jnp.where(row == 2, b_out, 0.0)),
    )
    for r, block in enumerate(
        (
            grad_modal[:count],
            grad_modal[count:],
            g_in[:, :LANES],
            g_in[:, LANES:],
            g_out[:, :LANES],
            g_out[:, LANES:],
            bias,
            jnp.zeros((count, LANES), F32),
        )
    ):
        parts_ref[pl.ds(r, count, stride=TILE), :] = block


def share_kernel(recv_ref, modal_ref, share_ref, sum_ref):
    x = jnp.sum(recv_ref[...].astype(F32).reshape(-1, TILE, LANES), axis=0)
    sum_ref[...] = x
    both = jnp.concatenate([x, modal_ref[...]], axis=0)
    share_ref[...] = jnp.concatenate([both] * (share_ref.shape[0] // (2 * TILE)), axis=0)


def grad_in_kernel(sum_ref, weights_ref, out_ref):
    x = jnp.where(row_id((TILE, LANES)) < 2, sum_ref[...], 0.0)
    x = x + pltpu.roll(x, 4, 0)
    x = x + pltpu.roll(x, 2, 0)
    out_ref[...] = complex_rows(x, weights_ref[...], 1.0)


def total_kernel(scale, shares_ref, grad_in_ref, out_ref):
    x = jnp.sum(shares_ref[...].reshape(-1, 2 * TILE, LANES), axis=0)[:TILE]
    own = jnp.where(row_id((TILE, LANES)) < 2, grad_in_ref[...], x * scale)
    out_ref[...] = jnp.concatenate([own] * (out_ref.shape[0] // TILE), axis=0).astype(BF16)


def spectral_kernel(scale, shares_ref, out_ref):
    n = shares_ref.shape[0] // (2 * TILE)
    d_re, d_im, u_re, u_im = (every(shares_ref, r, n, 2 * TILE) for r in (0, 1, TILE, TILE + 1))
    left = jnp.concatenate([u_re, u_im], axis=0)
    right = jnp.concatenate(
        [jnp.concatenate([d_re, d_im], axis=0), jnp.concatenate([d_im, -d_re], axis=0)], axis=1
    )
    outer = lax.dot_general(
        left,
        right,
        (((0,), (0,)), ((), ())),
        precision=lax.Precision.HIGHEST,
        preferred_element_type=F32,
    )
    c = LANES // 2
    out_ref[0] = (outer[:c, :c] + outer[c:, c : 2 * c]) * scale
    out_ref[1] = (outer[:c, 2 * c : 3 * c] + outer[c:, 3 * c :]) * scale


def final_kernel(recv_ref, table_t_ref, cot_ref, fgrad_ref, win_ref, wout_ref, bin_ref, bout_ref, wide_ref):
    count = table_t_ref.shape[1] // 2
    wide_ref[...] = recv_ref[...].astype(F32)
    rows = [every(wide_ref, r, count, TILE) for r in range(TILE - 1)]
    grad_in = jnp.concatenate(rows[:2], axis=0).astype(BF16)
    back = dot(table_t_ref[...], grad_in)
    fgrad_ref[...] = (cot_ref[...].astype(F32) + back).astype(BF16)
    win_ref[:, :LANES] = rows[2]
    win_ref[:, LANES:] = rows[3]
    wout_ref[:LANES, :] = rows[4].T
    wout_ref[LANES:, :] = rows[5].T
    bin_ref[:, :LANES] = rows[6][0:1]
    bin_ref[:, LANES:] = rows[6][1:2]
    bout_ref[...] = rows[6][2:3, : bout_ref.shape[1]]


def exchange(x, axis):
    return lax.all_to_all(x, axis, 0, 0, tiled=True)


def exchange_pairs(x, axis):
    n = x.shape[0] // 2
    return exchange(x.reshape(n, 2, LANES), axis).reshape(2 * n, LANES)


def twice_diag(x):
    zero = jnp.zeros_like(x)
    return jnp.concatenate(
        [jnp.concatenate([x, zero], axis=1), jnp.concatenate([zero, x], axis=1)], axis=0
    )


def local(field, cotangent, mode_blocks, spectral, w_in, b_in, w_out, b_out):
    rows, width = field.shape
    chans, hid = w_in.shape
    ncol = width // chans
    grid = lax.axis_size("grid")
    dp = lax.axis_size("dp")
    inv_cols = 1.0 / (ncol * dp)
    count = mode_blocks.shape[0] * BLK
    first = (lax.axis_index("grid") * rows).reshape(1).astype(jnp.int32)
    s_re, s_im = spectral[0, 0], spectral[1, 0]
    mix_weights = jnp.concatenate([twice_diag(s_re), twice_diag(s_im)], axis=1)
    back_weights = jnp.concatenate([twice_diag(s_re.T), twice_diag(s_im.T)], axis=1)
    w_in_two, w_out_two = twice_diag(w_in), twice_diag(w_out)
    w_in_back, w_out_back = twice_diag(w_in.T), twice_diag(w_out.T)
    b_in_two = jnp.concatenate([b_in, b_in]).reshape(1, 2 * hid)
    b_out_two = jnp.concatenate([b_out, b_out]).reshape(1, width)

    modal, table = call(
        modal_kernel,
        "modal",
        [((2 * count, width), F32), ((2 * count, rows), BF16)],
        [SMEM, SMEM, VMEM],
    )(mode_blocks, first, field)
    table_t = table.T
    mixed, modal_sum = call(
        mix_kernel, "mix", [((2 * grid, width), BF16), ((TILE, width), F32)], [VMEM] * 2
    )(exchange_pairs(modal, "grid"), mix_weights)
    piece = exchange_pairs(mixed, "grid")

    output, parts = call(
        functools.partial(cells_kernel, 256),
        "cells",
        [((rows, width), BF16), ((TILE * grid, width), F32)],
        [VMEM] * 12,
        [
            pltpu.VMEM((2 * count, width), F32),
            pltpu.VMEM((rows, 2 * hid), BF16),
            pltpu.VMEM((rows, 2 * hid), BF16),
            pltpu.VMEM((rows, width), BF16),
        ],
    )(
        piece,
        table,
        table_t,
        field,
        cotangent,
        cotangent.T,
        w_in_two,
        w_in_back,
        b_in_two,
        w_out_two,
        w_out_back,
        b_out_two,
    )
    share, sums = call(
        share_kernel, "share", [((2 * TILE * dp, width), F32), ((TILE, width), F32)], [VMEM] * 2
    )(exchange(parts, "grid"), modal_sum)
    (grad_in,) = call(grad_in_kernel, "grad_in", [((TILE, width), F32)], [VMEM] * 2)(
        sums, back_weights
    )
    shares = exchange(share, "dp")
    (own,) = call(
        functools.partial(total_kernel, inv_cols), "total", [((TILE * grid, width), BF16)], [VMEM] * 2
    )(shares, grad_in)
    (spectral_grad,) = call(
        functools.partial(spectral_kernel, inv_cols), "spectral", [((2, chans, chans), F32)], [VMEM]
    )(shares)
    field_grad, w_in_grad, w_out_grad, b_in_grad, b_out_grad = call(
        final_kernel,
        "final",
        [
            ((rows, width), BF16),
            ((chans, hid), F32),
            ((hid, chans), F32),
            ((1, hid), F32),
            ((1, chans), F32),
        ],
        [VMEM] * 3,
        [pltpu.VMEM((TILE * grid, width), F32)],
    )(exchange(own, "grid"), table_t, cotangent)
    return (
        output,
        field_grad,
        spectral_grad.reshape(2, 1, chans, chans),
        w_in_grad,
        b_in_grad.reshape(hid),
        w_out_grad,
        b_out_grad.reshape(chans),
    )


def solution(mesh):
    in_specs = (
        P("grid", "dp"),
        P("grid", "dp"),
        P(),
        P(None, "grid", None, None),
        P(),
        P(),
        P(),
        P(),
    )
    out_specs = (P("grid", "dp"), P("grid", "dp"), P(None, "grid", None, None), P(), P(), P(), P())
    return jax.shard_map(local, mesh=mesh, in_specs=in_specs, out_specs=out_specs, check_vma=False)
```

```python
import functools
import math

import jax
import jax.numpy as jnp
from jax import lax
from jax.experimental import pallas as pl
from jax.experimental.pallas import tpu as pltpu
from jax.sharding import PartitionSpec as P

NX = 65536
BLK = 8
LANES = 128
TILE = 8
F32 = jnp.float32
BF16 = jnp.bfloat16
VMEM = pl.BlockSpec(memory_space=pltpu.VMEM)
HBM = pl.BlockSpec(memory_space=pltpu.HBM)
PARTS = 10


def call(kernel, name, outs, specs, scratch=()):
    return pl.pallas_call(
        kernel,
        name=name,
        out_shape=[jax.ShapeDtypeStruct(o[0], o[1]) for o in outs],
        in_specs=specs,
        out_specs=[o[2] if len(o) > 2 else VMEM for o in outs],
        scratch_shapes=list(scratch),
        compiler_params=pltpu.CompilerParams(vmem_limit_bytes=48 << 20),
    )


def dot(a, b):
    return jnp.dot(a, b, preferred_element_type=F32)


def row_id(shape):
    return lax.broadcasted_iota(jnp.int32, shape, 0)


def every(ref, start, count, step):
    return ref[pl.ds(start, count, stride=step), :]


def cos_sin(turn):
    quarter = NX // 4
    quad = (turn + quarter // 2) >> (quarter.bit_length() - 1)
    rest = (turn - quad * quarter).astype(F32) * (2.0 * math.pi / NX)
    sq = rest * rest
    sin = rest * (1.0 + sq * (-1 / 6 + sq * (1 / 120 + sq * (-1 / 5040 + sq * (1 / 362880)))))
    cos = 1.0 + sq * (
        -1 / 2 + sq * (1 / 24 + sq * (-1 / 720 + sq * (1 / 40320 + sq * (-1 / 3628800))))
    )
    odd = (quad & 1) == 1
    c = jnp.where(odd, sin, cos)
    s = jnp.where(odd, cos, sin)
    return jnp.where(((quad + 1) & 2) != 0, -c, c), jnp.where((quad & 2) != 0, -s, s)


def modal_kernel(
    blocks_hbm, field_hbm, modal_ref, table_ref, blocks_ref, field_ref, blocks_sem, field_sem
):
    blocks_copy = pltpu.make_async_copy(blocks_hbm, blocks_ref, blocks_sem)
    blocks_copy.start()
    field_copy = pltpu.make_async_copy(field_hbm, field_ref, field_sem)
    field_copy.start()
    blocks_copy.wait()
    kblocks = blocks_ref.shape[0]
    count = kblocks * BLK
    rows = field_ref.shape[0]
    first = lax.axis_index("grid") * rows
    base = jnp.concatenate(
        [jnp.full((BLK, LANES), blocks_ref[b] * BLK, jnp.int32) for b in range(kblocks)], axis=0
    )
    modes = base + row_id((count, LANES)) % BLK
    lane = lax.broadcasted_iota(jnp.int32, (count, LANES), 1)
    scale = 1.0 / math.sqrt(NX)
    near_c, near_s = cos_sin((modes * lane) & (NX - 1))
    near_c, near_s = near_c * scale, near_s * scale
    far_c, far_s = cos_sin((modes * (first + lane * LANES)) & (NX - 1))
    for a in range(rows // LANES):
        ca = jnp.broadcast_to(far_c[:, a : a + 1], (count, LANES))
        sa = jnp.broadcast_to(far_s[:, a : a + 1], (count, LANES))
        span = pl.ds(a * LANES, LANES)
        table_ref[:count, span] = (near_c * ca - near_s * sa).astype(BF16)
        table_ref[count:, span] = (-(near_s * ca + near_c * sa)).astype(BF16)
    field_copy.wait()
    modal = dot(table_ref[...], field_ref[...])
    modal_ref[pl.ds(0, count, stride=2), :] = modal[:count]
    modal_ref[pl.ds(1, count, stride=2), :] = modal[count:]


def complex_rows(x, weights, axis, sign):
    high = x.astype(BF16).astype(F32)
    rest = x - high
    mid = rest.astype(BF16).astype(F32)
    low = rest - mid
    row = row_id(x.shape)
    left = jnp.where(row < 2, high, jnp.where(row < 4, mid, jnp.where(row < 6, low, 0.0)))
    dims = (((1,), (axis,)), ((), ()))
    y = lax.dot_general(left.astype(BF16), weights, dims, preferred_element_type=F32)
    y = y + pltpu.roll(y, 4, 0)
    y = y + pltpu.roll(y, 2, 0)
    by_re = y[:, :LANES]
    by_im = pltpu.roll(y[:, LANES:], 1, 0)
    return by_re + jnp.where(row % 2 == 0, sign, -sign) * by_im


def mix_kernel(recv_ref, weights_ref, out_ref, sum_ref):
    x = jnp.sum(recv_ref[...].reshape(-1, TILE, LANES), axis=0)
    x = x + pltpu.roll(x, 4, 0)
    x = x + pltpu.roll(x, 2, 0)
    sum_ref[...] = x
    mixed = complex_rows(x, weights_ref[...], 0, -1.0)
    out_ref[...] = jnp.concatenate([mixed] * (out_ref.shape[0] // TILE), axis=0).astype(BF16)


def gelu_pair(pre):
    k = math.sqrt(2.0 / math.pi)
    sq = pre * pre
    t = jnp.tanh(pre * (k + (0.044715 * k) * sq))
    half = 0.5 * pre
    up = 1.0 + t
    return half * up, up * (0.5 + half * (1.0 - t) * (k + (3 * 0.044715 * k) * sq))


def cells_kernel(
    chunk,
    piece_ref,
    table_ref,
    table_t_ref,
    field_ref,
    cot_ref,
    cot_t_ref,
    win_ref,
    win_t_ref,
    bin_ref,
    wout_ref,
    wout_t_ref,
    bout_ref,
    out_hbm,
    parts_ref,
    wide_ref,
    hidden_ref,
    gpre_ref,
    gspec_ref,
    out_ref,
    sums_ref,
    out_sems,
):
    rows = field_ref.shape[0]
    count = table_ref.shape[0] // 2
    hid = bin_ref.shape[1] // 2
    chans = LANES // 2
    wide_ref[...] = piece_ref[...].astype(F32)
    mixed = jnp.concatenate([every(wide_ref, 0, count, 2), every(wide_ref, 1, count, 2)], axis=0)
    mixed_t = mixed.T.astype(BF16)
    mixed = mixed.astype(BF16)
    copies = []
    for i in range(rows // chunk):
        span = pl.ds(i * chunk, chunk)
        spec = (2.0 * dot(table_t_ref[span, :], mixed)).astype(BF16)
        pre = dot(spec, win_ref[...]) + bin_ref[...]
        gate, slope = gelu_pair(pre)
        hidden = gate.astype(BF16)
        hidden_ref[span, :] = hidden
        gpre = (dot(cot_ref[span, :], wout_t_ref[...]) * slope).astype(BF16)
        gpre_ref[span, :] = gpre
        gspec_ref[span, :] = dot(gpre, win_t_ref[...]).astype(BF16)
        out = dot(hidden, wout_ref[...]) + bout_ref[...]
        out_ref[span, :] = (field_ref[span, :].astype(F32) + out).astype(BF16)
        copies.append(pltpu.make_async_copy(out_ref.at[span], out_hbm.at[span], out_sems.at[i]))
        copies[-1].start()
    spec_t = (2.0 * dot(mixed_t, table_ref[...])).astype(BF16)
    ones = jnp.ones((2 * TILE, rows), BF16)
    by_in = dot(jnp.concatenate([spec_t, ones], axis=0), gpre_ref[...])
    by_out = dot(cot_t_ref[...], hidden_ref[...])
    grad_modal = 2.0 * dot(table_ref[...], gspec_ref[...])
    sums_out = dot(ones, cot_ref[...])
    g_in = by_in[:chans, :hid] + by_in[chans:LANES, hid:]
    g_out = by_out[:chans, :hid] + by_out[chans:, hid:]
    b_in = by_in[LANES : LANES + 1, :hid] + by_in[LANES : LANES + 1, hid:]
    b_out = (sums_out + pltpu.roll(sums_out, chans, 1))[:1]
    row = row_id((count, LANES))
    bias = jnp.where(
        row == 0,
        b_in[:, :LANES],
        jnp.where(row == 1, b_in[:, LANES:], jnp.where(row == 2, b_out, 0.0)),
    )
    for r, block in enumerate(
        (
            *split(grad_modal[:count]),
            *split(grad_modal[count:]),
            g_in[:, :LANES],
            g_in[:, LANES:],
            g_out[:, :LANES],
            g_out[:, LANES:],
            *split(bias),
        )
    ):
        sums_ref[pl.ds(r, count, stride=PARTS), :] = block
    parts_ref[...] = sums_ref[...].astype(BF16)
    for copy in copies:
        copy.wait()


def split(x):
    high = x.astype(BF16).astype(F32)
    return high, x - high


def share_kernel(recv_ref, modal_ref, weights_ref, share_ref, grad_in_ref):
    x = jnp.sum(recv_ref[...].astype(F32).reshape(-1, 4 * PARTS, LANES), axis=0)
    x = (x[:PARTS] + x[PARTS : 2 * PARTS]) + (x[2 * PARTS : 3 * PARTS] + x[3 * PARTS :])
    d_re, d_im, bias = x[0:1] + x[1:2], x[2:3] + x[3:4], x[8:9] + x[9:10]
    both = jnp.concatenate([d_re, d_im, x[4:8], bias, jnp.zeros_like(bias), modal_ref[...]], axis=0)
    share_ref[...] = jnp.concatenate([both] * (share_ref.shape[0] // (2 * TILE)), axis=0)
    grad = jnp.concatenate([d_re, d_im] * (TILE // 2), axis=0)
    grad_in_ref[...] = complex_rows(grad, weights_ref[...], 1, 1.0)


def total_kernel(scale, shares_ref, grad_in_ref, out_ref):
    x = jnp.sum(shares_ref[...].reshape(-1, 2 * TILE, LANES), axis=0)[:TILE]
    own = jnp.where(row_id((TILE, LANES)) < 2, grad_in_ref[...], x * scale)
    out_ref[...] = jnp.concatenate([own] * (out_ref.shape[0] // TILE), axis=0).astype(BF16)


def spectral_kernel(scale, shares_ref, out_ref):
    n = shares_ref.shape[0] // (2 * TILE)
    d_re, d_im, u_re, u_im = (every(shares_ref, r, n, 2 * TILE) for r in (0, 1, TILE, TILE + 1))
    left = jnp.concatenate([u_re, u_im], axis=0)
    right = jnp.concatenate(
        [jnp.concatenate([d_re, d_im], axis=0), jnp.concatenate([d_im, -d_re], axis=0)], axis=1
    )
    outer = lax.dot_general(
        left,
        right,
        (((0,), (0,)), ((), ())),
        precision=lax.Precision.HIGHEST,
        preferred_element_type=F32,
    )
    c = LANES // 2
    out_ref[0] = (outer[:c, :c] + outer[c:, c : 2 * c]) * scale
    out_ref[1] = (outer[:c, 2 * c : 3 * c] + outer[c:, 3 * c :]) * scale


def final_kernel(
    chunk,
    recv_ref,
    table_t_ref,
    cot_ref,
    fgrad_hbm,
    win_ref,
    wout_ref,
    bin_ref,
    bout_ref,
    wide_ref,
    fgrad_ref,
    sems,
):
    count = table_t_ref.shape[1] // 2
    wide_ref[...] = recv_ref[...].astype(F32)
    rows = [every(wide_ref, r, count, TILE) for r in range(TILE - 1)]
    grad_in = jnp.concatenate(rows[:2], axis=0).astype(BF16)
    copies = []
    for i in range(table_t_ref.shape[0] // chunk):
        span = pl.ds(i * chunk, chunk)
        back = dot(table_t_ref[span, :], grad_in)
        fgrad_ref[span, :] = (cot_ref[span, :].astype(F32) + back).astype(BF16)
        copies.append(pltpu.make_async_copy(fgrad_ref.at[span], fgrad_hbm.at[span], sems.at[i]))
        copies[-1].start()
    win_ref[:, :LANES] = rows[2]
    win_ref[:, LANES:] = rows[3]
    wout_ref[:, :LANES] = rows[4]
    wout_ref[:, LANES:] = rows[5]
    bin_ref[:, :LANES] = rows[6][0:1]
    bin_ref[:, LANES:] = rows[6][1:2]
    bout_ref[...] = rows[6][2:3, : bout_ref.shape[1]]
    for copy in copies:
        copy.wait()


def exchange(x, axis):
    return lax.all_to_all(x, axis, 0, 0, tiled=True)


def exchange_pairs(x, axis):
    n = x.shape[0] // 2
    return exchange(x.reshape(n, 2, LANES), axis).reshape(2 * n, LANES)


def twice_diag(x):
    zero = jnp.zeros_like(x)
    return jnp.concatenate(
        [jnp.concatenate([x, zero], axis=1), jnp.concatenate([zero, x], axis=1)], axis=0
    )


def local(field, cotangent, mode_blocks, spectral, w_in, b_in, w_out, b_out):
    rows, width = field.shape
    chans, hid = w_in.shape
    ncol = width // chans
    grid = lax.axis_size("grid")
    dp = lax.axis_size("dp")
    inv_cols = 1.0 / (ncol * dp)
    count = mode_blocks.shape[0] * BLK
    s_re, s_im = spectral[0, 0], spectral[1, 0]
    mix_weights = jnp.concatenate([twice_diag(s_re), twice_diag(s_im)], axis=1)
    back_weights = jnp.concatenate([twice_diag(s_re), twice_diag(s_im)], axis=0)
    w_in_two, w_out_two = twice_diag(w_in), twice_diag(w_out)
    w_in_back, w_out_back = twice_diag(w_in.T), twice_diag(w_out.T)
    b_in_two = jnp.concatenate([b_in, b_in]).reshape(1, 2 * hid)
    b_out_two = jnp.concatenate([b_out, b_out]).reshape(1, width)

    modal, table = call(
        modal_kernel,
        "modal",
        [((2 * count, width), F32), ((2 * count, rows), BF16)],
        [HBM, HBM],
        [
            pltpu.SMEM(mode_blocks.shape, jnp.int32),
            pltpu.VMEM((rows, width), BF16),
            pltpu.SemaphoreType.DMA,
            pltpu.SemaphoreType.DMA,
        ],
    )(
        pltpu.with_memory_space_constraint(mode_blocks, pltpu.HBM),
        pltpu.with_memory_space_constraint(field, pltpu.HBM),
    )
    recv, ready = lax.optimization_barrier(
        (
            exchange_pairs(modal, "grid"),
            (
                table.T,
                cotangent.T,
                mix_weights,
                back_weights,
                w_in_two,
                w_in_back,
                b_in_two,
                w_out_two,
                w_out_back,
                b_out_two,
            ),
        )
    )
    table_t, cotangent_t, mix_weights, back_weights = ready[:4]
    w_in_two, w_in_back, b_in_two, w_out_two, w_out_back, b_out_two = ready[4:]
    mixed, modal_sum = call(
        mix_kernel, "mix", [((2 * grid, width), BF16), ((TILE, width), F32)], [VMEM] * 2
    )(recv, mix_weights)
    piece = exchange_pairs(mixed, "grid")

    output, parts = call(
        functools.partial(cells_kernel, 256),
        "cells",
        [((rows, width), BF16, HBM), ((PARTS * grid, width), BF16)],
        [VMEM] * 12,
        [
            pltpu.VMEM((2 * count, width), F32),
            pltpu.VMEM((rows, 2 * hid), BF16),
            pltpu.VMEM((rows, 2 * hid), BF16),
            pltpu.VMEM((rows, width), BF16),
            pltpu.VMEM((rows, width), BF16),
            pltpu.VMEM((PARTS * grid, width), F32),
            pltpu.SemaphoreType.DMA((rows // 256,)),
        ],
    )(
        piece,
        table,
        table_t,
        field,
        cotangent,
        cotangent_t,
        w_in_two,
        w_in_back,
        b_in_two,
        w_out_two,
        w_out_back,
        b_out_two,
    )
    share, grad_in = call(
        share_kernel, "share", [((2 * TILE * dp, width), F32), ((TILE, width), F32)], [VMEM] * 3
    )(exchange_pairs(parts, "grid"), modal_sum, back_weights)
    shares = exchange(share, "dp")
    (own,) = call(
        functools.partial(total_kernel, inv_cols), "total", [((TILE * grid, width), BF16)], [VMEM] * 2
    )(shares, grad_in)
    (spectral_grad,) = call(
        functools.partial(spectral_kernel, inv_cols), "spectral", [((2, chans, chans), F32)], [VMEM]
    )(shares)
    field_grad, w_in_grad, w_out_grad, b_in_grad, b_out_grad = call(
        functools.partial(final_kernel, 256),
        "final",
        [
            ((rows, width), BF16, HBM),
            ((chans, hid), F32),
            ((chans, hid), F32),
            ((1, hid), F32),
            ((1, chans), F32),
        ],
        [VMEM] * 3,
        [
            pltpu.VMEM((TILE * grid, width), F32),
            pltpu.VMEM((rows, width), BF16),
            pltpu.SemaphoreType.DMA((rows // 256,)),
        ],
    )(exchange(own, "grid"), table_t, cotangent)
    return (
        output,
        field_grad,
        spectral_grad.reshape(2, 1, chans, chans),
        w_in_grad,
        b_in_grad.reshape(hid),
        w_out_grad.T,
        b_out_grad.reshape(chans),
    )


def solution(mesh):
    in_specs = (
        P("grid", "dp"),
        P("grid", "dp"),
        P(),
        P(None, "grid", None, None),
        P(),
        P(),
        P(),
        P(),
    )
    out_specs = (P("grid", "dp"), P("grid", "dp"), P(None, "grid", None, None), P(), P(), P(), P())
    return jax.shard_map(local, mesh=mesh, in_specs=in_specs, out_specs=out_specs, check_vma=False)
```

```python
import functools
import math

import jax
import jax.numpy as jnp
from jax import lax
from jax.experimental import pallas as pl
from jax.experimental.pallas import tpu as pltpu
from jax.sharding import PartitionSpec as P

NX = 65536
BLK = 8
LANES = 128
TILE = 8
F32 = jnp.float32
BF16 = jnp.bfloat16
VMEM = pl.BlockSpec(memory_space=pltpu.VMEM)
HBM = pl.BlockSpec(memory_space=pltpu.HBM)
PARTS = 10


def call(kernel, name, outs, specs, scratch=()):
    return pl.pallas_call(
        kernel,
        name=name,
        out_shape=[jax.ShapeDtypeStruct(o[0], o[1]) for o in outs],
        in_specs=specs,
        out_specs=[o[2] if len(o) > 2 else VMEM for o in outs],
        scratch_shapes=list(scratch),
        compiler_params=pltpu.CompilerParams(vmem_limit_bytes=48 << 20),
    )


def dot(a, b):
    return jnp.dot(a, b, preferred_element_type=F32)


def row_id(shape):
    return lax.broadcasted_iota(jnp.int32, shape, 0)


def every(ref, start, count, step):
    return ref[pl.ds(start, count, stride=step), :]


def cos_sin(turn):
    quarter = NX // 4
    quad = (turn + quarter // 2) >> (quarter.bit_length() - 1)
    rest = (turn - quad * quarter).astype(F32) * (2.0 * math.pi / NX)
    sq = rest * rest
    sin = rest * (1.0 + sq * (-1 / 6 + sq * (1 / 120 + sq * (-1 / 5040 + sq * (1 / 362880)))))
    cos = 1.0 + sq * (
        -1 / 2 + sq * (1 / 24 + sq * (-1 / 720 + sq * (1 / 40320 + sq * (-1 / 3628800))))
    )
    odd = (quad & 1) == 1
    c = jnp.where(odd, sin, cos)
    s = jnp.where(odd, cos, sin)
    return jnp.where(((quad + 1) & 2) != 0, -c, c), jnp.where((quad & 2) != 0, -s, s)


def modal_kernel(
    blocks_hbm, field_hbm, modal_ref, table_ref, blocks_ref, field_ref, blocks_sem, field_sem
):
    blocks_copy = pltpu.make_async_copy(blocks_hbm, blocks_ref, blocks_sem)
    blocks_copy.start()
    field_copy = pltpu.make_async_copy(field_hbm, field_ref, field_sem)
    field_copy.start()
    blocks_copy.wait()
    kblocks = blocks_ref.shape[0]
    count = kblocks * BLK
    rows = field_ref.shape[0]
    first = lax.axis_index("grid") * rows
    base = jnp.concatenate(
        [jnp.full((BLK, LANES), blocks_ref[b] * BLK, jnp.int32) for b in range(kblocks)], axis=0
    )
    modes = base + row_id((count, LANES)) % BLK
    lane = lax.broadcasted_iota(jnp.int32, (count, LANES), 1)
    scale = 1.0 / math.sqrt(NX)
    near_c, near_s = cos_sin((modes * lane) & (NX - 1))
    near_c, near_s = near_c * scale, near_s * scale
    far_c, far_s = cos_sin((modes * (first + lane * LANES)) & (NX - 1))
    for a in range(rows // LANES):
        ca = jnp.broadcast_to(far_c[:, a : a + 1], (count, LANES))
        sa = jnp.broadcast_to(far_s[:, a : a + 1], (count, LANES))
        span = pl.ds(a * LANES, LANES)
        table_ref[:count, span] = (near_c * ca - near_s * sa).astype(BF16)
        table_ref[count:, span] = (-(near_s * ca + near_c * sa)).astype(BF16)
    field_copy.wait()
    modal = dot(table_ref[...], field_ref[...])
    modal_ref[pl.ds(0, count, stride=2), :] = modal[:count]
    modal_ref[pl.ds(1, count, stride=2), :] = modal[count:]


def complex_rows(x, weights, axis, sign):
    high = x.astype(BF16).astype(F32)
    rest = x - high
    mid = rest.astype(BF16).astype(F32)
    low = rest - mid
    row = row_id(x.shape)
    left = jnp.where(row < 2, high, jnp.where(row < 4, mid, jnp.where(row < 6, low, 0.0)))
    dims = (((1,), (axis,)), ((), ()))
    y = lax.dot_general(left.astype(BF16), weights, dims, preferred_element_type=F32)
    y = y + pltpu.roll(y, 4, 0)
    y = y + pltpu.roll(y, 2, 0)
    by_re = y[:, :LANES]
    by_im = pltpu.roll(y[:, LANES:], 1, 0)
    return by_re + jnp.where(row % 2 == 0, sign, -sign) * by_im


def mix_kernel(recv_ref, weights_ref, out_ref, sum_ref):
    x = jnp.sum(recv_ref[...].reshape(-1, TILE, LANES), axis=0)
    x = x + pltpu.roll(x, 4, 0)
    x = x + pltpu.roll(x, 2, 0)
    sum_ref[...] = x
    mixed = complex_rows(x, weights_ref[...], 0, -1.0)
    out_ref[...] = jnp.concatenate([mixed] * (out_ref.shape[0] // TILE), axis=0).astype(BF16)


def gelu_pair(pre):
    k = math.sqrt(2.0 / math.pi)
    sq = pre * pre
    t = jnp.tanh(pre * (k + (0.044715 * k) * sq))
    half = 0.5 * pre
    up = 1.0 + t
    return half * up, up * (0.5 + half * (1.0 - t) * (k + (3 * 0.044715 * k) * sq))


def cells_kernel(
    chunk,
    piece_ref,
    table_ref,
    table_tt_ref,
    field_ref,
    cot_ref,
    cot_t_ref,
    win_ref,
    win_t_ref,
    bin_ref,
    wout_ref,
    wout_t_ref,
    bout_ref,
    out_hbm,
    parts_ref,
    wide_ref,
    hidden_ref,
    gpre_ref,
    out_ref,
    sums_ref,
    out_sems,
):
    rows = field_ref.shape[0]
    count = table_ref.shape[0] // 2
    hid = bin_ref.shape[1] // 2
    chans = LANES // 2
    wide_ref[...] = 2.0 * piece_ref[...].astype(F32)
    mixed = jnp.concatenate([every(wide_ref, 0, count, 2), every(wide_ref, 1, count, 2)], axis=0)
    right = stack_parts(dot(mixed.astype(BF16), win_ref[...]))
    copies = []
    for i in range(rows // chunk):
        span = pl.ds(i * chunk, chunk)
        pre = dot(table_tt_ref[span, :], right) + bin_ref[...]
        gate, slope = gelu_pair(pre)
        hidden = gate.astype(BF16)
        hidden_ref[span, :] = hidden
        gpre_ref[span, :] = (dot(cot_ref[span, :], wout_t_ref[...]) * slope).astype(BF16)
        out = dot(hidden, wout_ref[...]) + bout_ref[...]
        out_ref[span, :] = (field_ref[span, :].astype(F32) + out).astype(BF16)
        copies.append(pltpu.make_async_copy(out_ref.at[span], out_hbm.at[span], out_sems.at[i]))
        copies[-1].start()
    ones = jnp.ones((2 * TILE, rows), BF16)
    t = dot(jnp.concatenate([table_ref[...], ones], axis=0), gpre_ref[...])
    by_out = dot(cot_t_ref[...], hidden_ref[...])
    sums_out = dot(ones, cot_ref[...])
    b_in = t[2 * count : 2 * count + 1]
    t_parts = stack_parts(t[: 2 * count])
    grad_modal = dot(t_parts, win_t_ref[...])
    grad_modal = 2.0 * (grad_modal[: 2 * count] + grad_modal[2 * count :])
    mixed_t = mixed.T.astype(BF16)
    by_in = dot(jnp.concatenate([mixed_t, mixed_t], axis=1), t_parts)
    g_in = by_in[:chans, :hid] + by_in[chans:, hid:]
    g_out = by_out[:chans, :hid] + by_out[chans:, hid:]
    b_in = b_in[:, :hid] + b_in[:, hid:]
    b_out = (sums_out + pltpu.roll(sums_out, chans, 1))[:1]
    row = row_id((count, LANES))
    bias = jnp.where(
        row == 0,
        b_in[:, :LANES],
        jnp.where(row == 1, b_in[:, LANES:], jnp.where(row == 2, b_out, 0.0)),
    )
    for r, block in enumerate(
        (
            *split(grad_modal[:count]),
            *split(grad_modal[count:]),
            g_in[:, :LANES],
            g_in[:, LANES:],
            g_out[:, :LANES],
            g_out[:, LANES:],
            *split(bias),
        )
    ):
        sums_ref[pl.ds(r, count, stride=PARTS), :] = block
    parts_ref[...] = sums_ref[...].astype(BF16)
    for copy in copies:
        copy.wait()


def stack_parts(x):
    high, low = split(x)
    return jnp.concatenate([high, low], axis=0).astype(BF16)


def split(x):
    high = x.astype(BF16).astype(F32)
    return high, x - high


def share_kernel(recv_ref, modal_ref, weights_ref, share_ref, grad_in_ref):
    x = jnp.sum(recv_ref[...].astype(F32).reshape(-1, 4 * PARTS, LANES), axis=0)
    x = (x[:PARTS] + x[PARTS : 2 * PARTS]) + (x[2 * PARTS : 3 * PARTS] + x[3 * PARTS :])
    d_re, d_im, bias = x[0:1] + x[1:2], x[2:3] + x[3:4], x[8:9] + x[9:10]
    both = jnp.concatenate([d_re, d_im, x[4:8], bias, jnp.zeros_like(bias), modal_ref[...]], axis=0)
    share_ref[...] = jnp.concatenate([both] * (share_ref.shape[0] // (2 * TILE)), axis=0)
    grad = jnp.concatenate([d_re, d_im] * (TILE // 2), axis=0)
    grad_in_ref[...] = complex_rows(grad, weights_ref[...], 1, 1.0)


def total_kernel(scale, shares_ref, grad_in_ref, out_ref):
    x = jnp.sum(shares_ref[...].reshape(-1, 2 * TILE, LANES), axis=0)[:TILE]
    own = jnp.where(row_id((TILE, LANES)) < 2, grad_in_ref[...], x * scale)
    out_ref[...] = jnp.concatenate([own] * (out_ref.shape[0] // TILE), axis=0).astype(BF16)


def final_kernel(
    scale,
    recv_ref,
    shares_ref,
    table_tt_ref,
    cot_ref,
    fgrad_ref,
    spectral_ref,
    win_ref,
    wout_ref,
    bin_ref,
    bout_ref,
    wide_ref,
):
    count = table_tt_ref.shape[1] // 4
    wide_ref[...] = recv_ref[...].astype(F32)
    rows = [every(wide_ref, r, count, TILE) for r in range(TILE - 1)]
    grad_in = jnp.concatenate(rows[:2], axis=0).astype(BF16)
    back = dot(table_tt_ref[:, : 2 * count], grad_in)
    fgrad_ref[...] = (cot_ref[...].astype(F32) + back).astype(BF16)
    win_ref[:, :LANES] = rows[2]
    win_ref[:, LANES:] = rows[3]
    wout_ref[:, :LANES] = rows[4]
    wout_ref[:, LANES:] = rows[5]
    bin_ref[:, :LANES] = rows[6][0:1]
    bin_ref[:, LANES:] = rows[6][1:2]
    bout_ref[...] = rows[6][2:3, : bout_ref.shape[1]]
    spectral_sums(scale, shares_ref, spectral_ref)


def spectral_sums(scale, shares_ref, out_ref):
    n = shares_ref.shape[0] // (2 * TILE)
    d_re, d_im, u_re, u_im = (every(shares_ref, r, n, 2 * TILE) for r in (0, 1, TILE, TILE + 1))
    left_high, left_low = split(jnp.concatenate([u_re, u_im], axis=0))
    right_high, right_low = split(
        jnp.concatenate(
            [jnp.concatenate([d_re, d_im], axis=0), jnp.concatenate([d_im, -d_re], axis=0)], axis=1
        )
    )
    left = jnp.concatenate([left_high, left_high, left_low], axis=0).astype(BF16)
    right = jnp.concatenate([right_high, right_low, right_high], axis=0).astype(BF16)
    outer = lax.dot_general(left, right, (((0,), (0,)), ((), ())), preferred_element_type=F32)
    c = LANES // 2
    out_ref[0] = (outer[:c, :c] + outer[c:, c : 2 * c]) * scale
    out_ref[1] = (outer[:c, 2 * c : 3 * c] + outer[c:, 3 * c :]) * scale


def exchange(x, axis):
    return lax.all_to_all(x, axis, 0, 0, tiled=True)


def exchange_pairs(x, axis):
    n = x.shape[0] // 2
    return exchange(x.reshape(n, 2, LANES), axis).reshape(2 * n, LANES)


def twice_diag(x):
    zero = jnp.zeros_like(x)
    return jnp.concatenate(
        [jnp.concatenate([x, zero], axis=1), jnp.concatenate([zero, x], axis=1)], axis=0
    )


def local(field, cotangent, mode_blocks, spectral, w_in, b_in, w_out, b_out):
    rows, width = field.shape
    chans, hid = w_in.shape
    ncol = width // chans
    grid = lax.axis_size("grid")
    dp = lax.axis_size("dp")
    inv_cols = 1.0 / (ncol * dp)
    count = mode_blocks.shape[0] * BLK
    s_re, s_im = spectral[0, 0], spectral[1, 0]
    mix_weights = jnp.concatenate([twice_diag(s_re), twice_diag(s_im)], axis=1)
    back_weights = jnp.concatenate([twice_diag(s_re), twice_diag(s_im)], axis=0)
    w_in_two, w_out_two = twice_diag(w_in), twice_diag(w_out)
    w_in_back, w_out_back = twice_diag(w_in.T), twice_diag(w_out.T)
    b_in_two = jnp.concatenate([b_in, b_in]).reshape(1, 2 * hid)
    b_out_two = jnp.concatenate([b_out, b_out]).reshape(1, width)

    modal, table = call(
        modal_kernel,
        "modal",
        [((2 * count, width), F32), ((2 * count, rows), BF16)],
        [HBM, HBM],
        [
            pltpu.SMEM(mode_blocks.shape, jnp.int32),
            pltpu.VMEM((rows, width), BF16),
            pltpu.SemaphoreType.DMA,
            pltpu.SemaphoreType.DMA,
        ],
    )(
        pltpu.with_memory_space_constraint(mode_blocks, pltpu.HBM),
        pltpu.with_memory_space_constraint(field, pltpu.HBM),
    )
    recv, ready = lax.optimization_barrier(
        (
            exchange_pairs(modal, "grid"),
            (
                jnp.concatenate([table.T, table.T], axis=1),
                cotangent.T,
                mix_weights,
                back_weights,
                w_in_two,
                w_in_back,
                b_in_two,
                w_out_two,
                w_out_back,
                b_out_two,
            ),
        )
    )
    table_tt, cotangent_t, mix_weights, back_weights = ready[:4]
    w_in_two, w_in_back, b_in_two, w_out_two, w_out_back, b_out_two = ready[4:]
    mixed, modal_sum = call(
        mix_kernel, "mix", [((2 * grid, width), BF16), ((TILE, width), F32)], [VMEM] * 2
    )(recv, mix_weights)
    piece = exchange_pairs(mixed, "grid")

    output, parts = call(
        functools.partial(cells_kernel, 256),
        "cells",
        [((rows, width), BF16, HBM), ((PARTS * grid, width), BF16)],
        [VMEM] * 12,
        [
            pltpu.VMEM((2 * count, width), F32),
            pltpu.VMEM((rows, 2 * hid), BF16),
            pltpu.VMEM((rows, 2 * hid), BF16),
            pltpu.VMEM((rows, width), BF16),
            pltpu.VMEM((PARTS * grid, width), F32),
            pltpu.SemaphoreType.DMA((rows // 256,)),
        ],
    )(
        piece,
        table,
        table_tt,
        field,
        cotangent,
        cotangent_t,
        w_in_two,
        w_in_back,
        b_in_two,
        w_out_two,
        w_out_back,
        b_out_two,
    )
    share, grad_in = call(
        share_kernel, "share", [((2 * TILE * dp, width), F32), ((TILE, width), F32)], [VMEM] * 3
    )(exchange_pairs(parts, "grid"), modal_sum, back_weights)
    shares = exchange(share, "dp")
    (own,) = call(
        functools.partial(total_kernel, inv_cols), "total", [((TILE * grid, width), BF16)], [VMEM] * 2
    )(shares, grad_in)
    field_grad, spectral_grad, w_in_grad, w_out_grad, b_in_grad, b_out_grad = call(
        functools.partial(final_kernel, inv_cols),
        "final",
        [
            ((rows, width), BF16),
            ((2, chans, chans), F32),
            ((chans, hid), F32),
            ((chans, hid), F32),
            ((1, hid), F32),
            ((1, chans), F32),
        ],
        [VMEM] * 4,
        [pltpu.VMEM((TILE * grid, width), F32)],
    )(exchange(own, "grid"), shares, table_tt, cotangent)
    return (
        output,
        field_grad,
        spectral_grad.reshape(2, 1, chans, chans),
        w_in_grad,
        b_in_grad.reshape(hid),
        w_out_grad.T,
        b_out_grad.reshape(chans),
    )


def solution(mesh):
    in_specs = (
        P("grid", "dp"),
        P("grid", "dp"),
        P(),
        P(None, "grid", None, None),
        P(),
        P(),
        P(),
        P(),
    )
    out_specs = (P("grid", "dp"), P("grid", "dp"), P(None, "grid", None, None), P(), P(), P(), P())
    return jax.shard_map(local, mesh=mesh, in_specs=in_specs, out_specs=out_specs, check_vma=False)
```

```python
import functools
import math

import jax
import jax.numpy as jnp
from jax import lax
from jax.experimental import pallas as pl
from jax.experimental.pallas import tpu as pltpu
from jax.sharding import PartitionSpec as P

NX = 65536
BLK = 8
LANES = 128
TILE = 8
F32 = jnp.float32
BF16 = jnp.bfloat16
VMEM = pl.BlockSpec(memory_space=pltpu.VMEM)
HBM = pl.BlockSpec(memory_space=pltpu.HBM)


def call(kernel, name, outs, specs, scratch=()):
    return pl.pallas_call(
        kernel,
        name=name,
        out_shape=[jax.ShapeDtypeStruct(o[0], o[1]) for o in outs],
        in_specs=specs,
        out_specs=[o[2] if len(o) > 2 else VMEM for o in outs],
        scratch_shapes=list(scratch),
        compiler_params=pltpu.CompilerParams(vmem_limit_bytes=48 << 20),
    )


def dot(a, b):
    return jnp.dot(a, b, preferred_element_type=F32)


def row_id(shape):
    return lax.broadcasted_iota(jnp.int32, shape, 0)


def every(ref, start, count, step):
    return ref[pl.ds(start, count, stride=step), :]


def cos_sin(turn):
    quarter = NX // 4
    quad = (turn + quarter // 2) >> (quarter.bit_length() - 1)
    rest = (turn - quad * quarter).astype(F32) * (2.0 * math.pi / NX)
    sq = rest * rest
    sin = rest * (1.0 + sq * (-1 / 6 + sq * (1 / 120 + sq * (-1 / 5040 + sq * (1 / 362880)))))
    cos = 1.0 + sq * (
        -1 / 2 + sq * (1 / 24 + sq * (-1 / 720 + sq * (1 / 40320 + sq * (-1 / 3628800))))
    )
    odd = (quad & 1) == 1
    c = jnp.where(odd, sin, cos)
    s = jnp.where(odd, cos, sin)
    return jnp.where(((quad + 1) & 2) != 0, -c, c), jnp.where((quad & 2) != 0, -s, s)


def modal_kernel(
    blocks_hbm, field_hbm, modal_ref, table_ref, blocks_ref, field_ref, wide_ref, blocks_sem, field_sem
):
    blocks_copy = pltpu.make_async_copy(blocks_hbm, blocks_ref, blocks_sem)
    blocks_copy.start()
    field_copy = pltpu.make_async_copy(field_hbm, field_ref, field_sem)
    field_copy.start()
    blocks_copy.wait()
    kblocks = blocks_ref.shape[0]
    count = kblocks * BLK
    rows = field_ref.shape[0]
    first = lax.axis_index("grid") * rows
    base = jnp.concatenate(
        [jnp.full((BLK, LANES), blocks_ref[b] * BLK, jnp.int32) for b in range(kblocks)], axis=0
    )
    modes = base + row_id((count, LANES)) % BLK
    lane = lax.broadcasted_iota(jnp.int32, (count, LANES), 1)
    scale = 1.0 / math.sqrt(NX)
    near_c, near_s = cos_sin((modes * lane) & (NX - 1))
    near_c, near_s = near_c * scale, near_s * scale
    far_c, far_s = cos_sin((modes * (first + lane * LANES)) & (NX - 1))
    for a in range(rows // LANES):
        ca = jnp.broadcast_to(far_c[:, a : a + 1], (count, LANES))
        sa = jnp.broadcast_to(far_s[:, a : a + 1], (count, LANES))
        span = pl.ds(a * LANES, LANES)
        table_ref[:count, span] = (near_c * ca - near_s * sa).astype(BF16)
        table_ref[count:, span] = (-(near_s * ca + near_c * sa)).astype(BF16)
    field_copy.wait()
    modal = dot(table_ref[...], field_ref[...])
    wide_ref[pl.ds(0, count, stride=2), :] = modal[:count]
    wide_ref[pl.ds(1, count, stride=2), :] = modal[count:]
    modal_ref[...] = wide_ref[...].astype(BF16)


def complex_rows(x, weights, axis, sign):
    high = x.astype(BF16).astype(F32)
    rest = x - high
    mid = rest.astype(BF16).astype(F32)
    low = rest - mid
    row = row_id(x.shape)
    left = jnp.where(row < 2, high, jnp.where(row < 4, mid, jnp.where(row < 6, low, 0.0)))
    dims = (((1,), (axis,)), ((), ()))
    y = lax.dot_general(left.astype(BF16), weights, dims, preferred_element_type=F32)
    y = y + pltpu.roll(y, 4, 0)
    y = y + pltpu.roll(y, 2, 0)
    by_re = y[:, :LANES]
    by_im = pltpu.roll(y[:, LANES:], 1, 0)
    return by_re + jnp.where(row % 2 == 0, sign, -sign) * by_im


def mix_kernel(recv_ref, weights_ref, out_ref, sum_ref):
    x = jnp.sum(recv_ref[...].astype(F32).reshape(-1, TILE, LANES), axis=0)
    x = x + pltpu.roll(x, 4, 0)
    x = x + pltpu.roll(x, 2, 0)
    sum_ref[...] = x
    mixed = complex_rows(x, weights_ref[...], 0, -1.0)
    out_ref[...] = jnp.concatenate([mixed] * (out_ref.shape[0] // TILE), axis=0).astype(BF16)


def gelu_pair(pre):
    k = math.sqrt(2.0 / math.pi)
    sq = pre * pre
    t = jnp.tanh(pre * (k + (0.044715 * k) * sq))
    half = 0.5 * pre
    up = 1.0 + t
    return half * up, up * (0.5 + half * (1.0 - t) * (k + (3 * 0.044715 * k) * sq))


def cells_kernel(
    chunk,
    piece_ref,
    table_ref,
    table_tt_ref,
    field_ref,
    cot_ref,
    cot_t_ref,
    win_ref,
    win_t_ref,
    bin_ref,
    wout_ref,
    wout_t_ref,
    bout_ref,
    out_hbm,
    parts_ref,
    wide_ref,
    hidden_ref,
    gpre_ref,
    out_ref,
    sums_ref,
    out_sems,
):
    rows = field_ref.shape[0]
    count = table_ref.shape[0] // 2
    hid = bin_ref.shape[1] // 2
    chans = LANES // 2
    wide_ref[...] = 2.0 * piece_ref[...].astype(F32)
    mixed = jnp.concatenate([every(wide_ref, 0, count, 2), every(wide_ref, 1, count, 2)], axis=0)
    right = stack_parts(dot(mixed.astype(BF16), win_ref[...]))
    copies = []
    for i in range(rows // chunk):
        span = pl.ds(i * chunk, chunk)
        pre = dot(table_tt_ref[span, :], right) + bin_ref[...]
        gate, slope = gelu_pair(pre)
        hidden = gate.astype(BF16)
        hidden_ref[span, :] = hidden
        gpre_ref[span, :] = (dot(cot_ref[span, :], wout_t_ref[...]) * slope).astype(BF16)
        out = dot(hidden, wout_ref[...]) + bout_ref[...]
        out_ref[span, :] = (field_ref[span, :].astype(F32) + out).astype(BF16)
        copies.append(pltpu.make_async_copy(out_ref.at[span], out_hbm.at[span], out_sems.at[i]))
        copies[-1].start()
    ones = jnp.ones((2 * TILE, rows), BF16)
    t = dot(jnp.concatenate([table_ref[...], ones], axis=0), gpre_ref[...])
    by_out = dot(cot_t_ref[...], hidden_ref[...])
    sums_out = dot(ones, cot_ref[...])
    b_in = t[2 * count : 2 * count + 1]
    t_parts = stack_parts(t[: 2 * count])
    grad_modal = dot(t_parts, win_t_ref[...])
    grad_modal = 2.0 * (grad_modal[: 2 * count] + grad_modal[2 * count :])
    mixed_t = mixed.T.astype(BF16)
    by_in = dot(jnp.concatenate([mixed_t, mixed_t], axis=1), t_parts)
    g_in = by_in[:chans, :hid] + by_in[chans:, hid:]
    g_out = by_out[:chans, :hid] + by_out[chans:, hid:]
    b_in = b_in[:, :hid] + b_in[:, hid:]
    b_out = (sums_out + pltpu.roll(sums_out, chans, 1))[:1]
    row = row_id((count, LANES))
    bias = jnp.where(
        row == 0,
        b_in[:, :LANES],
        jnp.where(row == 1, b_in[:, LANES:], jnp.where(row == 2, b_out, 0.0)),
    )
    for r, block in enumerate(
        (
            grad_modal[:count],
            grad_modal[count:],
            g_in[:, :LANES],
            g_in[:, LANES:],
            g_out[:, :LANES],
            g_out[:, LANES:],
            *split(bias),
        )
    ):
        sums_ref[pl.ds(r, count, stride=TILE), :] = block
    parts_ref[...] = sums_ref[...].astype(BF16)
    for copy in copies:
        copy.wait()


def stack_parts(x):
    high, low = split(x)
    return jnp.concatenate([high, low], axis=0).astype(BF16)


def split(x):
    high = x.astype(BF16).astype(F32)
    return high, x - high


def share_kernel(recv_ref, modal_ref, weights_ref, share_ref, grad_in_ref):
    x = jnp.sum(recv_ref[...].astype(F32).reshape(-1, TILE, LANES), axis=0)
    x = jnp.where(row_id(x.shape) == 6, x + pltpu.roll(x, TILE - 1, 0), x)
    both = jnp.concatenate([x, modal_ref[...]], axis=0)
    share_ref[...] = jnp.concatenate([both] * (share_ref.shape[0] // (2 * TILE)), axis=0)
    grad = jnp.concatenate([x[:2]] * (TILE // 2), axis=0)
    grad_in_ref[...] = complex_rows(grad, weights_ref[...], 1, 1.0)


def total_kernel(scale, shares_ref, grad_in_ref, out_ref):
    x = jnp.sum(shares_ref[...].reshape(-1, 2 * TILE, LANES), axis=0)[:TILE]
    own = jnp.where(row_id((TILE, LANES)) < 2, grad_in_ref[...], x * scale)
    out_ref[...] = jnp.concatenate([own] * (out_ref.shape[0] // TILE), axis=0).astype(BF16)


def final_kernel(
    scale,
    recv_ref,
    shares_ref,
    table_tt_ref,
    cot_ref,
    fgrad_ref,
    spectral_ref,
    win_ref,
    wout_ref,
    bin_ref,
    bout_ref,
    wide_ref,
):
    count = table_tt_ref.shape[1] // 4
    wide_ref[...] = recv_ref[...].astype(F32)
    rows = [every(wide_ref, r, count, TILE) for r in range(TILE - 1)]
    grad_in = jnp.concatenate(rows[:2], axis=0).astype(BF16)
    back = dot(table_tt_ref[:, : 2 * count], grad_in)
    fgrad_ref[...] = (cot_ref[...].astype(F32) + back).astype(BF16)
    win_ref[:, :LANES] = rows[2]
    win_ref[:, LANES:] = rows[3]
    wout_ref[:, :LANES] = rows[4]
    wout_ref[:, LANES:] = rows[5]
    bin_ref[:, :LANES] = rows[6][0:1]
    bin_ref[:, LANES:] = rows[6][1:2]
    bout_ref[...] = rows[6][2:3, : bout_ref.shape[1]]
    spectral_sums(scale, shares_ref, spectral_ref)


def spectral_sums(scale, shares_ref, out_ref):
    n = shares_ref.shape[0] // (2 * TILE)
    d_re, d_im, u_re, u_im = (every(shares_ref, r, n, 2 * TILE) for r in (0, 1, TILE, TILE + 1))
    left_high, left_low = split(jnp.concatenate([u_re, u_im], axis=0))
    right_high, right_low = split(
        jnp.concatenate(
            [jnp.concatenate([d_re, d_im], axis=0), jnp.concatenate([d_im, -d_re], axis=0)], axis=1
        )
    )
    left = jnp.concatenate([left_high, left_high, left_low], axis=0).astype(BF16)
    right = jnp.concatenate([right_high, right_low, right_high], axis=0).astype(BF16)
    outer = lax.dot_general(left, right, (((0,), (0,)), ((), ())), preferred_element_type=F32)
    c = LANES // 2
    out_ref[0] = (outer[:c, :c] + outer[c:, c : 2 * c]) * scale
    out_ref[1] = (outer[:c, 2 * c : 3 * c] + outer[c:, 3 * c :]) * scale


def exchange(x, axis):
    return lax.all_to_all(x, axis, 0, 0, tiled=True)


def exchange_pairs(x, axis):
    n = x.shape[0] // 2
    return exchange(x.reshape(n, 2, LANES), axis).reshape(2 * n, LANES)


def exchange_tiles(x, axis):
    n = x.shape[0] // TILE
    return exchange(x.reshape(n, TILE, LANES), axis).reshape(TILE * n, LANES)


def twice_diag(x):
    zero = jnp.zeros_like(x)
    return jnp.concatenate(
        [jnp.concatenate([x, zero], axis=1), jnp.concatenate([zero, x], axis=1)], axis=0
    )


def local(field, cotangent, mode_blocks, spectral, w_in, b_in, w_out, b_out):
    rows, width = field.shape
    chans, hid = w_in.shape
    ncol = width // chans
    grid = lax.axis_size("grid")
    dp = lax.axis_size("dp")
    inv_cols = 1.0 / (ncol * dp)
    count = mode_blocks.shape[0] * BLK
    s_re, s_im = spectral[0, 0], spectral[1, 0]
    mix_weights = jnp.concatenate([twice_diag(s_re), twice_diag(s_im)], axis=1)
    back_weights = jnp.concatenate([twice_diag(s_re), twice_diag(s_im)], axis=0)
    w_in_two, w_out_two = twice_diag(w_in), twice_diag(w_out)
    w_in_back, w_out_back = twice_diag(w_in.T), twice_diag(w_out.T)
    b_in_two = jnp.concatenate([b_in, b_in]).reshape(1, 2 * hid)
    b_out_two = jnp.concatenate([b_out, b_out]).reshape(1, width)

    modal, table = call(
        modal_kernel,
        "modal",
        [((2 * count, width), BF16), ((2 * count, rows), BF16)],
        [HBM, HBM],
        [
            pltpu.SMEM(mode_blocks.shape, jnp.int32),
            pltpu.VMEM((rows, width), BF16),
            pltpu.VMEM((2 * count, width), F32),
            pltpu.SemaphoreType.DMA,
            pltpu.SemaphoreType.DMA,
        ],
    )(
        pltpu.with_memory_space_constraint(mode_blocks, pltpu.HBM),
        pltpu.with_memory_space_constraint(field, pltpu.HBM),
    )
    recv, ready = lax.optimization_barrier(
        (
            exchange_pairs(modal, "grid"),
            (
                jnp.concatenate([table.T, table.T], axis=1),
                cotangent.T,
                mix_weights,
                back_weights,
                w_in_two,
                w_in_back,
                b_in_two,
                w_out_two,
                w_out_back,
                b_out_two,
            ),
        )
    )
    table_tt, cotangent_t, mix_weights, back_weights = ready[:4]
    w_in_two, w_in_back, b_in_two, w_out_two, w_out_back, b_out_two = ready[4:]
    mixed, modal_sum = call(
        mix_kernel, "mix", [((2 * grid, width), BF16), ((TILE, width), F32)], [VMEM] * 2
    )(recv, mix_weights)
    piece = exchange_pairs(mixed, "grid")

    output, parts = call(
        functools.partial(cells_kernel, 256),
        "cells",
        [((rows, width), BF16, HBM), ((TILE * grid, width), BF16)],
        [VMEM] * 12,
        [
            pltpu.VMEM((2 * count, width), F32),
            pltpu.VMEM((rows, 2 * hid), BF16),
            pltpu.VMEM((rows, 2 * hid), BF16),
            pltpu.VMEM((rows, width), BF16),
            pltpu.VMEM((TILE * grid, width), F32),
            pltpu.SemaphoreType.DMA((rows // 256,)),
        ],
    )(
        piece,
        table,
        table_tt,
        field,
        cotangent,
        cotangent_t,
        w_in_two,
        w_in_back,
        b_in_two,
        w_out_two,
        w_out_back,
        b_out_two,
    )
    share, grad_in = call(
        share_kernel, "share", [((2 * TILE * dp, width), F32), ((TILE, width), F32)], [VMEM] * 3
    )(exchange_tiles(parts, "grid"), modal_sum, back_weights)
    shares = exchange(share, "dp")
    (own,) = call(
        functools.partial(total_kernel, inv_cols), "total", [((TILE * grid, width), BF16)], [VMEM] * 2
    )(shares, grad_in)
    field_grad, spectral_grad, w_in_grad, w_out_grad, b_in_grad, b_out_grad = call(
        functools.partial(final_kernel, inv_cols),
        "final",
        [
            ((rows, width), BF16),
            ((2, chans, chans), F32),
            ((chans, hid), F32),
            ((chans, hid), F32),
            ((1, hid), F32),
            ((1, chans), F32),
        ],
        [VMEM] * 4,
        [pltpu.VMEM((TILE * grid, width), F32)],
    )(exchange(own, "grid"), shares, table_tt, cotangent)
    return (
        output,
        field_grad,
        spectral_grad.reshape(2, 1, chans, chans),
        w_in_grad,
        b_in_grad.reshape(hid),
        w_out_grad.T,
        b_out_grad.reshape(chans),
    )


def solution(mesh):
    in_specs = (
        P("grid", "dp"),
        P("grid", "dp"),
        P(),
        P(None, "grid", None, None),
        P(),
        P(),
        P(),
        P(),
    )
    out_specs = (P("grid", "dp"), P("grid", "dp"), P(None, "grid", None, None), P(), P(), P(), P())
    return jax.shard_map(local, mesh=mesh, in_specs=in_specs, out_specs=out_specs, check_vma=False)
```

```python
import functools
import math

import jax
import jax.numpy as jnp
from jax import lax
from jax.experimental import pallas as pl
from jax.experimental.pallas import tpu as pltpu
from jax.sharding import PartitionSpec as P

NX = 65536
BLK = 8
LANES = 128
TILE = 8
F32 = jnp.float32
BF16 = jnp.bfloat16
VMEM = pl.BlockSpec(memory_space=pltpu.VMEM)
HBM = pl.BlockSpec(memory_space=pltpu.HBM)


def call(kernel, name, outs, specs, scratch=()):
    return pl.pallas_call(
        kernel,
        name=name,
        out_shape=[jax.ShapeDtypeStruct(o[0], o[1]) for o in outs],
        in_specs=specs,
        out_specs=[o[2] if len(o) > 2 else VMEM for o in outs],
        scratch_shapes=list(scratch),
        compiler_params=pltpu.CompilerParams(vmem_limit_bytes=48 << 20),
    )


def dot(a, b):
    return jnp.dot(a, b, preferred_element_type=F32)


def row_id(shape):
    return lax.broadcasted_iota(jnp.int32, shape, 0)


def every(ref, start, count, step):
    return ref[pl.ds(start, count, stride=step), :]


def cos_sin(turn):
    quarter = NX // 4
    quad = (turn + quarter // 2) >> (quarter.bit_length() - 1)
    rest = (turn - quad * quarter).astype(F32) * (2.0 * math.pi / NX)
    sq = rest * rest
    sin = rest * (1.0 + sq * (-1 / 6 + sq * (1 / 120 + sq * (-1 / 5040 + sq * (1 / 362880)))))
    cos = 1.0 + sq * (
        -1 / 2 + sq * (1 / 24 + sq * (-1 / 720 + sq * (1 / 40320 + sq * (-1 / 3628800))))
    )
    odd = (quad & 1) == 1
    c = jnp.where(odd, sin, cos)
    s = jnp.where(odd, cos, sin)
    return jnp.where(((quad + 1) & 2) != 0, -c, c), jnp.where((quad & 2) != 0, -s, s)


def modal_kernel(
    blocks_hbm, field_hbm, modal_ref, table_ref, blocks_ref, field_ref, wide_ref, blocks_sem, field_sem
):
    blocks_copy = pltpu.make_async_copy(blocks_hbm, blocks_ref, blocks_sem)
    blocks_copy.start()
    field_copy = pltpu.make_async_copy(field_hbm, field_ref, field_sem)
    field_copy.start()
    blocks_copy.wait()
    kblocks = blocks_ref.shape[0]
    count = kblocks * BLK
    rows = field_ref.shape[0]
    first = lax.axis_index("grid") * rows
    base = jnp.concatenate(
        [jnp.full((BLK, LANES), blocks_ref[b] * BLK, jnp.int32) for b in range(kblocks)], axis=0
    )
    modes = base + row_id((count, LANES)) % BLK
    lane = lax.broadcasted_iota(jnp.int32, (count, LANES), 1)
    scale = 1.0 / math.sqrt(NX)
    near_c, near_s = cos_sin((modes * lane) & (NX - 1))
    near_c, near_s = near_c * scale, near_s * scale
    far_c, far_s = cos_sin((modes * (first + lane * LANES)) & (NX - 1))
    for a in range(rows // LANES):
        ca = jnp.broadcast_to(far_c[:, a : a + 1], (count, LANES))
        sa = jnp.broadcast_to(far_s[:, a : a + 1], (count, LANES))
        span = pl.ds(a * LANES, LANES)
        table_ref[:count, span] = (near_c * ca - near_s * sa).astype(BF16)
        table_ref[count:, span] = (-(near_s * ca + near_c * sa)).astype(BF16)
    field_copy.wait()
    modal = dot(table_ref[...], field_ref[...])
    wide_ref[pl.ds(0, count, stride=2), :] = modal[:count]
    wide_ref[pl.ds(1, count, stride=2), :] = modal[count:]
    modal_ref[...] = wide_ref[...].astype(BF16)


def prepare_kernel(
    spectral_hbm,
    win_hbm,
    wout_hbm,
    bin_hbm,
    bout_hbm,
    cot_hbm,
    field_hbm,
    table_ref,
    mix_ref,
    back_ref,
    win_two_ref,
    win_back_ref,
    bin_two_ref,
    wout_two_ref,
    wout_back_ref,
    bout_two_ref,
    table_tt_ref,
    cot_ref,
    cot_t_ref,
    field_ref,
    s_ref,
    win_ref,
    wout_ref,
    bin_ref,
    bout_ref,
    sems,
):
    pairs = (
        (spectral_hbm, s_ref),
        (win_hbm, win_ref),
        (wout_hbm, wout_ref),
        (bin_hbm, bin_ref),
        (bout_hbm, bout_ref),
        (cot_hbm, cot_ref),
        (field_hbm, field_ref),
    )
    copies = [pltpu.make_async_copy(a, b, sems.at[i]) for i, (a, b) in enumerate(pairs)]
    for copy in copies:
        copy.start()
    rows = cot_ref.shape[0]
    width = 2 * table_ref.shape[0]
    for a in range(rows // LANES):
        span = pl.ds(a * LANES, LANES)
        flipped = table_ref[:, span].astype(F32).T.astype(BF16)
        table_tt_ref[span, : width // 2] = flipped
        table_tt_ref[span, width // 2 :] = flipped
    for copy in copies:
        copy.wait()
    s_re, s_im = twice_diag(s_ref[0]), twice_diag(s_ref[1])
    mix_ref[...] = jnp.concatenate([s_re, s_im], axis=1)
    back_ref[...] = jnp.concatenate([s_re, s_im], axis=0)
    put_twice_diag(win_two_ref, win_back_ref, win_ref[...])
    put_twice_diag(wout_back_ref, wout_two_ref, wout_ref[...])
    bin_two_ref[...] = jnp.concatenate([bin_ref[...]] * 2, axis=1)
    bout_two_ref[...] = jnp.concatenate([bout_ref[...]] * 2, axis=1)
    for a in range(rows // LANES):
        span = pl.ds(a * LANES, LANES)
        cot_t_ref[:, span] = cot_ref[span, :].astype(F32).T.astype(BF16)


def put_twice_diag(wide_ref, tall_ref, x):
    chans, hid = x.shape
    wide_ref[...] = jnp.zeros_like(wide_ref)
    wide_ref[:chans, :hid] = x
    wide_ref[chans:, hid:] = x
    flipped = x.astype(F32).T.astype(BF16)
    zero = jnp.zeros_like(flipped)
    tall_ref[:hid, :] = jnp.concatenate([flipped, zero], axis=1)
    tall_ref[hid:, :] = jnp.concatenate([zero, flipped], axis=1)


def complex_rows(x, weights, axis, sign):
    high = x.astype(BF16).astype(F32)
    rest = x - high
    mid = rest.astype(BF16).astype(F32)
    low = rest - mid
    row = row_id(x.shape)
    left = jnp.where(row < 2, high, jnp.where(row < 4, mid, jnp.where(row < 6, low, 0.0)))
    dims = (((1,), (axis,)), ((), ()))
    y = lax.dot_general(left.astype(BF16), weights, dims, preferred_element_type=F32)
    y = y + pltpu.roll(y, 4, 0)
    y = y + pltpu.roll(y, 2, 0)
    by_re = y[:, :LANES]
    by_im = pltpu.roll(y[:, LANES:], 1, 0)
    return by_re + jnp.where(row % 2 == 0, sign, -sign) * by_im


def mix_kernel(recv_ref, weights_ref, out_ref, sum_ref):
    x = jnp.sum(recv_ref[...].astype(F32).reshape(-1, TILE, LANES), axis=0)
    x = x + pltpu.roll(x, 4, 0)
    x = x + pltpu.roll(x, 2, 0)
    sum_ref[...] = x
    mixed = complex_rows(x, weights_ref[...], 0, -1.0)
    out_ref[...] = jnp.concatenate([mixed] * (out_ref.shape[0] // TILE), axis=0).astype(BF16)


def gelu_pair(pre):
    k = math.sqrt(2.0 / math.pi)
    sq = pre * pre
    t = jnp.tanh(pre * (k + (0.044715 * k) * sq))
    half = 0.5 * pre
    up = 1.0 + t
    return half * up, up * (0.5 + half * (1.0 - t) * (k + (3 * 0.044715 * k) * sq))


def cells_kernel(
    chunk,
    piece_ref,
    table_ref,
    table_tt_ref,
    field_ref,
    cot_ref,
    cot_t_ref,
    win_ref,
    win_t_ref,
    bin_ref,
    wout_ref,
    wout_t_ref,
    bout_ref,
    out_hbm,
    parts_ref,
    wide_ref,
    hidden_ref,
    gpre_ref,
    out_ref,
    sums_ref,
    out_sems,
):
    rows = field_ref.shape[0]
    count = table_ref.shape[0] // 2
    hid = bin_ref.shape[1] // 2
    chans = LANES // 2
    wide_ref[...] = 2.0 * piece_ref[...].astype(F32)
    mixed = jnp.concatenate([every(wide_ref, 0, count, 2), every(wide_ref, 1, count, 2)], axis=0)
    right = stack_parts(dot(mixed.astype(BF16), win_ref[...]))
    copies = []
    for i in range(rows // chunk):
        span = pl.ds(i * chunk, chunk)
        pre = dot(table_tt_ref[span, :], right) + bin_ref[...]
        gate, slope = gelu_pair(pre)
        hidden = gate.astype(BF16)
        hidden_ref[span, :] = hidden
        gpre_ref[span, :] = (dot(cot_ref[span, :], wout_t_ref[...]) * slope).astype(BF16)
        out = dot(hidden, wout_ref[...]) + bout_ref[...]
        out_ref[span, :] = (field_ref[span, :].astype(F32) + out).astype(BF16)
        copies.append(pltpu.make_async_copy(out_ref.at[span], out_hbm.at[span], out_sems.at[i]))
        copies[-1].start()
    ones = jnp.ones((2 * TILE, rows), BF16)
    t = dot(jnp.concatenate([table_ref[...], ones], axis=0), gpre_ref[...])
    by_out = dot(cot_t_ref[...], hidden_ref[...])
    sums_out = dot(ones, cot_ref[...])
    b_in = t[2 * count : 2 * count + 1]
    t_parts = stack_parts(t[: 2 * count])
    grad_modal = dot(t_parts, win_t_ref[...])
    grad_modal = 2.0 * (grad_modal[: 2 * count] + grad_modal[2 * count :])
    mixed_t = mixed.T.astype(BF16)
    by_in = dot(jnp.concatenate([mixed_t, mixed_t], axis=1), t_parts)
    g_in = by_in[:chans, :hid] + by_in[chans:, hid:]
    g_out = by_out[:chans, :hid] + by_out[chans:, hid:]
    b_in = b_in[:, :hid] + b_in[:, hid:]
    b_out = (sums_out + pltpu.roll(sums_out, chans, 1))[:1]
    row = row_id((count, LANES))
    bias = jnp.where(
        row == 0,
        b_in[:, :LANES],
        jnp.where(row == 1, b_in[:, LANES:], jnp.where(row == 2, b_out, 0.0)),
    )
    for r, block in enumerate(
        (
            grad_modal[:count],
            grad_modal[count:],
            g_in[:, :LANES],
            g_in[:, LANES:],
            g_out[:, :LANES],
            g_out[:, LANES:],
            *split(bias),
        )
    ):
        sums_ref[pl.ds(r, count, stride=TILE), :] = block
    parts_ref[...] = sums_ref[...].astype(BF16)
    for copy in copies:
        copy.wait()


def stack_parts(x):
    high, low = split(x)
    return jnp.concatenate([high, low], axis=0).astype(BF16)


def split(x):
    high = x.astype(BF16).astype(F32)
    return high, x - high


def share_kernel(recv_ref, modal_ref, weights_ref, share_ref, grad_in_ref):
    x = jnp.sum(recv_ref[...].astype(F32).reshape(-1, TILE, LANES), axis=0)
    x = jnp.where(row_id(x.shape) == 6, x + pltpu.roll(x, TILE - 1, 0), x)
    both = jnp.concatenate([x, modal_ref[...]], axis=0)
    share_ref[...] = jnp.concatenate([both] * (share_ref.shape[0] // (2 * TILE)), axis=0)
    grad = jnp.concatenate([x[:2]] * (TILE // 2), axis=0)
    grad_in_ref[...] = complex_rows(grad, weights_ref[...], 1, 1.0)


def total_kernel(scale, shares_ref, grad_in_ref, out_ref):
    x = jnp.sum(shares_ref[...].reshape(-1, 2 * TILE, LANES), axis=0)[:TILE]
    own = jnp.where(row_id((TILE, LANES)) < 2, grad_in_ref[...], x * scale)
    out_ref[...] = jnp.concatenate([own] * (out_ref.shape[0] // TILE), axis=0).astype(BF16)


def final_kernel(
    scale,
    recv_ref,
    shares_ref,
    table_tt_ref,
    cot_ref,
    fgrad_ref,
    spectral_ref,
    win_ref,
    wout_ref,
    bin_ref,
    bout_ref,
    wide_ref,
):
    count = table_tt_ref.shape[1] // 4
    wide_ref[...] = recv_ref[...].astype(F32)
    rows = [every(wide_ref, r, count, TILE) for r in range(TILE - 1)]
    grad_in = jnp.concatenate(rows[:2], axis=0).astype(BF16)
    back = dot(table_tt_ref[:, : 2 * count], grad_in)
    fgrad_ref[...] = (cot_ref[...].astype(F32) + back).astype(BF16)
    win_ref[:, :LANES] = rows[2]
    win_ref[:, LANES:] = rows[3]
    wout_ref[:, :LANES] = rows[4]
    wout_ref[:, LANES:] = rows[5]
    bin_ref[:, :LANES] = rows[6][0:1]
    bin_ref[:, LANES:] = rows[6][1:2]
    bout_ref[...] = rows[6][2:3, : bout_ref.shape[1]]
    spectral_sums(scale, shares_ref, spectral_ref)


def spectral_sums(scale, shares_ref, out_ref):
    n = shares_ref.shape[0] // (2 * TILE)
    d_re, d_im, u_re, u_im = (every(shares_ref, r, n, 2 * TILE) for r in (0, 1, TILE, TILE + 1))
    left_high, left_low = split(jnp.concatenate([u_re, u_im], axis=0))
    right_high, right_low = split(
        jnp.concatenate(
            [jnp.concatenate([d_re, d_im], axis=0), jnp.concatenate([d_im, -d_re], axis=0)], axis=1
        )
    )
    left = jnp.concatenate([left_high, left_high, left_low], axis=0).astype(BF16)
    right = jnp.concatenate([right_high, right_low, right_high], axis=0).astype(BF16)
    outer = lax.dot_general(left, right, (((0,), (0,)), ((), ())), preferred_element_type=F32)
    c = LANES // 2
    out_ref[0] = (outer[:c, :c] + outer[c:, c : 2 * c]) * scale
    out_ref[1] = (outer[:c, 2 * c : 3 * c] + outer[c:, 3 * c :]) * scale


def exchange(x, axis):
    return lax.all_to_all(x, axis, 0, 0, tiled=True)


def exchange_pairs(x, axis):
    n = x.shape[0] // 2
    return exchange(x.reshape(n, 2, LANES), axis).reshape(2 * n, LANES)


def exchange_tiles(x, axis):
    n = x.shape[0] // TILE
    return exchange(x.reshape(n, TILE, LANES), axis).reshape(TILE * n, LANES)


def twice_diag(x):
    zero = jnp.zeros_like(x)
    return jnp.concatenate(
        [jnp.concatenate([x, zero], axis=1), jnp.concatenate([zero, x], axis=1)], axis=0
    )


def local(field, cotangent, mode_blocks, spectral, w_in, b_in, w_out, b_out):
    rows, width = field.shape
    chans, hid = w_in.shape
    ncol = width // chans
    grid = lax.axis_size("grid")
    dp = lax.axis_size("dp")
    inv_cols = 1.0 / (ncol * dp)
    count = mode_blocks.shape[0] * BLK

    modal, table = call(
        modal_kernel,
        "modal",
        [((2 * count, width), BF16), ((2 * count, rows), BF16)],
        [HBM, HBM],
        [
            pltpu.SMEM(mode_blocks.shape, jnp.int32),
            pltpu.VMEM((rows, width), BF16),
            pltpu.VMEM((2 * count, width), F32),
            pltpu.SemaphoreType.DMA,
            pltpu.SemaphoreType.DMA,
        ],
    )(
        pltpu.with_memory_space_constraint(mode_blocks, pltpu.HBM),
        pltpu.with_memory_space_constraint(field, pltpu.HBM),
    )
    recv = exchange_pairs(modal, "grid")
    sources = (
        spectral.reshape(2, chans, chans),
        w_in,
        w_out.T,
        b_in.reshape(1, hid),
        b_out.reshape(1, chans),
        cotangent,
        field,
    )
    (
        mix_weights,
        back_weights,
        w_in_two,
        w_in_back,
        b_in_two,
        w_out_two,
        w_out_back,
        b_out_two,
        table_tt,
        cotangent_here,
        cotangent_t,
        field_here,
    ) = call(
        prepare_kernel,
        "prepare",
        [
            ((width, 2 * width), BF16),
            ((2 * width, width), BF16),
            ((width, 2 * hid), BF16),
            ((2 * hid, width), BF16),
            ((1, 2 * hid), F32),
            ((2 * hid, width), BF16),
            ((width, 2 * hid), BF16),
            ((1, width), F32),
            ((rows, 4 * count), BF16),
            ((rows, width), BF16),
            ((width, rows), BF16),
            ((rows, width), BF16),
        ],
        [HBM] * len(sources) + [VMEM],
        [pltpu.VMEM(a.shape, a.dtype) for a in sources[:5]]
        + [pltpu.SemaphoreType.DMA((len(sources),))],
    )(*(pltpu.with_memory_space_constraint(a, pltpu.HBM) for a in sources), table)
    mixed, modal_sum = call(
        mix_kernel, "mix", [((2 * grid, width), BF16), ((TILE, width), F32)], [VMEM] * 2
    )(recv, mix_weights)
    piece = exchange_pairs(mixed, "grid")

    output, parts = call(
        functools.partial(cells_kernel, 256),
        "cells",
        [((rows, width), BF16, HBM), ((TILE * grid, width), BF16)],
        [VMEM] * 12,
        [
            pltpu.VMEM((2 * count, width), F32),
            pltpu.VMEM((rows, 2 * hid), BF16),
            pltpu.VMEM((rows, 2 * hid), BF16),
            pltpu.VMEM((rows, width), BF16),
            pltpu.VMEM((TILE * grid, width), F32),
            pltpu.SemaphoreType.DMA((rows // 256,)),
        ],
    )(
        piece,
        table,
        table_tt,
        field_here,
        cotangent_here,
        cotangent_t,
        w_in_two,
        w_in_back,
        b_in_two,
        w_out_two,
        w_out_back,
        b_out_two,
    )
    share, grad_in = call(
        share_kernel, "share", [((2 * TILE * dp, width), F32), ((TILE, width), F32)], [VMEM] * 3
    )(exchange_tiles(parts, "grid"), modal_sum, back_weights)
    shares = exchange(share, "dp")
    (own,) = call(
        functools.partial(total_kernel, inv_cols), "total", [((TILE * grid, width), BF16)], [VMEM] * 2
    )(shares, grad_in)
    field_grad, spectral_grad, w_in_grad, w_out_grad, b_in_grad, b_out_grad = call(
        functools.partial(final_kernel, inv_cols),
        "final",
        [
            ((rows, width), BF16),
            ((2, chans, chans), F32),
            ((chans, hid), F32),
            ((chans, hid), F32),
            ((1, hid), F32),
            ((1, chans), F32),
        ],
        [VMEM] * 4,
        [pltpu.VMEM((TILE * grid, width), F32)],
    )(exchange(own, "grid"), shares, table_tt, cotangent_here)
    return (
        output,
        field_grad,
        spectral_grad.reshape(2, 1, chans, chans),
        w_in_grad,
        b_in_grad.reshape(hid),
        w_out_grad.T,
        b_out_grad.reshape(chans),
    )


def solution(mesh):
    in_specs = (
        P("grid", "dp"),
        P("grid", "dp"),
        P(),
        P(None, "grid", None, None),
        P(),
        P(),
        P(),
        P(),
    )
    out_specs = (P("grid", "dp"), P("grid", "dp"), P(None, "grid", None, None), P(), P(), P(), P())
    return jax.shard_map(local, mesh=mesh, in_specs=in_specs, out_specs=out_specs, check_vma=False)
```

```python
import functools
import math

import jax
import jax.numpy as jnp
from jax import lax
from jax.experimental import pallas as pl
from jax.experimental.pallas import tpu as pltpu
from jax.sharding import PartitionSpec as P

NX = 65536
BLK = 8
LANES = 128
TILE = 8
F32 = jnp.float32
BF16 = jnp.bfloat16
VMEM = pl.BlockSpec(memory_space=pltpu.VMEM)
HBM = pl.BlockSpec(memory_space=pltpu.HBM)
OWN = 6


def call(kernel, name, outs, specs, scratch=()):
    return pl.pallas_call(
        kernel,
        name=name,
        out_shape=[jax.ShapeDtypeStruct(o[0], o[1]) for o in outs],
        in_specs=specs,
        out_specs=[o[2] if len(o) > 2 else VMEM for o in outs],
        scratch_shapes=list(scratch),
        compiler_params=pltpu.CompilerParams(vmem_limit_bytes=48 << 20),
    )


def dot(a, b):
    return jnp.dot(a, b, preferred_element_type=F32)


def row_id(shape):
    return lax.broadcasted_iota(jnp.int32, shape, 0)


def every(ref, start, count, step):
    return ref[pl.ds(start, count, stride=step), :]


def cos_sin(turn):
    quarter = NX // 4
    quad = (turn + quarter // 2) >> (quarter.bit_length() - 1)
    rest = (turn - quad * quarter).astype(F32) * (2.0 * math.pi / NX)
    sq = rest * rest
    sin = rest * (1.0 + sq * (-1 / 6 + sq * (1 / 120 + sq * (-1 / 5040 + sq * (1 / 362880)))))
    cos = 1.0 + sq * (
        -1 / 2 + sq * (1 / 24 + sq * (-1 / 720 + sq * (1 / 40320 + sq * (-1 / 3628800))))
    )
    odd = (quad & 1) == 1
    c = jnp.where(odd, sin, cos)
    s = jnp.where(odd, cos, sin)
    return jnp.where(((quad + 1) & 2) != 0, -c, c), jnp.where((quad & 2) != 0, -s, s)


def modal_kernel(
    blocks_hbm, field_hbm, modal_ref, table_ref, blocks_ref, field_ref, wide_ref, blocks_sem, field_sem
):
    blocks_copy = pltpu.make_async_copy(blocks_hbm, blocks_ref, blocks_sem)
    blocks_copy.start()
    field_copy = pltpu.make_async_copy(field_hbm, field_ref, field_sem)
    field_copy.start()
    blocks_copy.wait()
    kblocks = blocks_ref.shape[0]
    count = kblocks * BLK
    rows = field_ref.shape[0]
    first = lax.axis_index("grid") * rows
    base = jnp.concatenate(
        [jnp.full((BLK, LANES), blocks_ref[b] * BLK, jnp.int32) for b in range(kblocks)], axis=0
    )
    modes = base + row_id((count, LANES)) % BLK
    lane = lax.broadcasted_iota(jnp.int32, (count, LANES), 1)
    scale = 1.0 / math.sqrt(NX)
    near_c, near_s = cos_sin((modes * lane) & (NX - 1))
    near_c, near_s = near_c * scale, near_s * scale
    far_c, far_s = cos_sin((modes * (first + lane * LANES)) & (NX - 1))
    for a in range(rows // LANES):
        ca = jnp.broadcast_to(far_c[:, a : a + 1], (count, LANES))
        sa = jnp.broadcast_to(far_s[:, a : a + 1], (count, LANES))
        span = pl.ds(a * LANES, LANES)
        table_ref[:count, span] = (near_c * ca - near_s * sa).astype(BF16)
        table_ref[count:, span] = (-(near_s * ca + near_c * sa)).astype(BF16)
    field_copy.wait()
    modal = dot(table_ref[...], field_ref[...])
    wide_ref[pl.ds(0, count, stride=2), :] = modal[:count]
    wide_ref[pl.ds(1, count, stride=2), :] = modal[count:]
    modal_ref[...] = wide_ref[...].astype(BF16)


def prepare_kernel(
    blocks_hbm,
    spectral_hbm,
    win_hbm,
    wout_hbm,
    bin_hbm,
    bout_hbm,
    cot_hbm,
    field_hbm,
    table_ref,
    mix_ref,
    back_ref,
    win_two_ref,
    win_back_ref,
    bin_two_ref,
    wout_two_ref,
    wout_back_ref,
    bout_two_ref,
    table_tt_ref,
    cot_ref,
    cot_t_ref,
    field_ref,
    zero_row_ref,
    zero_own_ref,
    blocks_ref,
    s_ref,
    win_ref,
    wout_ref,
    bin_ref,
    bout_ref,
    sems,
):
    pairs = (
        (blocks_hbm, blocks_ref),
        (spectral_hbm, s_ref),
        (win_hbm, win_ref),
        (wout_hbm, wout_ref),
        (bin_hbm, bin_ref),
        (bout_hbm, bout_ref),
        (cot_hbm, cot_ref),
        (field_hbm, field_ref),
    )
    copies = [pltpu.make_async_copy(a, b, sems.at[i]) for i, (a, b) in enumerate(pairs)]
    for copy in copies:
        copy.start()
    rows = cot_ref.shape[0]
    width = 2 * table_ref.shape[0]
    for a in range(rows // LANES):
        span = pl.ds(a * LANES, LANES)
        flipped = table_ref[:, span].astype(F32).T.astype(BF16)
        table_tt_ref[span, : width // 2] = flipped
        table_tt_ref[span, width // 2 :] = flipped
    for copy in copies:
        copy.wait()
    count = zero_row_ref.shape[0]
    row = row_id((count, LANES))
    at = jnp.int32(0)
    for b in range(blocks_ref.shape[0]):
        at = jnp.where(blocks_ref[b] == 0, b * BLK, at)
    zero_row_ref[...] = jnp.where(row == at, 1.0, 0.0)
    own = jnp.full((TILE, LANES), lax.axis_index("grid"), jnp.int32)
    zero_own_ref[...] = jnp.where(own == at, 1.0, 0.0)
    s_re, s_im = twice_diag(s_ref[0]), twice_diag(s_ref[1])
    mix_ref[...] = jnp.concatenate([s_re, s_im], axis=1)
    back_ref[...] = jnp.concatenate([s_re, s_im], axis=0)
    put_twice_diag(win_two_ref, win_back_ref, win_ref[...])
    put_twice_diag(wout_back_ref, wout_two_ref, wout_ref[...])
    bin_two_ref[...] = jnp.concatenate([bin_ref[...]] * 2, axis=1)
    bout_two_ref[...] = jnp.concatenate([bout_ref[...]] * 2, axis=1)
    for a in range(rows // LANES):
        span = pl.ds(a * LANES, LANES)
        cot_t_ref[:, span] = cot_ref[span, :].astype(F32).T.astype(BF16)


def put_twice_diag(wide_ref, tall_ref, x):
    chans, hid = x.shape
    wide_ref[...] = jnp.zeros_like(wide_ref)
    wide_ref[:chans, :hid] = x
    wide_ref[chans:, hid:] = x
    flipped = x.astype(F32).T.astype(BF16)
    zero = jnp.zeros_like(flipped)
    tall_ref[:hid, :] = jnp.concatenate([flipped, zero], axis=1)
    tall_ref[hid:, :] = jnp.concatenate([zero, flipped], axis=1)


def complex_rows(x, weights, axis, sign):
    high = x.astype(BF16).astype(F32)
    rest = x - high
    mid = rest.astype(BF16).astype(F32)
    low = rest - mid
    row = row_id(x.shape)
    left = jnp.where(row < 2, high, jnp.where(row < 4, mid, jnp.where(row < 6, low, 0.0)))
    dims = (((1,), (axis,)), ((), ()))
    y = lax.dot_general(left.astype(BF16), weights, dims, preferred_element_type=F32)
    y = y + pltpu.roll(y, 4, 0)
    y = y + pltpu.roll(y, 2, 0)
    by_re = y[:, :LANES]
    by_im = pltpu.roll(y[:, LANES:], 1, 0)
    return by_re + jnp.where(row % 2 == 0, sign, -sign) * by_im


def mix_kernel(recv_ref, weights_ref, out_ref, sum_ref):
    x = jnp.sum(recv_ref[...].astype(F32).reshape(-1, TILE, LANES), axis=0)
    x = x + pltpu.roll(x, 4, 0)
    x = x + pltpu.roll(x, 2, 0)
    sum_ref[...] = x
    mixed = complex_rows(x, weights_ref[...], 0, -1.0)
    out_ref[...] = jnp.concatenate([mixed] * (out_ref.shape[0] // TILE), axis=0).astype(BF16)


def gelu_pair(pre):
    k = math.sqrt(2.0 / math.pi)
    sq = pre * pre
    t = jnp.tanh(pre * (k + (0.044715 * k) * sq))
    half = 0.5 * pre
    up = 1.0 + t
    return half * up, up * (0.5 + half * (1.0 - t) * (k + (3 * 0.044715 * k) * sq))


def cells_kernel(
    chunk,
    piece_ref,
    table_ref,
    table_tt_ref,
    field_ref,
    cot_ref,
    cot_t_ref,
    win_ref,
    win_t_ref,
    bin_ref,
    wout_ref,
    wout_t_ref,
    bout_ref,
    zero_row_ref,
    out_hbm,
    parts_ref,
    wide_ref,
    hidden_ref,
    gpre_ref,
    out_ref,
    sums_ref,
    out_sems,
):
    rows = field_ref.shape[0]
    count = table_ref.shape[0] // 2
    hid = bin_ref.shape[1] // 2
    chans = LANES // 2
    wide_ref[...] = 2.0 * piece_ref[...].astype(F32)
    mixed = jnp.concatenate([every(wide_ref, 0, count, 2), every(wide_ref, 1, count, 2)], axis=0)
    right = stack_parts(dot(mixed.astype(BF16), win_ref[...]))
    copies = []
    for i in range(rows // chunk):
        span = pl.ds(i * chunk, chunk)
        pre = dot(table_tt_ref[span, :], right) + bin_ref[...]
        gate, slope = gelu_pair(pre)
        hidden = gate.astype(BF16)
        hidden_ref[span, :] = hidden
        gpre_ref[span, :] = (dot(cot_ref[span, :], wout_t_ref[...]) * slope).astype(BF16)
        out = dot(hidden, wout_ref[...]) + bout_ref[...]
        out_ref[span, :] = (field_ref[span, :].astype(F32) + out).astype(BF16)
        copies.append(pltpu.make_async_copy(out_ref.at[span], out_hbm.at[span], out_sems.at[i]))
        copies[-1].start()
    ones = jnp.ones((2 * TILE, rows), BF16)
    t = dot(jnp.concatenate([table_ref[...], ones], axis=0), gpre_ref[...])
    by_out = dot(cot_t_ref[...], hidden_ref[...])
    sums_out = dot(ones, cot_ref[...])
    b_in = t[2 * count : 2 * count + 1]
    t_parts = stack_parts(t[: 2 * count])
    grad_modal = dot(t_parts, win_t_ref[...])
    grad_modal = 2.0 * (grad_modal[: 2 * count] + grad_modal[2 * count :])
    mixed_t = mixed.T.astype(BF16)
    by_in = dot(jnp.concatenate([mixed_t, mixed_t], axis=1), t_parts)
    g_in = by_in[:chans, :hid] + by_in[chans:, hid:]
    g_out = by_out[:chans, :hid] + by_out[chans:, hid:]
    b_in = b_in[:, :hid] + b_in[:, hid:]
    b_out = halves((sums_out + pltpu.roll(sums_out, chans, 1))[:1])
    for r, block in enumerate(
        (
            grad_modal[:count],
            jnp.where(zero_row_ref[...] > 0.0, b_out, grad_modal[count:]),
            g_in[:, :LANES],
            g_in[:, LANES:],
            g_out[:, :LANES],
            g_out[:, LANES:],
            jnp.broadcast_to(b_in[:, :LANES], (count, LANES)),
            jnp.broadcast_to(b_in[:, LANES:], (count, LANES)),
        )
    ):
        sums_ref[pl.ds(r, count, stride=TILE), :] = block
    parts_ref[...] = sums_ref[...].astype(BF16)
    for copy in copies:
        copy.wait()


def stack_parts(x):
    high, low = split(x)
    return jnp.concatenate([high, low], axis=0).astype(BF16)


def halves(x):
    high, low = split(x)
    lane = lax.broadcasted_iota(jnp.int32, x.shape, 1)
    return jnp.where(lane < LANES // 2, high, low)


def split(x):
    high = x.astype(BF16).astype(F32)
    return high, x - high


def share_kernel(recv_ref, modal_ref, weights_ref, zero_own_ref, share_ref, grad_in_ref):
    x = jnp.sum(recv_ref[...].astype(F32).reshape(-1, TILE, LANES), axis=0)
    row = row_id(x.shape)
    owner = zero_own_ref[...] > 0.0
    extra = jnp.where(owner & (row == 2), pltpu.roll(x, 1, 0), 0.0)
    x = jnp.where(owner & (row == 1), 0.0, x)
    both = jnp.concatenate([x, jnp.where(row < 2, modal_ref[...], extra)], axis=0)
    share_ref[...] = jnp.concatenate([both] * (share_ref.shape[0] // (2 * TILE)), axis=0)
    grad = jnp.concatenate([x[:2]] * (TILE // 2), axis=0)
    grad_in_ref[...] = complex_rows(grad, weights_ref[...], 1, 1.0)


def total_kernel(scale, shares_ref, grad_in_ref, zero_own_ref, out_ref):
    x = jnp.sum(shares_ref[...].reshape(-1, 2 * TILE, LANES), axis=0) * scale
    bias = x[TILE + 2 : TILE + 3]
    bias = halves(bias + pltpu.roll(bias, LANES // 2, 1))
    row = row_id((TILE, LANES))
    own = jnp.where(row < 2, grad_in_ref[...], x[:TILE])
    own = jnp.where((zero_own_ref[...] > 0.0) & (row == 1), bias, own)
    group = jnp.concatenate([own[:OWN]] * 4, axis=0)
    out_ref[...] = jnp.concatenate([group] * (out_ref.shape[0] // (4 * OWN)), axis=0).astype(BF16)


def final_kernel(
    scale,
    recv_ref,
    shares_ref,
    table_tt_ref,
    cot_ref,
    zero_row_ref,
    fgrad_ref,
    spectral_ref,
    win_ref,
    wout_ref,
    bin_ref,
    bout_ref,
    wide_ref,
):
    count = table_tt_ref.shape[1] // 4
    wide_ref[...] = recv_ref[...].astype(F32)
    rows = [every(wide_ref, r, count, OWN) for r in range(OWN)]
    grad_in = jnp.concatenate(rows[:2], axis=0).astype(BF16)
    back = dot(table_tt_ref[:, : 2 * count], grad_in)
    fgrad_ref[...] = (cot_ref[...].astype(F32) + back).astype(BF16)
    win_ref[:, :LANES] = rows[2]
    win_ref[:, LANES:] = rows[3]
    wout_ref[:, :LANES] = rows[4]
    wout_ref[:, LANES:] = rows[5]
    n = shares_ref.shape[0] // (2 * TILE)
    for r in range(2):
        b_in = jnp.sum(every(shares_ref, OWN + r, n, 2 * TILE), axis=0, keepdims=True)
        bin_ref[:, r * LANES : (r + 1) * LANES] = b_in * scale
    b_out = jnp.sum(jnp.where(zero_row_ref[...] > 0.0, rows[1], 0.0), axis=0, keepdims=True)
    bout_ref[...] = (b_out + pltpu.roll(b_out, LANES // 2, 1))[:, : bout_ref.shape[1]]
    spectral_sums(scale, shares_ref, spectral_ref)


def spectral_sums(scale, shares_ref, out_ref):
    n = shares_ref.shape[0] // (2 * TILE)
    d_re, d_im, u_re, u_im = (every(shares_ref, r, n, 2 * TILE) for r in (0, 1, TILE, TILE + 1))
    left_high, left_low = split(jnp.concatenate([u_re, u_im], axis=0))
    right_high, right_low = split(
        jnp.concatenate(
            [jnp.concatenate([d_re, d_im], axis=0), jnp.concatenate([d_im, -d_re], axis=0)], axis=1
        )
    )
    left = jnp.concatenate([left_high, left_high, left_low], axis=0).astype(BF16)
    right = jnp.concatenate([right_high, right_low, right_high], axis=0).astype(BF16)
    outer = lax.dot_general(left, right, (((0,), (0,)), ((), ())), preferred_element_type=F32)
    c = LANES // 2
    out_ref[0] = (outer[:c, :c] + outer[c:, c : 2 * c]) * scale
    out_ref[1] = (outer[:c, 2 * c : 3 * c] + outer[c:, 3 * c :]) * scale


def exchange(x, axis):
    return lax.all_to_all(x, axis, 0, 0, tiled=True)


def exchange_pairs(x, axis):
    n = x.shape[0] // 2
    return exchange(x.reshape(n, 2, LANES), axis).reshape(2 * n, LANES)


def exchange_tiles(x, axis):
    n = x.shape[0] // TILE
    return exchange(x.reshape(n, TILE, LANES), axis).reshape(TILE * n, LANES)


def twice_diag(x):
    zero = jnp.zeros_like(x)
    return jnp.concatenate(
        [jnp.concatenate([x, zero], axis=1), jnp.concatenate([zero, x], axis=1)], axis=0
    )


def local(field, cotangent, mode_blocks, spectral, w_in, b_in, w_out, b_out):
    rows, width = field.shape
    chans, hid = w_in.shape
    ncol = width // chans
    grid = lax.axis_size("grid")
    dp = lax.axis_size("dp")
    inv_cols = 1.0 / (ncol * dp)
    count = mode_blocks.shape[0] * BLK

    modal, table = call(
        modal_kernel,
        "modal",
        [((2 * count, width), BF16), ((2 * count, rows), BF16)],
        [HBM, HBM],
        [
            pltpu.SMEM(mode_blocks.shape, jnp.int32),
            pltpu.VMEM((rows, width), BF16),
            pltpu.VMEM((2 * count, width), F32),
            pltpu.SemaphoreType.DMA,
            pltpu.SemaphoreType.DMA,
        ],
    )(
        pltpu.with_memory_space_constraint(mode_blocks, pltpu.HBM),
        pltpu.with_memory_space_constraint(field, pltpu.HBM),
    )
    recv = exchange_pairs(modal, "grid")
    sources = (
        mode_blocks,
        spectral.reshape(2, chans, chans),
        w_in,
        w_out.T,
        b_in.reshape(1, hid),
        b_out.reshape(1, chans),
        cotangent,
        field,
    )
    (
        mix_weights,
        back_weights,
        w_in_two,
        w_in_back,
        b_in_two,
        w_out_two,
        w_out_back,
        b_out_two,
        table_tt,
        cotangent_here,
        cotangent_t,
        field_here,
        zero_row,
        zero_own,
    ) = call(
        prepare_kernel,
        "prepare",
        [
            ((width, 2 * width), BF16),
            ((2 * width, width), BF16),
            ((width, 2 * hid), BF16),
            ((2 * hid, width), BF16),
            ((1, 2 * hid), F32),
            ((2 * hid, width), BF16),
            ((width, 2 * hid), BF16),
            ((1, width), F32),
            ((rows, 4 * count), BF16),
            ((rows, width), BF16),
            ((width, rows), BF16),
            ((rows, width), BF16),
            ((count, width), F32),
            ((TILE, width), F32),
        ],
        [HBM] * len(sources) + [VMEM],
        [pltpu.SMEM(mode_blocks.shape, jnp.int32)]
        + [pltpu.VMEM(a.shape, a.dtype) for a in sources[1:6]]
        + [pltpu.SemaphoreType.DMA((len(sources),))],
    )(*(pltpu.with_memory_space_constraint(a, pltpu.HBM) for a in sources), table)
    mixed, modal_sum = call(
        mix_kernel, "mix", [((2 * grid, width), BF16), ((TILE, width), F32)], [VMEM] * 2
    )(recv, mix_weights)
    piece = exchange_pairs(mixed, "grid")

    output, parts = call(
        functools.partial(cells_kernel, 256),
        "cells",
        [((rows, width), BF16, HBM), ((TILE * grid, width), BF16)],
        [VMEM] * 13,
        [
            pltpu.VMEM((2 * count, width), F32),
            pltpu.VMEM((rows, 2 * hid), BF16),
            pltpu.VMEM((rows, 2 * hid), BF16),
            pltpu.VMEM((rows, width), BF16),
            pltpu.VMEM((TILE * grid, width), F32),
            pltpu.SemaphoreType.DMA((rows // 256,)),
        ],
    )(
        piece,
        table,
        table_tt,
        field_here,
        cotangent_here,
        cotangent_t,
        w_in_two,
        w_in_back,
        b_in_two,
        w_out_two,
        w_out_back,
        b_out_two,
        zero_row,
    )
    share, grad_in = call(
        share_kernel, "share", [((2 * TILE * dp, width), F32), ((TILE, width), F32)], [VMEM] * 4
    )(exchange_tiles(parts, "grid"), modal_sum, back_weights, zero_own)
    shares = exchange(share, "dp")
    (own,) = call(
        functools.partial(total_kernel, inv_cols), "total", [((OWN * grid, width), BF16)], [VMEM] * 3
    )(shares, grad_in, zero_own)
    field_grad, spectral_grad, w_in_grad, w_out_grad, b_in_grad, b_out_grad = call(
        functools.partial(final_kernel, inv_cols),
        "final",
        [
            ((rows, width), BF16),
            ((2, chans, chans), F32),
            ((chans, hid), F32),
            ((chans, hid), F32),
            ((1, hid), F32),
            ((1, chans), F32),
        ],
        [VMEM] * 5,
        [pltpu.VMEM((OWN * grid, width), F32)],
    )(exchange_pairs(own, "grid"), shares, table_tt, cotangent_here, zero_row)
    return (
        output,
        field_grad,
        spectral_grad.reshape(2, 1, chans, chans),
        w_in_grad,
        b_in_grad.reshape(hid),
        w_out_grad.T,
        b_out_grad.reshape(chans),
    )


def solution(mesh):
    in_specs = (
        P("grid", "dp"),
        P("grid", "dp"),
        P(),
        P(None, "grid", None, None),
        P(),
        P(),
        P(),
        P(),
    )
    out_specs = (P("grid", "dp"), P("grid", "dp"), P(None, "grid", None, None), P(), P(), P(), P())
    return jax.shard_map(local, mesh=mesh, in_specs=in_specs, out_specs=out_specs, check_vma=False)
```

```python
import functools
import math

import jax
import jax.numpy as jnp
from jax import lax
from jax.experimental import pallas as pl
from jax.experimental.pallas import tpu as pltpu
from jax.sharding import PartitionSpec as P

NX = 65536
BLK = 8
LANES = 128
TILE = 8
F32 = jnp.float32
BF16 = jnp.bfloat16
VMEM = pl.BlockSpec(memory_space=pltpu.VMEM)
HBM = pl.BlockSpec(memory_space=pltpu.HBM)
OWN = 6


def call(kernel, name, outs, specs, scratch=()):
    return pl.pallas_call(
        kernel,
        name=name,
        out_shape=[jax.ShapeDtypeStruct(o[0], o[1]) for o in outs],
        in_specs=specs,
        out_specs=[o[2] if len(o) > 2 else VMEM for o in outs],
        scratch_shapes=list(scratch),
        compiler_params=pltpu.CompilerParams(vmem_limit_bytes=48 << 20),
    )


def dot(a, b):
    return jnp.dot(a, b, preferred_element_type=F32)


def dot_on(a, b, over_a, over_b):
    return lax.dot_general(a, b, (((over_a,), (over_b,)), ((), ())), preferred_element_type=F32)


def row_id(shape):
    return lax.broadcasted_iota(jnp.int32, shape, 0)


def every(ref, start, count, step):
    return ref[pl.ds(start, count, stride=step), :]


def cos_sin(turn):
    quarter = NX // 4
    quad = (turn + quarter // 2) >> (quarter.bit_length() - 1)
    rest = (turn - quad * quarter).astype(F32) * (2.0 * math.pi / NX)
    sq = rest * rest
    sin = rest * (1.0 + sq * (-1 / 6 + sq * (1 / 120 + sq * (-1 / 5040 + sq * (1 / 362880)))))
    cos = 1.0 + sq * (
        -1 / 2 + sq * (1 / 24 + sq * (-1 / 720 + sq * (1 / 40320 + sq * (-1 / 3628800))))
    )
    odd = (quad & 1) == 1
    c = jnp.where(odd, sin, cos)
    s = jnp.where(odd, cos, sin)
    return jnp.where(((quad + 1) & 2) != 0, -c, c), jnp.where((quad & 2) != 0, -s, s)


def twice_diag(x):
    zero = jnp.zeros_like(x)
    return jnp.concatenate(
        [jnp.concatenate([x, zero], axis=1), jnp.concatenate([zero, x], axis=1)], axis=0
    )


def first_kernel(
    blocks_hbm,
    field_hbm,
    spectral_hbm,
    win_hbm,
    wout_hbm,
    bin_hbm,
    bout_hbm,
    cot_hbm,
    modal_ref,
    table_ref,
    field_ref,
    cot_ref,
    mix_ref,
    back_ref,
    win_two_ref,
    wout_two_ref,
    bin_two_ref,
    bout_two_ref,
    zero_row_ref,
    zero_own_ref,
    blocks_ref,
    s_ref,
    win_ref,
    wout_ref,
    bin_ref,
    bout_ref,
    wide_ref,
    sems,
):
    pairs = (
        (blocks_hbm, blocks_ref),
        (field_hbm, field_ref),
        (spectral_hbm, s_ref),
        (win_hbm, win_ref),
        (wout_hbm, wout_ref),
        (bin_hbm, bin_ref),
        (bout_hbm, bout_ref),
        (cot_hbm, cot_ref),
    )
    copies = [pltpu.make_async_copy(a, b, sems.at[i]) for i, (a, b) in enumerate(pairs)]
    for copy in copies:
        copy.start()
    win_two_ref[...] = jnp.zeros_like(win_two_ref)
    wout_two_ref[...] = jnp.zeros_like(wout_two_ref)
    copies[0].wait()
    kblocks = blocks_ref.shape[0]
    count = kblocks * BLK
    rows = field_ref.shape[0]
    index = lax.axis_index("grid")
    base = jnp.concatenate(
        [jnp.full((BLK, LANES), blocks_ref[b] * BLK, jnp.int32) for b in range(kblocks)], axis=0
    )
    modes = base + row_id((count, LANES)) % BLK
    lane = lax.broadcasted_iota(jnp.int32, (count, LANES), 1)
    scale = 1.0 / math.sqrt(NX)
    near_c, near_s = cos_sin((modes * lane) & (NX - 1))
    near_c, near_s = near_c * scale, near_s * scale
    far_c, far_s = cos_sin((modes * (index * rows + lane * LANES)) & (NX - 1))
    for a in range(rows // LANES):
        ca = jnp.broadcast_to(far_c[:, a : a + 1], (count, LANES))
        sa = jnp.broadcast_to(far_s[:, a : a + 1], (count, LANES))
        span = pl.ds(a * LANES, LANES)
        table_ref[:count, span] = (near_c * ca - near_s * sa).astype(BF16)
        table_ref[count:, span] = (-(near_s * ca + near_c * sa)).astype(BF16)
    copies[1].wait()
    modal = dot(table_ref[...], field_ref[...])
    wide_ref[pl.ds(0, count, stride=2), :] = modal[:count]
    wide_ref[pl.ds(1, count, stride=2), :] = modal[count:]
    modal_ref[...] = wide_ref[...].astype(BF16)
    zero_row_ref[...] = jnp.where(modes == 0, 1.0, 0.0)
    at = jnp.int32(0)
    for b in range(kblocks):
        at = jnp.where(blocks_ref[b] == 0, b * BLK, at)
    own = jnp.full((TILE, LANES), index, jnp.int32)
    zero_own_ref[...] = jnp.where(own == at, 1.0, 0.0)
    for copy in copies[2:]:
        copy.wait()
    s_re, s_im = twice_diag(s_ref[0]), twice_diag(s_ref[1])
    mix_ref[...] = jnp.concatenate([s_re, s_im], axis=1)
    back_ref[...] = jnp.concatenate([s_re, s_im], axis=0)
    chans, hid = win_ref.shape
    for two_ref, one_ref in ((win_two_ref, win_ref), (wout_two_ref, wout_ref)):
        two_ref[:chans, :hid] = one_ref[...]
        two_ref[chans:, hid:] = one_ref[...]
    bin_two_ref[...] = jnp.concatenate([bin_ref[...]] * 2, axis=1)
    bout_two_ref[...] = jnp.concatenate([bout_ref[...]] * 2, axis=1)


def complex_rows(x, weights, axis, sign):
    high = x.astype(BF16).astype(F32)
    rest = x - high
    mid = rest.astype(BF16).astype(F32)
    low = rest - mid
    row = row_id(x.shape)
    left = jnp.where(row < 2, high, jnp.where(row < 4, mid, jnp.where(row < 6, low, 0.0)))
    dims = (((1,), (axis,)), ((), ()))
    y = lax.dot_general(left.astype(BF16), weights, dims, preferred_element_type=F32)
    y = y + pltpu.roll(y, 4, 0)
    y = y + pltpu.roll(y, 2, 0)
    by_re = y[:, :LANES]
    by_im = pltpu.roll(y[:, LANES:], 1, 0)
    return by_re + jnp.where(row % 2 == 0, sign, -sign) * by_im


def mix_kernel(recv_ref, weights_ref, out_ref, sum_ref):
    x = jnp.sum(recv_ref[...].astype(F32).reshape(-1, TILE, LANES), axis=0)
    x = x + pltpu.roll(x, 4, 0)
    x = x + pltpu.roll(x, 2, 0)
    sum_ref[...] = x
    mixed = complex_rows(x, weights_ref[...], 0, -1.0)
    out_ref[...] = jnp.concatenate([mixed] * (out_ref.shape[0] // TILE), axis=0).astype(BF16)


def gelu_pair(pre):
    k = math.sqrt(2.0 / math.pi)
    sq = pre * pre
    t = jnp.tanh(pre * (k + (0.044715 * k) * sq))
    half = 0.5 * pre
    up = 1.0 + t
    return half * up, up * (0.5 + half * (1.0 - t) * (k + (3 * 0.044715 * k) * sq))


def cells_kernel(
    chunk,
    piece_ref,
    table_ref,
    field_ref,
    cot_ref,
    win_ref,
    bin_ref,
    wout_t_ref,
    bout_ref,
    zero_row_ref,
    out_hbm,
    parts_ref,
    wide_ref,
    hidden_ref,
    gpre_ref,
    out_ref,
    sums_ref,
    out_sems,
):
    rows = field_ref.shape[0]
    count = table_ref.shape[0] // 2
    hid = bin_ref.shape[1] // 2
    chans = LANES // 2
    wide_ref[...] = 2.0 * piece_ref[...].astype(F32)
    mixed = jnp.concatenate([every(wide_ref, 0, count, 2), every(wide_ref, 1, count, 2)], axis=0)
    right = stack_parts(dot(mixed.astype(BF16), win_ref[...]))
    copies = []
    for i in range(rows // chunk):
        span = pl.ds(i * chunk, chunk)
        table = table_ref[:, span]
        pre = dot_on(jnp.concatenate([table, table], axis=0), right, 0, 0) + bin_ref[...]
        gate, slope = gelu_pair(pre)
        hidden = gate.astype(BF16)
        hidden_ref[span, :] = hidden
        gpre_ref[span, :] = (dot(cot_ref[span, :], wout_t_ref[...]) * slope).astype(BF16)
        out = dot_on(hidden, wout_t_ref[...], 1, 1) + bout_ref[...]
        out_ref[span, :] = (field_ref[span, :].astype(F32) + out).astype(BF16)
        copies.append(pltpu.make_async_copy(out_ref.at[span], out_hbm.at[span], out_sems.at[i]))
        copies[-1].start()
    ones = jnp.ones((2 * TILE, rows), BF16)
    t = dot(jnp.concatenate([table_ref[...], ones], axis=0), gpre_ref[...])
    by_out = dot_on(cot_ref[...], hidden_ref[...], 0, 0)
    sums_out = dot(ones, cot_ref[...])
    b_in = t[2 * count : 2 * count + 1]
    t_parts = stack_parts(t[: 2 * count])
    grad_modal = dot_on(t_parts, win_ref[...], 1, 1)
    grad_modal = 2.0 * (grad_modal[: 2 * count] + grad_modal[2 * count :])
    mixed_t = mixed.T.astype(BF16)
    by_in = dot(jnp.concatenate([mixed_t, mixed_t], axis=1), t_parts)
    g_in = by_in[:chans, :hid] + by_in[chans:, hid:]
    g_out = by_out[:chans, :hid] + by_out[chans:, hid:]
    b_in = b_in[:, :hid] + b_in[:, hid:]
    b_out = halves((sums_out + pltpu.roll(sums_out, chans, 1))[:1])
    for r, block in enumerate(
        (
            grad_modal[:count],
            jnp.where(zero_row_ref[...] > 0.0, b_out, grad_modal[count:]),
            g_in[:, :LANES],
            g_in[:, LANES:],
            g_out[:, :LANES],
            g_out[:, LANES:],
            jnp.broadcast_to(b_in[:, :LANES], (count, LANES)),
            jnp.broadcast_to(b_in[:, LANES:], (count, LANES)),
        )
    ):
        sums_ref[pl.ds(r, count, stride=TILE), :] = block
    parts_ref[...] = sums_ref[...].astype(BF16)
    for copy in copies:
        copy.wait()


def stack_parts(x):
    high, low = split(x)
    return jnp.concatenate([high, low], axis=0).astype(BF16)


def halves(x):
    high, low = split(x)
    lane = lax.broadcasted_iota(jnp.int32, x.shape, 1)
    return jnp.where(lane < LANES // 2, high, low)


def split(x):
    high = x.astype(BF16).astype(F32)
    return high, x - high


def share_kernel(recv_ref, modal_ref, weights_ref, zero_own_ref, share_ref, grad_in_ref):
    x = jnp.sum(recv_ref[...].astype(F32).reshape(-1, TILE, LANES), axis=0)
    row = row_id(x.shape)
    owner = zero_own_ref[...] > 0.0
    extra = jnp.where(owner & (row == 2), pltpu.roll(x, 1, 0), 0.0)
    x = jnp.where(owner & (row == 1), 0.0, x)
    both = jnp.concatenate([x, jnp.where(row < 2, modal_ref[...], extra)], axis=0)
    share_ref[...] = jnp.concatenate([both] * (share_ref.shape[0] // (2 * TILE)), axis=0)
    grad = jnp.concatenate([x[:2]] * (TILE // 2), axis=0)
    grad_in_ref[...] = complex_rows(grad, weights_ref[...], 1, 1.0)


def total_kernel(scale, shares_ref, grad_in_ref, zero_own_ref, out_ref):
    x = jnp.sum(shares_ref[...].reshape(-1, 2 * TILE, LANES), axis=0) * scale
    bias = x[TILE + 2 : TILE + 3]
    bias = halves(bias + pltpu.roll(bias, LANES // 2, 1))
    row = row_id((TILE, LANES))
    own = jnp.where(row < 2, grad_in_ref[...], x[:TILE])
    own = jnp.where((zero_own_ref[...] > 0.0) & (row == 1), bias, own)
    group = jnp.concatenate([own[:OWN]] * 4, axis=0)
    out_ref[...] = jnp.concatenate([group] * (out_ref.shape[0] // (4 * OWN)), axis=0).astype(BF16)


def final_kernel(
    scale,
    recv_ref,
    shares_ref,
    table_ref,
    cot_ref,
    zero_row_ref,
    fgrad_ref,
    spectral_ref,
    win_ref,
    wout_ref,
    bin_ref,
    bout_ref,
    wide_ref,
):
    count = table_ref.shape[0] // 2
    wide_ref[...] = recv_ref[...].astype(F32)
    rows = [every(wide_ref, r, count, OWN) for r in range(OWN)]
    grad_in = jnp.concatenate(rows[:2], axis=0).astype(BF16)
    back = dot_on(table_ref[...], grad_in, 0, 0)
    fgrad_ref[...] = (cot_ref[...].astype(F32) + back).astype(BF16)
    win_ref[:, :LANES] = rows[2]
    win_ref[:, LANES:] = rows[3]
    wout_ref[:, :LANES] = rows[4]
    wout_ref[:, LANES:] = rows[5]
    n = shares_ref.shape[0] // (2 * TILE)
    for r in range(2):
        b_in = jnp.sum(every(shares_ref, OWN + r, n, 2 * TILE), axis=0, keepdims=True)
        bin_ref[:, r * LANES : (r + 1) * LANES] = b_in * scale
    b_out = jnp.sum(jnp.where(zero_row_ref[...] > 0.0, rows[1], 0.0), axis=0, keepdims=True)
    bout_ref[...] = (b_out + pltpu.roll(b_out, LANES // 2, 1))[:, : bout_ref.shape[1]]
    spectral_sums(scale, shares_ref, spectral_ref)


def spectral_sums(scale, shares_ref, out_ref):
    n = shares_ref.shape[0] // (2 * TILE)
    d_re, d_im, u_re, u_im = (every(shares_ref, r, n, 2 * TILE) for r in (0, 1, TILE, TILE + 1))
    left_high, left_low = split(jnp.concatenate([u_re, u_im], axis=0))
    right_high, right_low = split(
        jnp.concatenate(
            [jnp.concatenate([d_re, d_im], axis=0), jnp.concatenate([d_im, -d_re], axis=0)], axis=1
        )
    )
    left = jnp.concatenate([left_high, left_high, left_low], axis=0).astype(BF16)
    right = jnp.concatenate([right_high, right_low, right_high], axis=0).astype(BF16)
    outer = lax.dot_general(left, right, (((0,), (0,)), ((), ())), preferred_element_type=F32)
    c = LANES // 2
    out_ref[0] = (outer[:c, :c] + outer[c:, c : 2 * c]) * scale
    out_ref[1] = (outer[:c, 2 * c : 3 * c] + outer[c:, 3 * c :]) * scale


def exchange(x, axis):
    return lax.all_to_all(x, axis, 0, 0, tiled=True)


def exchange_pairs(x, axis):
    n = x.shape[0] // 2
    return exchange(x.reshape(n, 2, LANES), axis).reshape(2 * n, LANES)


def exchange_tiles(x, axis):
    n = x.shape[0] // TILE
    return exchange(x.reshape(n, TILE, LANES), axis).reshape(TILE * n, LANES)


def local(field, cotangent, mode_blocks, spectral, w_in, b_in, w_out, b_out):
    rows, width = field.shape
    chans, hid = w_in.shape
    ncol = width // chans
    grid = lax.axis_size("grid")
    dp = lax.axis_size("dp")
    inv_cols = 1.0 / (ncol * dp)
    count = mode_blocks.shape[0] * BLK

    sources = (
        mode_blocks,
        field,
        spectral.reshape(2, chans, chans),
        w_in,
        w_out.T,
        b_in.reshape(1, hid),
        b_out.reshape(1, chans),
        cotangent,
    )
    (
        modal,
        table,
        field_here,
        cotangent_here,
        mix_weights,
        back_weights,
        w_in_two,
        w_out_two,
        b_in_two,
        b_out_two,
        zero_row,
        zero_own,
    ) = call(
        first_kernel,
        "first",
        [
            ((2 * count, width), BF16),
            ((2 * count, rows), BF16),
            ((rows, width), BF16),
            ((rows, width), BF16),
            ((width, 2 * width), BF16),
            ((2 * width, width), BF16),
            ((width, 2 * hid), BF16),
            ((width, 2 * hid), BF16),
            ((1, 2 * hid), F32),
            ((1, width), F32),
            ((count, width), F32),
            ((TILE, width), F32),
        ],
        [HBM] * len(sources),
        [pltpu.SMEM(mode_blocks.shape, jnp.int32)]
        + [pltpu.VMEM(a.shape, a.dtype) for a in sources[2:7]]
        + [pltpu.VMEM((2 * count, width), F32), pltpu.SemaphoreType.DMA((len(sources),))],
    )(*(pltpu.with_memory_space_constraint(a, pltpu.HBM) for a in sources))
    mixed, modal_sum = call(
        mix_kernel, "mix", [((2 * grid, width), BF16), ((TILE, width), F32)], [VMEM] * 2
    )(exchange_pairs(modal, "grid"), mix_weights)
    piece = exchange_pairs(mixed, "grid")

    output, parts = call(
        functools.partial(cells_kernel, 256),
        "cells",
        [((rows, width), BF16, HBM), ((TILE * grid, width), BF16)],
        [VMEM] * 9,
        [
            pltpu.VMEM((2 * count, width), F32),
            pltpu.VMEM((rows, 2 * hid), BF16),
            pltpu.VMEM((rows, 2 * hid), BF16),
            pltpu.VMEM((rows, width), BF16),
            pltpu.VMEM((TILE * grid, width), F32),
            pltpu.SemaphoreType.DMA((rows // 256,)),
        ],
    )(
        piece,
        table,
        field_here,
        cotangent_here,
        w_in_two,
        b_in_two,
        w_out_two,
        b_out_two,
        zero_row,
    )
    share, grad_in = call(
        share_kernel, "share", [((2 * TILE * dp, width), F32), ((TILE, width), F32)], [VMEM] * 4
    )(exchange_tiles(parts, "grid"), modal_sum, back_weights, zero_own)
    shares = exchange(share, "dp")
    (own,) = call(
        functools.partial(total_kernel, inv_cols), "total", [((OWN * grid, width), BF16)], [VMEM] * 3
    )(shares, grad_in, zero_own)
    field_grad, spectral_grad, w_in_grad, w_out_grad, b_in_grad, b_out_grad = call(
        functools.partial(final_kernel, inv_cols),
        "final",
        [
            ((rows, width), BF16),
            ((2, chans, chans), F32),
            ((chans, hid), F32),
            ((chans, hid), F32),
            ((1, hid), F32),
            ((1, chans), F32),
        ],
        [VMEM] * 5,
        [pltpu.VMEM((OWN * grid, width), F32)],
    )(exchange_pairs(own, "grid"), shares, table, cotangent_here, zero_row)
    return (
        output,
        field_grad,
        spectral_grad.reshape(2, 1, chans, chans),
        w_in_grad,
        b_in_grad.reshape(hid),
        w_out_grad.T,
        b_out_grad.reshape(chans),
    )


def solution(mesh):
    in_specs = (
        P("grid", "dp"),
        P("grid", "dp"),
        P(),
        P(None, "grid", None, None),
        P(),
        P(),
        P(),
        P(),
    )
    out_specs = (P("grid", "dp"), P("grid", "dp"), P(None, "grid", None, None), P(), P(), P(), P())
    return jax.shard_map(local, mesh=mesh, in_specs=in_specs, out_specs=out_specs, check_vma=False)
```

```python
import functools
import math

import jax
import jax.numpy as jnp
from jax import lax
from jax.experimental import pallas as pl
from jax.experimental.pallas import tpu as pltpu
from jax.sharding import PartitionSpec as P

NX = 65536
BLK = 8
LANES = 128
TILE = 8
F32 = jnp.float32
BF16 = jnp.bfloat16
VMEM = pl.BlockSpec(memory_space=pltpu.VMEM)
HBM = pl.BlockSpec(memory_space=pltpu.HBM)
OWN = 6


def call(kernel, name, outs, specs, scratch=()):
    return pl.pallas_call(
        kernel,
        name=name,
        out_shape=[jax.ShapeDtypeStruct(o[0], o[1]) for o in outs],
        in_specs=specs,
        out_specs=[o[2] if len(o) > 2 else VMEM for o in outs],
        scratch_shapes=list(scratch),
        compiler_params=pltpu.CompilerParams(vmem_limit_bytes=48 << 20),
    )


def dot(a, b):
    return jnp.dot(a, b, preferred_element_type=F32)


def dot_on(a, b, over_a, over_b):
    return lax.dot_general(a, b, (((over_a,), (over_b,)), ((), ())), preferred_element_type=F32)


def row_id(shape):
    return lax.broadcasted_iota(jnp.int32, shape, 0)


def every(ref, start, count, step):
    return ref[pl.ds(start, count, stride=step), :]


def cos_sin(turn):
    quarter = NX // 4
    quad = (turn + quarter // 2) >> (quarter.bit_length() - 1)
    rest = (turn - quad * quarter).astype(F32) * (2.0 * math.pi / NX)
    sq = rest * rest
    sin = rest * (1.0 + sq * (-1 / 6 + sq * (1 / 120 + sq * (-1 / 5040 + sq * (1 / 362880)))))
    cos = 1.0 + sq * (
        -1 / 2 + sq * (1 / 24 + sq * (-1 / 720 + sq * (1 / 40320 + sq * (-1 / 3628800))))
    )
    odd = (quad & 1) == 1
    c = jnp.where(odd, sin, cos)
    s = jnp.where(odd, cos, sin)
    return jnp.where(((quad + 1) & 2) != 0, -c, c), jnp.where((quad & 2) != 0, -s, s)


def twice_diag(x):
    zero = jnp.zeros_like(x)
    return jnp.concatenate(
        [jnp.concatenate([x, zero], axis=1), jnp.concatenate([zero, x], axis=1)], axis=0
    )


def first_kernel(
    blocks_hbm,
    field_hbm,
    spectral_hbm,
    win_hbm,
    wout_hbm,
    bin_hbm,
    bout_hbm,
    cot_hbm,
    modal_ref,
    table_ref,
    field_ref,
    cot_ref,
    mix_ref,
    back_ref,
    win_two_ref,
    wout_two_ref,
    bin_two_ref,
    bout_two_ref,
    zero_row_ref,
    zero_own_ref,
    blocks_ref,
    s_ref,
    win_ref,
    wout_ref,
    bin_ref,
    bout_ref,
    wide_ref,
    sems,
):
    pairs = (
        (blocks_hbm, blocks_ref),
        (field_hbm, field_ref),
        (spectral_hbm, s_ref),
        (win_hbm, win_ref),
        (wout_hbm, wout_ref),
        (bin_hbm, bin_ref),
        (bout_hbm, bout_ref),
        (cot_hbm, cot_ref),
    )
    copies = [pltpu.make_async_copy(a, b, sems.at[i]) for i, (a, b) in enumerate(pairs)]
    for copy in copies:
        copy.start()
    win_two_ref[...] = jnp.zeros_like(win_two_ref)
    wout_two_ref[...] = jnp.zeros_like(wout_two_ref)
    copies[0].wait()
    kblocks = blocks_ref.shape[0]
    count = kblocks * BLK
    rows = field_ref.shape[0]
    index = lax.axis_index("grid")
    base = jnp.concatenate(
        [jnp.full((BLK, LANES), blocks_ref[b] * BLK, jnp.int32) for b in range(kblocks)], axis=0
    )
    modes = base + row_id((count, LANES)) % BLK
    lane = lax.broadcasted_iota(jnp.int32, (count, LANES), 1)
    scale = 1.0 / math.sqrt(NX)
    near_c, near_s = cos_sin((modes * lane) & (NX - 1))
    near_c, near_s = near_c * scale, near_s * scale
    far_c, far_s = cos_sin((modes * (index * rows + lane * LANES)) & (NX - 1))
    for a in range(rows // LANES):
        ca = jnp.broadcast_to(far_c[:, a : a + 1], (count, LANES))
        sa = jnp.broadcast_to(far_s[:, a : a + 1], (count, LANES))
        span = pl.ds(a * LANES, LANES)
        table_ref[:count, span] = (near_c * ca - near_s * sa).astype(BF16)
        table_ref[count:, span] = (-(near_s * ca + near_c * sa)).astype(BF16)
    copies[1].wait()
    modal = dot(table_ref[...], field_ref[...])
    wide_ref[pl.ds(0, count, stride=2), :] = modal[:count]
    wide_ref[pl.ds(1, count, stride=2), :] = modal[count:]
    modal_ref[...] = wide_ref[...].astype(BF16)
    zero_row_ref[...] = jnp.where(modes == 0, 1.0, 0.0)
    at = jnp.int32(0)
    for b in range(kblocks):
        at = jnp.where(blocks_ref[b] == 0, b * BLK, at)
    own = jnp.full((TILE, LANES), index, jnp.int32)
    zero_own_ref[...] = jnp.where(own == at, 1.0, 0.0)
    for copy in copies[2:]:
        copy.wait()
    s_re, s_im = twice_diag(s_ref[0]), twice_diag(s_ref[1])
    mix_ref[...] = jnp.concatenate([s_re, s_im], axis=1)
    back_ref[...] = jnp.concatenate([s_re, s_im], axis=0)
    chans, hid = win_ref.shape
    for two_ref, one_ref in ((win_two_ref, win_ref), (wout_two_ref, wout_ref)):
        two_ref[:chans, :hid] = one_ref[...]
        two_ref[chans:, hid:] = one_ref[...]
    bin_two_ref[...] = jnp.concatenate([bin_ref[...]] * 2, axis=1)
    bout_two_ref[...] = jnp.concatenate([bout_ref[...]] * 2, axis=1)


def complex_rows(x, weights, axis, sign):
    high = x.astype(BF16).astype(F32)
    rest = x - high
    mid = rest.astype(BF16).astype(F32)
    low = rest - mid
    row = row_id(x.shape)
    left = jnp.where(row < 2, high, jnp.where(row < 4, mid, jnp.where(row < 6, low, 0.0)))
    dims = (((1,), (axis,)), ((), ()))
    y = lax.dot_general(left.astype(BF16), weights, dims, preferred_element_type=F32)
    y = y + pltpu.roll(y, 4, 0)
    y = y + pltpu.roll(y, 2, 0)
    by_re = y[:, :LANES]
    by_im = pltpu.roll(y[:, LANES:], 1, 0)
    return by_re + jnp.where(row % 2 == 0, sign, -sign) * by_im


def mix_kernel(recv_ref, weights_ref, out_ref, sum_ref):
    x = jnp.sum(recv_ref[...].astype(F32).reshape(-1, TILE, LANES), axis=0)
    x = x + pltpu.roll(x, 4, 0)
    x = x + pltpu.roll(x, 2, 0)
    sum_ref[...] = x
    mixed = complex_rows(x, weights_ref[...], 0, -1.0)
    out_ref[...] = jnp.concatenate([mixed] * (out_ref.shape[0] // TILE), axis=0).astype(BF16)


def gelu_pair(pre):
    k = math.sqrt(2.0 / math.pi)
    inner = k + (0.044715 * k) * (pre * pre)
    share = 0.5 * jnp.tanh(pre * inner) + 0.5
    gate = pre * share
    return gate, share + gate * (1.0 - share) * (6.0 * inner - 4.0 * k)


def cells_kernel(
    chunk,
    piece_ref,
    table_ref,
    field_ref,
    cot_ref,
    win_ref,
    bin_ref,
    wout_t_ref,
    bout_ref,
    zero_row_ref,
    out_hbm,
    parts_ref,
    wide_ref,
    hidden_ref,
    gpre_ref,
    out_ref,
    sums_ref,
    out_sems,
):
    rows = field_ref.shape[0]
    count = table_ref.shape[0] // 2
    hid = bin_ref.shape[1] // 2
    chans = LANES // 2
    wide_ref[...] = 2.0 * piece_ref[...].astype(F32)
    mixed = jnp.concatenate([every(wide_ref, 0, count, 2), every(wide_ref, 1, count, 2)], axis=0)
    right = stack_parts(dot(mixed.astype(BF16), win_ref[...]))
    copies = []
    for i in range(rows // chunk):
        span = pl.ds(i * chunk, chunk)
        table = table_ref[:, span]
        pre = dot_on(jnp.concatenate([table, table], axis=0), right, 0, 0) + bin_ref[...]
        gate, slope = gelu_pair(pre)
        hidden = gate.astype(BF16)
        hidden_ref[span, :] = hidden
        gpre_ref[span, :] = (dot(cot_ref[span, :], wout_t_ref[...]) * slope).astype(BF16)
        out = dot_on(hidden, wout_t_ref[...], 1, 1) + bout_ref[...]
        out_ref[span, :] = (field_ref[span, :].astype(F32) + out).astype(BF16)
        copies.append(pltpu.make_async_copy(out_ref.at[span], out_hbm.at[span], out_sems.at[i]))
        copies[-1].start()
    ones = jnp.ones((2 * TILE, rows), BF16)
    t = dot(jnp.concatenate([table_ref[...], ones], axis=0), gpre_ref[...])
    by_out = dot_on(cot_ref[...], hidden_ref[...], 0, 0)
    sums_out = dot(ones, cot_ref[...])
    b_in = t[2 * count : 2 * count + 1]
    t_parts = stack_parts(t[: 2 * count])
    grad_modal = dot_on(t_parts, win_ref[...], 1, 1)
    grad_modal = 2.0 * (grad_modal[: 2 * count] + grad_modal[2 * count :])
    mixed_t = mixed.T.astype(BF16)
    by_in = dot(jnp.concatenate([mixed_t, mixed_t], axis=1), t_parts)
    g_in = by_in[:chans, :hid] + by_in[chans:, hid:]
    g_out = by_out[:chans, :hid] + by_out[chans:, hid:]
    b_in = b_in[:, :hid] + b_in[:, hid:]
    b_out = halves((sums_out + pltpu.roll(sums_out, chans, 1))[:1])
    for r, block in enumerate(
        (
            grad_modal[:count],
            jnp.where(zero_row_ref[...] > 0.0, b_out, grad_modal[count:]),
            g_in[:, :LANES],
            g_in[:, LANES:],
            g_out[:, :LANES],
            g_out[:, LANES:],
            jnp.broadcast_to(b_in[:, :LANES], (count, LANES)),
            jnp.broadcast_to(b_in[:, LANES:], (count, LANES)),
        )
    ):
        sums_ref[pl.ds(r, count, stride=TILE), :] = block
    parts_ref[...] = sums_ref[...].astype(BF16)
    for copy in copies:
        copy.wait()


def stack_parts(x):
    high, low = split(x)
    return jnp.concatenate([high, low], axis=0).astype(BF16)


def halves(x):
    high, low = split(x)
    lane = lax.broadcasted_iota(jnp.int32, x.shape, 1)
    return jnp.where(lane < LANES // 2, high, low)


def split(x):
    high = x.astype(BF16).astype(F32)
    return high, x - high


def share_kernel(recv_ref, modal_ref, weights_ref, zero_own_ref, share_ref, grad_in_ref):
    x = jnp.sum(recv_ref[...].astype(F32).reshape(-1, TILE, LANES), axis=0)
    row = row_id(x.shape)
    owner = zero_own_ref[...] > 0.0
    extra = jnp.where(owner & (row == 2), pltpu.roll(x, 1, 0), 0.0)
    x = jnp.where(owner & (row == 1), 0.0, x)
    both = jnp.concatenate([x, jnp.where(row < 2, modal_ref[...], extra)], axis=0)
    share_ref[...] = jnp.concatenate([both] * (share_ref.shape[0] // (2 * TILE)), axis=0)
    grad = jnp.concatenate([x[:2]] * (TILE // 2), axis=0)
    grad_in_ref[...] = complex_rows(grad, weights_ref[...], 1, 1.0)


def total_kernel(scale, shares_ref, grad_in_ref, zero_own_ref, out_ref):
    x = jnp.sum(shares_ref[...].reshape(-1, 2 * TILE, LANES), axis=0) * scale
    bias = x[TILE + 2 : TILE + 3]
    bias = halves(bias + pltpu.roll(bias, LANES // 2, 1))
    row = row_id((TILE, LANES))
    own = jnp.where(row < 2, grad_in_ref[...], x[:TILE])
    own = jnp.where((zero_own_ref[...] > 0.0) & (row == 1), bias, own)
    group = jnp.concatenate([own[:OWN]] * 4, axis=0)
    out_ref[...] = jnp.concatenate([group] * (out_ref.shape[0] // (4 * OWN)), axis=0).astype(BF16)


def final_kernel(
    scale,
    recv_ref,
    shares_ref,
    table_ref,
    cot_ref,
    zero_row_ref,
    fgrad_ref,
    spectral_ref,
    win_ref,
    wout_ref,
    bin_ref,
    bout_ref,
    wide_ref,
):
    count = table_ref.shape[0] // 2
    wide_ref[...] = recv_ref[...].astype(F32)
    rows = [every(wide_ref, r, count, OWN) for r in range(OWN)]
    grad_in = jnp.concatenate(rows[:2], axis=0).astype(BF16)
    back = dot_on(table_ref[...], grad_in, 0, 0)
    fgrad_ref[...] = (cot_ref[...].astype(F32) + back).astype(BF16)
    win_ref[:, :LANES] = rows[2]
    win_ref[:, LANES:] = rows[3]
    wout_ref[:, :LANES] = rows[4]
    wout_ref[:, LANES:] = rows[5]
    n = shares_ref.shape[0] // (2 * TILE)
    for r in range(2):
        b_in = jnp.sum(every(shares_ref, OWN + r, n, 2 * TILE), axis=0, keepdims=True)
        bin_ref[:, r * LANES : (r + 1) * LANES] = b_in * scale
    b_out = jnp.sum(jnp.where(zero_row_ref[...] > 0.0, rows[1], 0.0), axis=0, keepdims=True)
    bout_ref[...] = (b_out + pltpu.roll(b_out, LANES // 2, 1))[:, : bout_ref.shape[1]]
    spectral_sums(scale, shares_ref, spectral_ref)


def spectral_sums(scale, shares_ref, out_ref):
    n = shares_ref.shape[0] // (2 * TILE)
    d_re, d_im, u_re, u_im = (every(shares_ref, r, n, 2 * TILE) for r in (0, 1, TILE, TILE + 1))
    left_high, left_low = split(jnp.concatenate([u_re, u_im], axis=0))
    right_high, right_low = split(
        jnp.concatenate(
            [jnp.concatenate([d_re, d_im], axis=0), jnp.concatenate([d_im, -d_re], axis=0)], axis=1
        )
    )
    left = jnp.concatenate([left_high, left_high, left_low], axis=0).astype(BF16)
    right = jnp.concatenate([right_high, right_low, right_high], axis=0).astype(BF16)
    outer = lax.dot_general(left, right, (((0,), (0,)), ((), ())), preferred_element_type=F32)
    c = LANES // 2
    out_ref[0] = (outer[:c, :c] + outer[c:, c : 2 * c]) * scale
    out_ref[1] = (outer[:c, 2 * c : 3 * c] + outer[c:, 3 * c :]) * scale


def exchange(x, axis):
    return lax.all_to_all(x, axis, 0, 0, tiled=True)


def exchange_pairs(x, axis):
    n = x.shape[0] // 2
    return exchange(x.reshape(n, 2, LANES), axis).reshape(2 * n, LANES)


def exchange_tiles(x, axis):
    n = x.shape[0] // TILE
    return exchange(x.reshape(n, TILE, LANES), axis).reshape(TILE * n, LANES)


def local(field, cotangent, mode_blocks, spectral, w_in, b_in, w_out, b_out):
    rows, width = field.shape
    chans, hid = w_in.shape
    ncol = width // chans
    grid = lax.axis_size("grid")
    dp = lax.axis_size("dp")
    inv_cols = 1.0 / (ncol * dp)
    count = mode_blocks.shape[0] * BLK

    sources = (
        mode_blocks,
        field,
        spectral.reshape(2, chans, chans),
        w_in,
        w_out.T,
        b_in.reshape(1, hid),
        b_out.reshape(1, chans),
        cotangent,
    )
    (
        modal,
        table,
        field_here,
        cotangent_here,
        mix_weights,
        back_weights,
        w_in_two,
        w_out_two,
        b_in_two,
        b_out_two,
        zero_row,
        zero_own,
    ) = call(
        first_kernel,
        "first",
        [
            ((2 * count, width), BF16),
            ((2 * count, rows), BF16),
            ((rows, width), BF16),
            ((rows, width), BF16),
            ((width, 2 * width), BF16),
            ((2 * width, width), BF16),
            ((width, 2 * hid), BF16),
            ((width, 2 * hid), BF16),
            ((1, 2 * hid), F32),
            ((1, width), F32),
            ((count, width), F32),
            ((TILE, width), F32),
        ],
        [HBM] * len(sources),
        [pltpu.SMEM(mode_blocks.shape, jnp.int32)]
        + [pltpu.VMEM(a.shape, a.dtype) for a in sources[2:7]]
        + [pltpu.VMEM((2 * count, width), F32), pltpu.SemaphoreType.DMA((len(sources),))],
    )(*(pltpu.with_memory_space_constraint(a, pltpu.HBM) for a in sources))
    mixed, modal_sum = call(
        mix_kernel, "mix", [((2 * grid, width), BF16), ((TILE, width), F32)], [VMEM] * 2
    )(exchange_pairs(modal, "grid"), mix_weights)
    piece = exchange_pairs(mixed, "grid")

    output, parts = call(
        functools.partial(cells_kernel, 256),
        "cells",
        [((rows, width), BF16, HBM), ((TILE * grid, width), BF16)],
        [VMEM] * 9,
        [
            pltpu.VMEM((2 * count, width), F32),
            pltpu.VMEM((rows, 2 * hid), BF16),
            pltpu.VMEM((rows, 2 * hid), BF16),
            pltpu.VMEM((rows, width), BF16),
            pltpu.VMEM((TILE * grid, width), F32),
            pltpu.SemaphoreType.DMA((rows // 256,)),
        ],
    )(
        piece,
        table,
        field_here,
        cotangent_here,
        w_in_two,
        b_in_two,
        w_out_two,
        b_out_two,
        zero_row,
    )
    share, grad_in = call(
        share_kernel, "share", [((2 * TILE * dp, width), F32), ((TILE, width), F32)], [VMEM] * 4
    )(exchange_tiles(parts, "grid"), modal_sum, back_weights, zero_own)
    shares = exchange(share, "dp")
    (own,) = call(
        functools.partial(total_kernel, inv_cols), "total", [((OWN * grid, width), BF16)], [VMEM] * 3
    )(shares, grad_in, zero_own)
    field_grad, spectral_grad, w_in_grad, w_out_grad, b_in_grad, b_out_grad = call(
        functools.partial(final_kernel, inv_cols),
        "final",
        [
            ((rows, width), BF16),
            ((2, chans, chans), F32),
            ((chans, hid), F32),
            ((chans, hid), F32),
            ((1, hid), F32),
            ((1, chans), F32),
        ],
        [VMEM] * 5,
        [pltpu.VMEM((OWN * grid, width), F32)],
    )(exchange_pairs(own, "grid"), shares, table, cotangent_here, zero_row)
    return (
        output,
        field_grad,
        spectral_grad.reshape(2, 1, chans, chans),
        w_in_grad,
        b_in_grad.reshape(hid),
        w_out_grad.T,
        b_out_grad.reshape(chans),
    )


def solution(mesh):
    in_specs = (
        P("grid", "dp"),
        P("grid", "dp"),
        P(),
        P(None, "grid", None, None),
        P(),
        P(),
        P(),
        P(),
    )
    out_specs = (P("grid", "dp"), P("grid", "dp"), P(None, "grid", None, None), P(), P(), P(), P())
    return jax.shard_map(local, mesh=mesh, in_specs=in_specs, out_specs=out_specs, check_vma=False)
```

```python
import functools
import math

import jax
import jax.numpy as jnp
from jax import lax
from jax.experimental import pallas as pl
from jax.experimental.pallas import tpu as pltpu
from jax.sharding import PartitionSpec as P

NX = 65536
BLK = 8
LANES = 128
TILE = 8
F32 = jnp.float32
BF16 = jnp.bfloat16
VMEM = pl.BlockSpec(memory_space=pltpu.VMEM)
HBM = pl.BlockSpec(memory_space=pltpu.HBM)
OWN = 6


def call(kernel, name, outs, specs, scratch=()):
    return pl.pallas_call(
        kernel,
        name=name,
        out_shape=[jax.ShapeDtypeStruct(o[0], o[1]) for o in outs],
        in_specs=specs,
        out_specs=[o[2] if len(o) > 2 else VMEM for o in outs],
        scratch_shapes=list(scratch),
        compiler_params=pltpu.CompilerParams(vmem_limit_bytes=48 << 20),
    )


def dot(a, b):
    return jnp.dot(a, b, preferred_element_type=F32)


def dot_on(a, b, over_a, over_b):
    return lax.dot_general(a, b, (((over_a,), (over_b,)), ((), ())), preferred_element_type=F32)


def row_id(shape):
    return lax.broadcasted_iota(jnp.int32, shape, 0)


def every(ref, start, count, step):
    return ref[pl.ds(start, count, stride=step), :]


def cos_sin(turn):
    quarter = NX // 4
    quad = (turn + quarter // 2) >> (quarter.bit_length() - 1)
    rest = (turn - quad * quarter).astype(F32) * (2.0 * math.pi / NX)
    sq = rest * rest
    sin = rest * (1.0 + sq * (-1 / 6 + sq * (1 / 120 + sq * (-1 / 5040 + sq * (1 / 362880)))))
    cos = 1.0 + sq * (
        -1 / 2 + sq * (1 / 24 + sq * (-1 / 720 + sq * (1 / 40320 + sq * (-1 / 3628800))))
    )
    odd = (quad & 1) == 1
    c = jnp.where(odd, sin, cos)
    s = jnp.where(odd, cos, sin)
    return jnp.where(((quad + 1) & 2) != 0, -c, c), jnp.where((quad & 2) != 0, -s, s)


def twice_diag(x):
    zero = jnp.zeros_like(x)
    return jnp.concatenate(
        [jnp.concatenate([x, zero], axis=1), jnp.concatenate([zero, x], axis=1)], axis=0
    )


def first_kernel(
    blocks_hbm,
    field_hbm,
    spectral_hbm,
    win_hbm,
    wout_hbm,
    bin_hbm,
    bout_hbm,
    cot_hbm,
    modal_ref,
    table_ref,
    field_ref,
    cot_ref,
    mix_ref,
    back_ref,
    win_two_ref,
    wout_two_ref,
    bin_two_ref,
    bout_two_ref,
    zero_row_ref,
    zero_own_ref,
    blocks_ref,
    s_ref,
    win_ref,
    wout_ref,
    bin_ref,
    bout_ref,
    wide_ref,
    sems,
):
    pairs = (
        (blocks_hbm, blocks_ref),
        (field_hbm, field_ref),
        (spectral_hbm, s_ref),
        (win_hbm, win_ref),
        (wout_hbm, wout_ref),
        (bin_hbm, bin_ref),
        (bout_hbm, bout_ref),
        (cot_hbm, cot_ref),
    )
    copies = [pltpu.make_async_copy(a, b, sems.at[i]) for i, (a, b) in enumerate(pairs)]
    for copy in copies:
        copy.start()
    win_two_ref[...] = jnp.zeros_like(win_two_ref)
    wout_two_ref[...] = jnp.zeros_like(wout_two_ref)
    copies[0].wait()
    kblocks = blocks_ref.shape[0]
    count = kblocks * BLK
    rows = field_ref.shape[0]
    index = lax.axis_index("grid")
    base = jnp.concatenate(
        [jnp.full((BLK, LANES), blocks_ref[b] * BLK, jnp.int32) for b in range(kblocks)], axis=0
    )
    modes = base + row_id((count, LANES)) % BLK
    lane = lax.broadcasted_iota(jnp.int32, (count, LANES), 1)
    scale = 1.0 / math.sqrt(NX)
    near_c, near_s = cos_sin((modes * lane) & (NX - 1))
    near_c, near_s = near_c * scale, near_s * scale
    far_c, far_s = cos_sin((modes * (index * rows + lane * LANES)) & (NX - 1))
    for a in range(rows // LANES):
        ca = jnp.broadcast_to(far_c[:, a : a + 1], (count, LANES))
        sa = jnp.broadcast_to(far_s[:, a : a + 1], (count, LANES))
        span = pl.ds(a * LANES, LANES)
        table_ref[:count, span] = (near_c * ca - near_s * sa).astype(BF16)
        table_ref[count:, span] = (-(near_s * ca + near_c * sa)).astype(BF16)
    copies[1].wait()
    modal = dot(table_ref[...], field_ref[...])
    wide_ref[pl.ds(0, count, stride=2), :] = modal[:count]
    wide_ref[pl.ds(1, count, stride=2), :] = modal[count:]
    modal_ref[...] = wide_ref[...]
    zero_row_ref[...] = jnp.where(modes == 0, 1.0, 0.0)
    at = jnp.int32(0)
    for b in range(kblocks):
        at = jnp.where(blocks_ref[b] == 0, b * BLK, at)
    own = jnp.full((TILE, LANES), index, jnp.int32)
    zero_own_ref[...] = jnp.where(own == at, 1.0, 0.0)
    for copy in copies[2:]:
        copy.wait()
    s_re, s_im = twice_diag(s_ref[0]), twice_diag(s_ref[1])
    mix_ref[...] = jnp.concatenate([s_re, s_im], axis=1)
    back_ref[...] = jnp.concatenate([s_re, s_im], axis=0)
    chans, hid = win_ref.shape
    for two_ref, one_ref in ((win_two_ref, win_ref), (wout_two_ref, wout_ref)):
        two_ref[:chans, :hid] = one_ref[...]
        two_ref[chans:, hid:] = one_ref[...]
    bin_two_ref[...] = jnp.concatenate([bin_ref[...]] * 2, axis=1)
    bout_two_ref[...] = jnp.concatenate([bout_ref[...]] * 2, axis=1)


def complex_rows(x, weights, axis, sign):
    high = x.astype(BF16).astype(F32)
    rest = x - high
    mid = rest.astype(BF16).astype(F32)
    low = rest - mid
    row = row_id(x.shape)
    left = jnp.where(row < 2, high, jnp.where(row < 4, mid, jnp.where(row < 6, low, 0.0)))
    dims = (((1,), (axis,)), ((), ()))
    y = lax.dot_general(left.astype(BF16), weights, dims, preferred_element_type=F32)
    y = y + pltpu.roll(y, 4, 0)
    y = y + pltpu.roll(y, 2, 0)
    by_re = y[:, :LANES]
    by_im = pltpu.roll(y[:, LANES:], 1, 0)
    return by_re + jnp.where(row % 2 == 0, sign, -sign) * by_im


def mix_kernel(recv_ref, weights_ref, out_ref, sum_ref):
    x = jnp.sum(recv_ref[...].astype(F32).reshape(-1, TILE, LANES), axis=0)
    x = x + pltpu.roll(x, 4, 0)
    x = x + pltpu.roll(x, 2, 0)
    sum_ref[...] = x
    mixed = complex_rows(x, weights_ref[...], 0, -1.0)
    out_ref[...] = jnp.concatenate([mixed] * (out_ref.shape[0] // TILE), axis=0).astype(BF16)


def gelu_pair(pre):
    k = math.sqrt(2.0 / math.pi)
    inner = k + (0.044715 * k) * (pre * pre)
    share = 0.5 * jnp.tanh(pre * inner) + 0.5
    gate = pre * share
    return gate, share + gate * (1.0 - share) * (6.0 * inner - 4.0 * k)


def cells_kernel(
    chunk,
    piece_ref,
    table_ref,
    field_ref,
    cot_ref,
    win_ref,
    bin_ref,
    wout_t_ref,
    bout_ref,
    zero_row_ref,
    out_hbm,
    parts_ref,
    wide_ref,
    hidden_ref,
    gpre_ref,
    out_ref,
    sums_ref,
    out_sems,
):
    rows = field_ref.shape[0]
    count = table_ref.shape[0] // 2
    hid = bin_ref.shape[1] // 2
    chans = LANES // 2
    wide_ref[...] = 2.0 * piece_ref[...].astype(F32)
    mixed = jnp.concatenate([every(wide_ref, 0, count, 2), every(wide_ref, 1, count, 2)], axis=0)
    right = stack_parts(dot(mixed.astype(BF16), win_ref[...]))
    copies = []
    for i in range(rows // chunk):
        span = pl.ds(i * chunk, chunk)
        table = table_ref[:, span]
        pre = dot_on(jnp.concatenate([table, table], axis=0), right, 0, 0) + bin_ref[...]
        gate, slope = gelu_pair(pre)
        hidden = gate.astype(BF16)
        hidden_ref[span, :] = hidden
        gpre_ref[span, :] = (dot(cot_ref[span, :], wout_t_ref[...]) * slope).astype(BF16)
        out = dot_on(hidden, wout_t_ref[...], 1, 1) + bout_ref[...]
        out_ref[span, :] = (field_ref[span, :].astype(F32) + out).astype(BF16)
        copies.append(pltpu.make_async_copy(out_ref.at[span], out_hbm.at[span], out_sems.at[i]))
        copies[-1].start()
    ones = jnp.ones((2 * TILE, rows), BF16)
    t = dot(jnp.concatenate([table_ref[...], ones], axis=0), gpre_ref[...])
    by_out = dot_on(cot_ref[...], hidden_ref[...], 0, 0)
    sums_out = dot(ones, cot_ref[...])
    b_in = t[2 * count : 2 * count + 1]
    t_parts = stack_parts(t[: 2 * count])
    grad_modal = dot_on(t_parts, win_ref[...], 1, 1)
    grad_modal = 2.0 * (grad_modal[: 2 * count] + grad_modal[2 * count :])
    mixed_t = mixed.T.astype(BF16)
    by_in = dot(jnp.concatenate([mixed_t, mixed_t], axis=1), t_parts)
    g_in = by_in[:chans, :hid] + by_in[chans:, hid:]
    g_out = by_out[:chans, :hid] + by_out[chans:, hid:]
    b_in = b_in[:, :hid] + b_in[:, hid:]
    b_out = halves((sums_out + pltpu.roll(sums_out, chans, 1))[:1])
    for r, block in enumerate(
        (
            grad_modal[:count],
            jnp.where(zero_row_ref[...] > 0.0, b_out, grad_modal[count:]),
            g_in[:, :LANES],
            g_in[:, LANES:],
            g_out[:, :LANES],
            g_out[:, LANES:],
            jnp.broadcast_to(b_in[:, :LANES], (count, LANES)),
            jnp.broadcast_to(b_in[:, LANES:], (count, LANES)),
        )
    ):
        sums_ref[pl.ds(r, count, stride=TILE), :] = block
    parts_ref[...] = sums_ref[...]
    for copy in copies:
        copy.wait()


def stack_parts(x):
    high, low = split(x)
    return jnp.concatenate([high, low], axis=0).astype(BF16)


def halves(x):
    high, low = split(x)
    lane = lax.broadcasted_iota(jnp.int32, x.shape, 1)
    return jnp.where(lane < LANES // 2, high, low)


def split(x):
    high = x.astype(BF16).astype(F32)
    return high, x - high


def share_kernel(recv_ref, modal_ref, weights_ref, zero_own_ref, share_ref, grad_in_ref):
    x = jnp.sum(recv_ref[...].astype(F32).reshape(-1, TILE, LANES), axis=0)
    row = row_id(x.shape)
    owner = zero_own_ref[...] > 0.0
    extra = jnp.where(owner & (row == 2), pltpu.roll(x, 1, 0), 0.0)
    x = jnp.where(owner & (row == 1), 0.0, x)
    both = jnp.concatenate([x, jnp.where(row < 2, modal_ref[...], extra)], axis=0)
    share_ref[...] = jnp.concatenate([both] * (share_ref.shape[0] // (2 * TILE)), axis=0)
    grad = jnp.concatenate([x[:2]] * (TILE // 2), axis=0)
    grad_in_ref[...] = complex_rows(grad, weights_ref[...], 1, 1.0)


def total_kernel(scale, shares_ref, grad_in_ref, zero_own_ref, out_ref):
    x = jnp.sum(shares_ref[...].reshape(-1, 2 * TILE, LANES), axis=0) * scale
    bias = x[TILE + 2 : TILE + 3]
    bias = halves(bias + pltpu.roll(bias, LANES // 2, 1))
    row = row_id((TILE, LANES))
    own = jnp.where(row < 2, grad_in_ref[...], x[:TILE])
    own = jnp.where((zero_own_ref[...] > 0.0) & (row == 1), bias, own)
    group = jnp.concatenate([own[:OWN]] * 4, axis=0)
    out_ref[...] = jnp.concatenate([group] * (out_ref.shape[0] // (4 * OWN)), axis=0).astype(BF16)


def final_kernel(
    scale,
    recv_ref,
    shares_ref,
    table_ref,
    cot_ref,
    zero_row_ref,
    fgrad_ref,
    spectral_ref,
    win_ref,
    wout_ref,
    bin_ref,
    bout_ref,
    wide_ref,
):
    count = table_ref.shape[0] // 2
    wide_ref[...] = recv_ref[...].astype(F32)
    rows = [every(wide_ref, r, count, OWN) for r in range(OWN)]
    grad_in = jnp.concatenate(rows[:2], axis=0).astype(BF16)
    back = dot_on(table_ref[...], grad_in, 0, 0)
    fgrad_ref[...] = (cot_ref[...].astype(F32) + back).astype(BF16)
    win_ref[:, :LANES] = rows[2]
    win_ref[:, LANES:] = rows[3]
    wout_ref[:, :LANES] = rows[4]
    wout_ref[:, LANES:] = rows[5]
    n = shares_ref.shape[0] // (2 * TILE)
    for r in range(2):
        b_in = jnp.sum(every(shares_ref, OWN + r, n, 2 * TILE), axis=0, keepdims=True)
        bin_ref[:, r * LANES : (r + 1) * LANES] = b_in * scale
    b_out = jnp.sum(jnp.where(zero_row_ref[...] > 0.0, rows[1], 0.0), axis=0, keepdims=True)
    bout_ref[...] = (b_out + pltpu.roll(b_out, LANES // 2, 1))[:, : bout_ref.shape[1]]
    spectral_sums(scale, shares_ref, spectral_ref)


def spectral_sums(scale, shares_ref, out_ref):
    n = shares_ref.shape[0] // (2 * TILE)
    d_re, d_im, u_re, u_im = (every(shares_ref, r, n, 2 * TILE) for r in (0, 1, TILE, TILE + 1))
    left_high, left_low = split(jnp.concatenate([u_re, u_im], axis=0))
    right_high, right_low = split(
        jnp.concatenate(
            [jnp.concatenate([d_re, d_im], axis=0), jnp.concatenate([d_im, -d_re], axis=0)], axis=1
        )
    )
    left = jnp.concatenate([left_high, left_high, left_low], axis=0).astype(BF16)
    right = jnp.concatenate([right_high, right_low, right_high], axis=0).astype(BF16)
    outer = lax.dot_general(left, right, (((0,), (0,)), ((), ())), preferred_element_type=F32)
    c = LANES // 2
    out_ref[0] = (outer[:c, :c] + outer[c:, c : 2 * c]) * scale
    out_ref[1] = (outer[:c, 2 * c : 3 * c] + outer[c:, 3 * c :]) * scale


def exchange(x, axis):
    return lax.all_to_all(x, axis, 0, 0, tiled=True)


def exchange_pairs(x, axis):
    n = x.shape[0] // 2
    return exchange(x.reshape(n, 2, LANES), axis).reshape(2 * n, LANES)


def exchange_tiles(x, axis):
    n = x.shape[0] // TILE
    return exchange(x.reshape(n, TILE, LANES), axis).reshape(TILE * n, LANES)


def local(field, cotangent, mode_blocks, spectral, w_in, b_in, w_out, b_out):
    rows, width = field.shape
    chans, hid = w_in.shape
    ncol = width // chans
    grid = lax.axis_size("grid")
    dp = lax.axis_size("dp")
    inv_cols = 1.0 / (ncol * dp)
    count = mode_blocks.shape[0] * BLK

    sources = (
        mode_blocks,
        field,
        spectral.reshape(2, chans, chans),
        w_in,
        w_out.T,
        b_in.reshape(1, hid),
        b_out.reshape(1, chans),
        cotangent,
    )
    (
        modal,
        table,
        field_here,
        cotangent_here,
        mix_weights,
        back_weights,
        w_in_two,
        w_out_two,
        b_in_two,
        b_out_two,
        zero_row,
        zero_own,
    ) = call(
        first_kernel,
        "first",
        [
            ((2 * count, width), F32),
            ((2 * count, rows), BF16),
            ((rows, width), BF16),
            ((rows, width), BF16),
            ((width, 2 * width), BF16),
            ((2 * width, width), BF16),
            ((width, 2 * hid), BF16),
            ((width, 2 * hid), BF16),
            ((1, 2 * hid), F32),
            ((1, width), F32),
            ((count, width), F32),
            ((TILE, width), F32),
        ],
        [HBM] * len(sources),
        [pltpu.SMEM(mode_blocks.shape, jnp.int32)]
        + [pltpu.VMEM(a.shape, a.dtype) for a in sources[2:7]]
        + [pltpu.VMEM((2 * count, width), F32), pltpu.SemaphoreType.DMA((len(sources),))],
    )(*(pltpu.with_memory_space_constraint(a, pltpu.HBM) for a in sources))
    mixed, modal_sum = call(
        mix_kernel, "mix", [((2 * grid, width), BF16), ((TILE, width), F32)], [VMEM] * 2
    )(exchange_pairs(modal, "grid"), mix_weights)
    piece = exchange_pairs(mixed, "grid")

    output, parts = call(
        functools.partial(cells_kernel, 256),
        "cells",
        [((rows, width), BF16, HBM), ((TILE * grid, width), F32)],
        [VMEM] * 9,
        [
            pltpu.VMEM((2 * count, width), F32),
            pltpu.VMEM((rows, 2 * hid), BF16),
            pltpu.VMEM((rows, 2 * hid), BF16),
            pltpu.VMEM((rows, width), BF16),
            pltpu.VMEM((TILE * grid, width), F32),
            pltpu.SemaphoreType.DMA((rows // 256,)),
        ],
    )(
        piece,
        table,
        field_here,
        cotangent_here,
        w_in_two,
        b_in_two,
        w_out_two,
        b_out_two,
        zero_row,
    )
    share, grad_in = call(
        share_kernel, "share", [((2 * TILE * dp, width), F32), ((TILE, width), F32)], [VMEM] * 4
    )(exchange_tiles(parts, "grid"), modal_sum, back_weights, zero_own)
    shares = exchange(share, "dp")
    (own,) = call(
        functools.partial(total_kernel, inv_cols), "total", [((OWN * grid, width), BF16)], [VMEM] * 3
    )(shares, grad_in, zero_own)
    field_grad, spectral_grad, w_in_grad, w_out_grad, b_in_grad, b_out_grad = call(
        functools.partial(final_kernel, inv_cols),
        "final",
        [
            ((rows, width), BF16),
            ((2, chans, chans), F32),
            ((chans, hid), F32),
            ((chans, hid), F32),
            ((1, hid), F32),
            ((1, chans), F32),
        ],
        [VMEM] * 5,
        [pltpu.VMEM((OWN * grid, width), F32)],
    )(exchange_pairs(own, "grid"), shares, table, cotangent_here, zero_row)
    return (
        output,
        field_grad,
        spectral_grad.reshape(2, 1, chans, chans),
        w_in_grad,
        b_in_grad.reshape(hid),
        w_out_grad.T,
        b_out_grad.reshape(chans),
    )


def solution(mesh):
    in_specs = (
        P("grid", "dp"),
        P("grid", "dp"),
        P(),
        P(None, "grid", None, None),
        P(),
        P(),
        P(),
        P(),
    )
    out_specs = (P("grid", "dp"), P("grid", "dp"), P(None, "grid", None, None), P(), P(), P(), P())
    return jax.shard_map(local, mesh=mesh, in_specs=in_specs, out_specs=out_specs, check_vma=False)
```

```python
import functools
import math

import jax
import jax.numpy as jnp
from jax import lax
from jax.experimental import pallas as pl
from jax.experimental.pallas import tpu as pltpu
from jax.sharding import PartitionSpec as P

NX = 65536
BLK = 8
LANES = 128
TILE = 8
F32 = jnp.float32
BF16 = jnp.bfloat16
VMEM = pl.BlockSpec(memory_space=pltpu.VMEM)
HBM = pl.BlockSpec(memory_space=pltpu.HBM)
OWN = 6


def call(kernel, name, outs, specs, scratch=()):
    return pl.pallas_call(
        kernel,
        name=name,
        out_shape=[jax.ShapeDtypeStruct(o[0], o[1]) for o in outs],
        in_specs=specs,
        out_specs=[o[2] if len(o) > 2 else VMEM for o in outs],
        scratch_shapes=list(scratch),
        compiler_params=pltpu.CompilerParams(vmem_limit_bytes=48 << 20),
    )


def dot(a, b):
    return jnp.dot(a, b, preferred_element_type=F32)


def dot_on(a, b, over_a, over_b):
    return lax.dot_general(a, b, (((over_a,), (over_b,)), ((), ())), preferred_element_type=F32)


def row_id(shape):
    return lax.broadcasted_iota(jnp.int32, shape, 0)


def every(ref, start, count, step):
    return ref[pl.ds(start, count, stride=step), :]


def cos_sin(turn):
    quarter = NX // 4
    quad = (turn + quarter // 2) >> (quarter.bit_length() - 1)
    rest = (turn - quad * quarter).astype(F32) * (2.0 * math.pi / NX)
    sq = rest * rest
    sin = rest * (1.0 + sq * (-1 / 6 + sq * (1 / 120 + sq * (-1 / 5040 + sq * (1 / 362880)))))
    cos = 1.0 + sq * (
        -1 / 2 + sq * (1 / 24 + sq * (-1 / 720 + sq * (1 / 40320 + sq * (-1 / 3628800))))
    )
    odd = (quad & 1) == 1
    c = jnp.where(odd, sin, cos)
    s = jnp.where(odd, cos, sin)
    return jnp.where(((quad + 1) & 2) != 0, -c, c), jnp.where((quad & 2) != 0, -s, s)


def twice_diag(x):
    zero = jnp.zeros_like(x)
    return jnp.concatenate(
        [jnp.concatenate([x, zero], axis=1), jnp.concatenate([zero, x], axis=1)], axis=0
    )


def first_kernel(
    blocks_hbm,
    field_hbm,
    spectral_hbm,
    win_hbm,
    wout_hbm,
    bin_hbm,
    bout_hbm,
    cot_hbm,
    modal_ref,
    table_ref,
    field_ref,
    cot_ref,
    mix_ref,
    back_ref,
    win_two_ref,
    wout_two_ref,
    bin_two_ref,
    bout_two_ref,
    zero_row_ref,
    zero_own_ref,
    blocks_ref,
    s_ref,
    win_ref,
    wout_ref,
    bin_ref,
    bout_ref,
    wide_ref,
    sems,
):
    pairs = (
        (blocks_hbm, blocks_ref),
        (field_hbm, field_ref),
        (spectral_hbm, s_ref),
        (win_hbm, win_ref),
        (wout_hbm, wout_ref),
        (bin_hbm, bin_ref),
        (bout_hbm, bout_ref),
        (cot_hbm, cot_ref),
    )
    copies = [pltpu.make_async_copy(a, b, sems.at[i]) for i, (a, b) in enumerate(pairs)]
    for copy in copies:
        copy.start()
    win_two_ref[...] = jnp.zeros_like(win_two_ref)
    wout_two_ref[...] = jnp.zeros_like(wout_two_ref)
    copies[0].wait()
    kblocks = blocks_ref.shape[0]
    count = kblocks * BLK
    rows = field_ref.shape[0]
    index = lax.axis_index("grid")
    base = jnp.concatenate(
        [jnp.full((BLK, LANES), blocks_ref[b] * BLK, jnp.int32) for b in range(kblocks)], axis=0
    )
    modes = base + row_id((count, LANES)) % BLK
    lane = lax.broadcasted_iota(jnp.int32, (count, LANES), 1)
    scale = 1.0 / math.sqrt(NX)
    near_c, near_s = cos_sin((modes * lane) & (NX - 1))
    near_c, near_s = near_c * scale, near_s * scale
    far_c, far_s = cos_sin((modes * (index * rows + lane * LANES)) & (NX - 1))
    for a in range(rows // LANES):
        ca = jnp.broadcast_to(far_c[:, a : a + 1], (count, LANES))
        sa = jnp.broadcast_to(far_s[:, a : a + 1], (count, LANES))
        span = pl.ds(a * LANES, LANES)
        table_ref[:count, span] = (near_c * ca - near_s * sa).astype(BF16)
        table_ref[count:, span] = (-(near_s * ca + near_c * sa)).astype(BF16)
    copies[1].wait()
    modal = dot(table_ref[...], field_ref[...])
    wide_ref[pl.ds(0, count, stride=2), :] = modal[:count]
    wide_ref[pl.ds(1, count, stride=2), :] = modal[count:]
    modal_ref[...] = wide_ref[...].astype(BF16)
    zero_row_ref[...] = jnp.where(modes == 0, 1.0, 0.0)
    at = jnp.int32(0)
    for b in range(kblocks):
        at = jnp.where(blocks_ref[b] == 0, b * BLK, at)
    own = jnp.full((TILE, LANES), index, jnp.int32)
    zero_own_ref[...] = jnp.where(own == at, 1.0, 0.0)
    for copy in copies[2:]:
        copy.wait()
    s_re, s_im = twice_diag(s_ref[0]), twice_diag(s_ref[1])
    mix_ref[...] = jnp.concatenate([s_re, s_im], axis=1)
    back_ref[...] = jnp.concatenate([s_re, s_im], axis=0)
    chans, hid = win_ref.shape
    for two_ref, one_ref in ((win_two_ref, win_ref), (wout_two_ref, wout_ref)):
        two_ref[:chans, :hid] = one_ref[...]
        two_ref[chans:, hid:] = one_ref[...]
    bin_two_ref[...] = jnp.concatenate([bin_ref[...]] * 2, axis=1)
    bout_two_ref[...] = jnp.concatenate([bout_ref[...]] * 2, axis=1)


def complex_rows(x, weights, axis, sign):
    high = x.astype(BF16).astype(F32)
    rest = x - high
    mid = rest.astype(BF16).astype(F32)
    low = rest - mid
    row = row_id(x.shape)
    left = jnp.where(row < 2, high, jnp.where(row < 4, mid, jnp.where(row < 6, low, 0.0)))
    dims = (((1,), (axis,)), ((), ()))
    y = lax.dot_general(left.astype(BF16), weights, dims, preferred_element_type=F32)
    y = y + pltpu.roll(y, 4, 0)
    y = y + pltpu.roll(y, 2, 0)
    by_re = y[:, :LANES]
    by_im = pltpu.roll(y[:, LANES:], 1, 0)
    return by_re + jnp.where(row % 2 == 0, sign, -sign) * by_im


def mix_kernel(recv_ref, weights_ref, out_ref, sum_ref):
    x = jnp.sum(recv_ref[...].astype(F32).reshape(-1, TILE, LANES), axis=0)
    x = x + pltpu.roll(x, 4, 0)
    x = x + pltpu.roll(x, 2, 0)
    sum_ref[...] = x
    mixed = complex_rows(x, weights_ref[...], 0, -1.0)
    out_ref[...] = jnp.concatenate([mixed] * (out_ref.shape[0] // TILE), axis=0).astype(BF16)


def gelu_pair(pre):
    k = math.sqrt(2.0 / math.pi)
    inner = k + (0.044715 * k) * (pre * pre)
    share = 0.5 * jnp.tanh(pre * inner) + 0.5
    gate = pre * share
    return gate, share + gate * (1.0 - share) * (6.0 * inner - 4.0 * k)


def cells_kernel(
    chunk,
    piece_ref,
    table_ref,
    field_ref,
    cot_ref,
    win_ref,
    bin_ref,
    wout_t_ref,
    bout_ref,
    zero_row_ref,
    out_hbm,
    parts_ref,
    wide_ref,
    hidden_ref,
    gpre_ref,
    out_ref,
    sums_ref,
    out_sems,
):
    rows = field_ref.shape[0]
    count = table_ref.shape[0] // 2
    hid = bin_ref.shape[1] // 2
    chans = LANES // 2
    wide_ref[...] = 2.0 * piece_ref[...].astype(F32)
    mixed = jnp.concatenate([every(wide_ref, 0, count, 2), every(wide_ref, 1, count, 2)], axis=0)
    right = stack_parts(dot(mixed.astype(BF16), win_ref[...]))
    copies = []
    for i in range(rows // chunk):
        span = pl.ds(i * chunk, chunk)
        table = table_ref[:, span]
        pre = dot_on(jnp.concatenate([table, table], axis=0), right, 0, 0) + bin_ref[...]
        gate, slope = gelu_pair(pre)
        hidden = gate.astype(BF16)
        hidden_ref[span, :] = hidden
        gpre_ref[span, :] = (dot(cot_ref[span, :], wout_t_ref[...]) * slope).astype(BF16)
        out = dot_on(hidden, wout_t_ref[...], 1, 1) + bout_ref[...]
        out_ref[span, :] = (field_ref[span, :].astype(F32) + out).astype(BF16)
        copies.append(pltpu.make_async_copy(out_ref.at[span], out_hbm.at[span], out_sems.at[i]))
        copies[-1].start()
    ones = jnp.ones((2 * TILE, rows), BF16)
    t = dot(jnp.concatenate([table_ref[...], ones], axis=0), gpre_ref[...])
    by_out = dot_on(cot_ref[...], hidden_ref[...], 0, 0)
    sums_out = dot(ones, cot_ref[...])
    b_in = t[2 * count : 2 * count + 1]
    t_parts = stack_parts(t[: 2 * count])
    grad_modal = dot_on(t_parts, win_ref[...], 1, 1)
    grad_modal = 2.0 * (grad_modal[: 2 * count] + grad_modal[2 * count :])
    mixed_t = mixed.T.astype(BF16)
    by_in = dot(jnp.concatenate([mixed_t, mixed_t], axis=1), t_parts)
    g_in = by_in[:chans, :hid] + by_in[chans:, hid:]
    g_out = by_out[:chans, :hid] + by_out[chans:, hid:]
    b_in = b_in[:, :hid] + b_in[:, hid:]
    b_out = halves((sums_out + pltpu.roll(sums_out, chans, 1))[:1])
    for r, block in enumerate(
        (
            grad_modal[:count],
            jnp.where(zero_row_ref[...] > 0.0, b_out, grad_modal[count:]),
            g_in[:, :LANES],
            g_in[:, LANES:],
            g_out[:, :LANES],
            g_out[:, LANES:],
            jnp.broadcast_to(b_in[:, :LANES], (count, LANES)),
            jnp.broadcast_to(b_in[:, LANES:], (count, LANES)),
        )
    ):
        sums_ref[pl.ds(r, count, stride=TILE), :] = block
    parts_ref[...] = sums_ref[...].astype(BF16)
    for copy in copies:
        copy.wait()


def stack_parts(x):
    high, low = split(x)
    return jnp.concatenate([high, low], axis=0).astype(BF16)


def halves(x):
    high, low = split(x)
    lane = lax.broadcasted_iota(jnp.int32, x.shape, 1)
    return jnp.where(lane < LANES // 2, high, low)


def split(x):
    high = x.astype(BF16).astype(F32)
    return high, x - high


def share_kernel(recv_ref, modal_ref, weights_ref, zero_own_ref, share_ref, grad_in_ref):
    x = jnp.sum(recv_ref[...].astype(F32).reshape(-1, TILE, LANES), axis=0)
    row = row_id(x.shape)
    owner = zero_own_ref[...] > 0.0
    extra = jnp.where(owner & (row == 2), pltpu.roll(x, 1, 0), 0.0)
    x = jnp.where(owner & (row == 1), 0.0, x)
    both = jnp.concatenate([x, jnp.where(row < 2, modal_ref[...], extra)], axis=0)
    share_ref[...] = jnp.concatenate([both] * (share_ref.shape[0] // (2 * TILE)), axis=0)
    grad = jnp.concatenate([x[:2]] * (TILE // 2), axis=0)
    grad_in_ref[...] = complex_rows(grad, weights_ref[...], 1, 1.0)


def total_kernel(scale, shares_ref, grad_in_ref, zero_own_ref, out_ref):
    x = jnp.sum(shares_ref[...].reshape(-1, 2 * TILE, LANES), axis=0) * scale
    bias = x[TILE + 2 : TILE + 3]
    bias = halves(bias + pltpu.roll(bias, LANES // 2, 1))
    row = row_id((TILE, LANES))
    own = jnp.where(row < 2, grad_in_ref[...], x[:TILE])
    own = jnp.where((zero_own_ref[...] > 0.0) & (row == 1), bias, own)
    group = jnp.concatenate([own[:OWN]] * 4, axis=0)
    out_ref[...] = jnp.concatenate([group] * (out_ref.shape[0] // (4 * OWN)), axis=0).astype(BF16)


def final_kernel(
    scale,
    recv_ref,
    shares_ref,
    table_ref,
    cot_ref,
    zero_row_ref,
    fgrad_hbm,
    spectral_hbm,
    win_hbm,
    wout_hbm,
    bin_hbm,
    bout_hbm,
    wide_ref,
    fgrad_ref,
    spectral_ref,
    win_ref,
    wout_ref,
    bin_ref,
    bout_ref,
    sems,
):
    count = table_ref.shape[0] // 2
    half = table_ref.shape[1] // 2
    copies = []

    def send(source, target):
        copies.append(pltpu.make_async_copy(source, target, sems.at[len(copies)]))
        copies[-1].start()

    wide_ref[...] = recv_ref[...].astype(F32)
    rows = [every(wide_ref, r, count, OWN) for r in range(OWN)]
    grad_in = jnp.concatenate(rows[:2], axis=0).astype(BF16)
    for i in range(2):
        span = pl.ds(i * half, half)
        back = dot_on(table_ref[:, span], grad_in, 0, 0)
        fgrad_ref[span, :] = (cot_ref[span, :].astype(F32) + back).astype(BF16)
        send(fgrad_ref.at[span], fgrad_hbm.at[span])
    win_ref[:, :LANES] = rows[2]
    win_ref[:, LANES:] = rows[3]
    send(win_ref, win_hbm)
    wout_ref[:, :LANES] = rows[4]
    wout_ref[:, LANES:] = rows[5]
    send(wout_ref, wout_hbm)
    spectral_sums(scale, shares_ref, spectral_ref)
    send(spectral_ref, spectral_hbm)
    n = shares_ref.shape[0] // (2 * TILE)
    for r in range(2):
        b_in = jnp.sum(every(shares_ref, OWN + r, n, 2 * TILE), axis=0, keepdims=True)
        bin_ref[:, r * LANES : (r + 1) * LANES] = b_in * scale
    send(bin_ref, bin_hbm)
    b_out = jnp.sum(jnp.where(zero_row_ref[...] > 0.0, rows[1], 0.0), axis=0, keepdims=True)
    bout_ref[...] = (b_out + pltpu.roll(b_out, LANES // 2, 1))[:, : bout_ref.shape[1]]
    send(bout_ref, bout_hbm)
    for copy in copies:
        copy.wait()


def spectral_sums(scale, shares_ref, out_ref):
    n = shares_ref.shape[0] // (2 * TILE)
    d_re, d_im, u_re, u_im = (every(shares_ref, r, n, 2 * TILE) for r in (0, 1, TILE, TILE + 1))
    left_high, left_low = split(jnp.concatenate([u_re, u_im], axis=0))
    right_high, right_low = split(
        jnp.concatenate(
            [jnp.concatenate([d_re, d_im], axis=0), jnp.concatenate([d_im, -d_re], axis=0)], axis=1
        )
    )
    left = jnp.concatenate([left_high, left_high, left_low], axis=0).astype(BF16)
    right = jnp.concatenate([right_high, right_low, right_high], axis=0).astype(BF16)
    outer = lax.dot_general(left, right, (((0,), (0,)), ((), ())), preferred_element_type=F32)
    c = LANES // 2
    out_ref[0] = (outer[:c, :c] + outer[c:, c : 2 * c]) * scale
    out_ref[1] = (outer[:c, 2 * c : 3 * c] + outer[c:, 3 * c :]) * scale


def exchange(x, axis):
    return lax.all_to_all(x, axis, 0, 0, tiled=True)


def exchange_pairs(x, axis):
    n = x.shape[0] // 2
    return exchange(x.reshape(n, 2, LANES), axis).reshape(2 * n, LANES)


def exchange_tiles(x, axis):
    n = x.shape[0] // TILE
    return exchange(x.reshape(n, TILE, LANES), axis).reshape(TILE * n, LANES)


def local(field, cotangent, mode_blocks, spectral, w_in, b_in, w_out, b_out):
    rows, width = field.shape
    chans, hid = w_in.shape
    ncol = width // chans
    grid = lax.axis_size("grid")
    dp = lax.axis_size("dp")
    inv_cols = 1.0 / (ncol * dp)
    count = mode_blocks.shape[0] * BLK

    sources = (
        mode_blocks,
        field,
        spectral.reshape(2, chans, chans),
        w_in,
        w_out.T,
        b_in.reshape(1, hid),
        b_out.reshape(1, chans),
        cotangent,
    )
    (
        modal,
        table,
        field_here,
        cotangent_here,
        mix_weights,
        back_weights,
        w_in_two,
        w_out_two,
        b_in_two,
        b_out_two,
        zero_row,
        zero_own,
    ) = call(
        first_kernel,
        "first",
        [
            ((2 * count, width), BF16),
            ((2 * count, rows), BF16),
            ((rows, width), BF16),
            ((rows, width), BF16),
            ((width, 2 * width), BF16),
            ((2 * width, width), BF16),
            ((width, 2 * hid), BF16),
            ((width, 2 * hid), BF16),
            ((1, 2 * hid), F32),
            ((1, width), F32),
            ((count, width), F32),
            ((TILE, width), F32),
        ],
        [HBM] * len(sources),
        [pltpu.SMEM(mode_blocks.shape, jnp.int32)]
        + [pltpu.VMEM(a.shape, a.dtype) for a in sources[2:7]]
        + [pltpu.VMEM((2 * count, width), F32), pltpu.SemaphoreType.DMA((len(sources),))],
    )(*(pltpu.with_memory_space_constraint(a, pltpu.HBM) for a in sources))
    mixed, modal_sum = call(
        mix_kernel, "mix", [((2 * grid, width), BF16), ((TILE, width), F32)], [VMEM] * 2
    )(exchange_pairs(modal, "grid"), mix_weights)
    piece = exchange_pairs(mixed, "grid")

    output, parts = call(
        functools.partial(cells_kernel, 256),
        "cells",
        [((rows, width), BF16, HBM), ((TILE * grid, width), BF16)],
        [VMEM] * 9,
        [
            pltpu.VMEM((2 * count, width), F32),
            pltpu.VMEM((rows, 2 * hid), BF16),
            pltpu.VMEM((rows, 2 * hid), BF16),
            pltpu.VMEM((rows, width), BF16),
            pltpu.VMEM((TILE * grid, width), F32),
            pltpu.SemaphoreType.DMA((rows // 256,)),
        ],
    )(
        piece,
        table,
        field_here,
        cotangent_here,
        w_in_two,
        b_in_two,
        w_out_two,
        b_out_two,
        zero_row,
    )
    share, grad_in = call(
        share_kernel, "share", [((2 * TILE * dp, width), F32), ((TILE, width), F32)], [VMEM] * 4
    )(exchange_tiles(parts, "grid"), modal_sum, back_weights, zero_own)
    shares = exchange(share, "dp")
    (own,) = call(
        functools.partial(total_kernel, inv_cols), "total", [((OWN * grid, width), BF16)], [VMEM] * 3
    )(shares, grad_in, zero_own)
    results = [
        ((rows, width), BF16),
        ((2, chans, chans), F32),
        ((chans, hid), F32),
        ((chans, hid), F32),
        ((1, hid), F32),
        ((1, chans), F32),
    ]
    field_grad, spectral_grad, w_in_grad, w_out_grad, b_in_grad, b_out_grad = call(
        functools.partial(final_kernel, inv_cols),
        "final",
        [(shape, dtype, HBM) for shape, dtype in results],
        [VMEM] * 5,
        [pltpu.VMEM((OWN * grid, width), F32)]
        + [pltpu.VMEM(shape, dtype) for shape, dtype in results]
        + [pltpu.SemaphoreType.DMA((len(results) + 1,))],
    )(exchange_pairs(own, "grid"), shares, table, cotangent_here, zero_row)
    return (
        output,
        field_grad,
        spectral_grad.reshape(2, 1, chans, chans),
        w_in_grad,
        b_in_grad.reshape(hid),
        w_out_grad.T,
        b_out_grad.reshape(chans),
    )


def solution(mesh):
    in_specs = (
        P("grid", "dp"),
        P("grid", "dp"),
        P(),
        P(None, "grid", None, None),
        P(),
        P(),
        P(),
        P(),
    )
    out_specs = (P("grid", "dp"), P("grid", "dp"), P(None, "grid", None, None), P(), P(), P(), P())
    return jax.shard_map(local, mesh=mesh, in_specs=in_specs, out_specs=out_specs, check_vma=False)
```

```python
import functools
import math

import jax
import jax.numpy as jnp
from jax import lax
from jax.experimental import pallas as pl
from jax.experimental.pallas import tpu as pltpu
from jax.sharding import PartitionSpec as P

NX = 65536
BLK = 8
LANES = 128
TILE = 8
F32 = jnp.float32
BF16 = jnp.bfloat16
VMEM = pl.BlockSpec(memory_space=pltpu.VMEM)
HBM = pl.BlockSpec(memory_space=pltpu.HBM)
OWN = 6


def call(kernel, name, outs, specs, scratch=()):
    return pl.pallas_call(
        kernel,
        name=name,
        out_shape=[jax.ShapeDtypeStruct(o[0], o[1]) for o in outs],
        in_specs=specs,
        out_specs=[o[2] if len(o) > 2 else VMEM for o in outs],
        scratch_shapes=list(scratch),
        compiler_params=pltpu.CompilerParams(vmem_limit_bytes=48 << 20),
    )


def dot(a, b):
    return jnp.dot(a, b, preferred_element_type=F32)


def dot_on(a, b, over_a, over_b):
    return lax.dot_general(a, b, (((over_a,), (over_b,)), ((), ())), preferred_element_type=F32)


def row_id(shape):
    return lax.broadcasted_iota(jnp.int32, shape, 0)


def every(ref, start, count, step):
    return ref[pl.ds(start, count, stride=step), :]


def cos_sin(turn):
    quarter = NX // 4
    quad = (turn + quarter // 2) >> (quarter.bit_length() - 1)
    rest = (turn - quad * quarter).astype(F32) * (2.0 * math.pi / NX)
    sq = rest * rest
    sin = rest * (1.0 + sq * (-1 / 6 + sq * (1 / 120 + sq * (-1 / 5040 + sq * (1 / 362880)))))
    cos = 1.0 + sq * (
        -1 / 2 + sq * (1 / 24 + sq * (-1 / 720 + sq * (1 / 40320 + sq * (-1 / 3628800))))
    )
    odd = (quad & 1) == 1
    c = jnp.where(odd, sin, cos)
    s = jnp.where(odd, cos, sin)
    return jnp.where(((quad + 1) & 2) != 0, -c, c), jnp.where((quad & 2) != 0, -s, s)


def twice_diag(x):
    zero = jnp.zeros_like(x)
    return jnp.concatenate(
        [jnp.concatenate([x, zero], axis=1), jnp.concatenate([zero, x], axis=1)], axis=0
    )


def first_kernel(
    blocks_hbm,
    field_hbm,
    spectral_hbm,
    win_hbm,
    wout_hbm,
    bin_hbm,
    bout_hbm,
    modal_ref,
    table_ref,
    field_ref,
    mix_ref,
    back_ref,
    win_two_ref,
    wout_two_ref,
    bin_two_ref,
    bout_two_ref,
    zero_row_ref,
    zero_own_ref,
    blocks_ref,
    s_ref,
    win_ref,
    wout_ref,
    bin_ref,
    bout_ref,
    wide_ref,
    sems,
):
    pairs = (
        (blocks_hbm, blocks_ref),
        (field_hbm, field_ref),
        (spectral_hbm, s_ref),
        (win_hbm, win_ref),
        (wout_hbm, wout_ref),
        (bin_hbm, bin_ref),
        (bout_hbm, bout_ref),
    )
    copies = [pltpu.make_async_copy(a, b, sems.at[i]) for i, (a, b) in enumerate(pairs)]
    for copy in copies:
        copy.start()
    win_two_ref[...] = jnp.zeros_like(win_two_ref)
    wout_two_ref[...] = jnp.zeros_like(wout_two_ref)
    copies[0].wait()
    kblocks = blocks_ref.shape[0]
    count = kblocks * BLK
    rows = field_ref.shape[0]
    index = lax.axis_index("grid")
    base = jnp.concatenate(
        [jnp.full((BLK, LANES), blocks_ref[b] * BLK, jnp.int32) for b in range(kblocks)], axis=0
    )
    modes = base + row_id((count, LANES)) % BLK
    lane = lax.broadcasted_iota(jnp.int32, (count, LANES), 1)
    scale = 1.0 / math.sqrt(NX)
    near_c, near_s = cos_sin((modes * lane) & (NX - 1))
    near_c, near_s = near_c * scale, near_s * scale
    far_c, far_s = cos_sin((modes * (index * rows + lane * LANES)) & (NX - 1))
    for a in range(rows // LANES):
        ca = jnp.broadcast_to(far_c[:, a : a + 1], (count, LANES))
        sa = jnp.broadcast_to(far_s[:, a : a + 1], (count, LANES))
        span = pl.ds(a * LANES, LANES)
        table_ref[:count, span] = (near_c * ca - near_s * sa).astype(BF16)
        table_ref[count:, span] = (-(near_s * ca + near_c * sa)).astype(BF16)
    copies[1].wait()
    modal = dot(table_ref[...], field_ref[...])
    wide_ref[pl.ds(0, count, stride=2), :] = modal[:count]
    wide_ref[pl.ds(1, count, stride=2), :] = modal[count:]
    modal_ref[...] = wide_ref[...].astype(BF16)
    zero_row_ref[...] = jnp.where(modes == 0, 1.0, 0.0)
    at = jnp.int32(0)
    for b in range(kblocks):
        at = jnp.where(blocks_ref[b] == 0, b * BLK, at)
    own = jnp.full((TILE, LANES), index, jnp.int32)
    zero_own_ref[...] = jnp.where(own == at, 1.0, 0.0)
    for copy in copies[2:]:
        copy.wait()
    s_re, s_im = twice_diag(s_ref[0]), twice_diag(s_ref[1])
    mix_ref[...] = jnp.concatenate([s_re, s_im], axis=1)
    back_ref[...] = jnp.concatenate([s_re, s_im], axis=0)
    chans, hid = win_ref.shape
    for two_ref, one_ref in ((win_two_ref, win_ref), (wout_two_ref, wout_ref)):
        two_ref[:chans, :hid] = one_ref[...]
        two_ref[chans:, hid:] = one_ref[...]
    bin_two_ref[...] = jnp.concatenate([bin_ref[...]] * 2, axis=1)
    bout_two_ref[...] = jnp.concatenate([bout_ref[...]] * 2, axis=1)


def complex_rows(x, weights, axis, sign):
    high = x.astype(BF16).astype(F32)
    rest = x - high
    mid = rest.astype(BF16).astype(F32)
    low = rest - mid
    row = row_id(x.shape)
    left = jnp.where(row < 2, high, jnp.where(row < 4, mid, jnp.where(row < 6, low, 0.0)))
    dims = (((1,), (axis,)), ((), ()))
    y = lax.dot_general(left.astype(BF16), weights, dims, preferred_element_type=F32)
    y = y + pltpu.roll(y, 4, 0)
    y = y + pltpu.roll(y, 2, 0)
    by_re = y[:, :LANES]
    by_im = pltpu.roll(y[:, LANES:], 1, 0)
    return by_re + jnp.where(row % 2 == 0, sign, -sign) * by_im


def mix_kernel(recv_ref, weights_ref, out_ref, sum_ref):
    x = jnp.sum(recv_ref[...].astype(F32).reshape(-1, TILE, LANES), axis=0)
    x = x + pltpu.roll(x, 4, 0)
    x = x + pltpu.roll(x, 2, 0)
    sum_ref[...] = x
    mixed = complex_rows(x, weights_ref[...], 0, -1.0)
    out_ref[...] = jnp.concatenate([mixed] * (out_ref.shape[0] // TILE), axis=0).astype(BF16)


def gelu_pair(pre):
    k = math.sqrt(2.0 / math.pi)
    inner = k + (0.044715 * k) * (pre * pre)
    share = 0.5 * jnp.tanh(pre * inner) + 0.5
    gate = pre * share
    return gate, share + gate * (1.0 - share) * (6.0 * inner - 4.0 * k)


def cells_kernel(
    chunk,
    piece_ref,
    table_ref,
    field_ref,
    cot_ref,
    win_ref,
    bin_ref,
    wout_t_ref,
    bout_ref,
    zero_row_ref,
    out_hbm,
    parts_ref,
    wide_ref,
    hidden_ref,
    gpre_ref,
    out_ref,
    sums_ref,
    out_sems,
):
    rows = field_ref.shape[0]
    count = table_ref.shape[0] // 2
    hid = bin_ref.shape[1] // 2
    chans = LANES // 2
    wide_ref[...] = 2.0 * piece_ref[...].astype(F32)
    mixed = jnp.concatenate([every(wide_ref, 0, count, 2), every(wide_ref, 1, count, 2)], axis=0)
    right = stack_parts(dot(mixed.astype(BF16), win_ref[...]))
    copies = []
    for i in range(rows // chunk):
        span = pl.ds(i * chunk, chunk)
        table = table_ref[:, span]
        pre = dot_on(jnp.concatenate([table, table], axis=0), right, 0, 0) + bin_ref[...]
        gate, slope = gelu_pair(pre)
        hidden = gate.astype(BF16)
        hidden_ref[span, :] = hidden
        gpre_ref[span, :] = (dot(cot_ref[span, :], wout_t_ref[...]) * slope).astype(BF16)
        out = dot_on(hidden, wout_t_ref[...], 1, 1) + bout_ref[...]
        out_ref[span, :] = (field_ref[span, :].astype(F32) + out).astype(BF16)
        copies.append(pltpu.make_async_copy(out_ref.at[span], out_hbm.at[span], out_sems.at[i]))
        copies[-1].start()
    ones = jnp.ones((2 * TILE, rows), BF16)
    t = dot(jnp.concatenate([table_ref[...], ones], axis=0), gpre_ref[...])
    by_out = dot_on(cot_ref[...], hidden_ref[...], 0, 0)
    sums_out = dot(ones, cot_ref[...])
    b_in = t[2 * count : 2 * count + 1]
    t_parts = stack_parts(t[: 2 * count])
    grad_modal = dot_on(t_parts, win_ref[...], 1, 1)
    grad_modal = 2.0 * (grad_modal[: 2 * count] + grad_modal[2 * count :])
    mixed_t = mixed.T.astype(BF16)
    by_in = dot(jnp.concatenate([mixed_t, mixed_t], axis=1), t_parts)
    g_in = by_in[:chans, :hid] + by_in[chans:, hid:]
    g_out = by_out[:chans, :hid] + by_out[chans:, hid:]
    b_in = b_in[:, :hid] + b_in[:, hid:]
    b_out = halves((sums_out + pltpu.roll(sums_out, chans, 1))[:1])
    for r, block in enumerate(
        (
            grad_modal[:count],
            jnp.where(zero_row_ref[...] > 0.0, b_out, grad_modal[count:]),
            g_in[:, :LANES],
            g_in[:, LANES:],
            g_out[:, :LANES],
            g_out[:, LANES:],
            jnp.broadcast_to(b_in[:, :LANES], (count, LANES)),
            jnp.broadcast_to(b_in[:, LANES:], (count, LANES)),
        )
    ):
        sums_ref[pl.ds(r, count, stride=TILE), :] = block
    parts_ref[...] = sums_ref[...].astype(BF16)
    for copy in copies:
        copy.wait()


def stack_parts(x):
    high, low = split(x)
    return jnp.concatenate([high, low], axis=0).astype(BF16)


def halves(x):
    high, low = split(x)
    lane = lax.broadcasted_iota(jnp.int32, x.shape, 1)
    return jnp.where(lane < LANES // 2, high, low)


def split(x):
    high = x.astype(BF16).astype(F32)
    return high, x - high


def share_kernel(recv_ref, modal_ref, weights_ref, zero_own_ref, share_ref, grad_in_ref):
    x = jnp.sum(recv_ref[...].astype(F32).reshape(-1, TILE, LANES), axis=0)
    row = row_id(x.shape)
    owner = zero_own_ref[...] > 0.0
    extra = jnp.where(owner & (row == 2), pltpu.roll(x, 1, 0), 0.0)
    x = jnp.where(owner & (row == 1), 0.0, x)
    both = jnp.concatenate([x, jnp.where(row < 2, modal_ref[...], extra)], axis=0)
    share_ref[...] = jnp.concatenate([both] * (share_ref.shape[0] // (2 * TILE)), axis=0)
    grad = jnp.concatenate([x[:2]] * (TILE // 2), axis=0)
    grad_in_ref[...] = complex_rows(grad, weights_ref[...], 1, 1.0)


def total_kernel(scale, shares_ref, grad_in_ref, zero_own_ref, out_ref):
    x = jnp.sum(shares_ref[...].reshape(-1, 2 * TILE, LANES), axis=0) * scale
    bias = x[TILE + 2 : TILE + 3]
    bias = halves(bias + pltpu.roll(bias, LANES // 2, 1))
    row = row_id((TILE, LANES))
    own = jnp.where(row < 2, grad_in_ref[...], x[:TILE])
    own = jnp.where((zero_own_ref[...] > 0.0) & (row == 1), bias, own)
    group = jnp.concatenate([own[:OWN]] * 4, axis=0)
    out_ref[...] = jnp.concatenate([group] * (out_ref.shape[0] // (4 * OWN)), axis=0).astype(BF16)


def final_kernel(
    scale,
    recv_ref,
    shares_ref,
    table_ref,
    cot_ref,
    zero_row_ref,
    fgrad_ref,
    spectral_ref,
    win_ref,
    wout_ref,
    bin_ref,
    bout_ref,
    wide_ref,
):
    count = table_ref.shape[0] // 2
    wide_ref[...] = recv_ref[...].astype(F32)
    rows = [every(wide_ref, r, count, OWN) for r in range(OWN)]
    grad_in = jnp.concatenate(rows[:2], axis=0).astype(BF16)
    back = dot_on(table_ref[...], grad_in, 0, 0)
    fgrad_ref[...] = (cot_ref[...].astype(F32) + back).astype(BF16)
    win_ref[:, :LANES] = rows[2]
    win_ref[:, LANES:] = rows[3]
    wout_ref[:, :LANES] = rows[4]
    wout_ref[:, LANES:] = rows[5]
    n = shares_ref.shape[0] // (2 * TILE)
    for r in range(2):
        b_in = jnp.sum(every(shares_ref, OWN + r, n, 2 * TILE), axis=0, keepdims=True)
        bin_ref[:, r * LANES : (r + 1) * LANES] = b_in * scale
    b_out = jnp.sum(jnp.where(zero_row_ref[...] > 0.0, rows[1], 0.0), axis=0, keepdims=True)
    bout_ref[...] = (b_out + pltpu.roll(b_out, LANES // 2, 1))[:, : bout_ref.shape[1]]
    spectral_sums(scale, shares_ref, spectral_ref)


def spectral_sums(scale, shares_ref, out_ref):
    n = shares_ref.shape[0] // (2 * TILE)
    d_re, d_im, u_re, u_im = (every(shares_ref, r, n, 2 * TILE) for r in (0, 1, TILE, TILE + 1))
    left_high, left_low = split(jnp.concatenate([u_re, u_im], axis=0))
    right_high, right_low = split(
        jnp.concatenate(
            [jnp.concatenate([d_re, d_im], axis=0), jnp.concatenate([d_im, -d_re], axis=0)], axis=1
        )
    )
    left = jnp.concatenate([left_high, left_high, left_low], axis=0).astype(BF16)
    right = jnp.concatenate([right_high, right_low, right_high], axis=0).astype(BF16)
    outer = lax.dot_general(left, right, (((0,), (0,)), ((), ())), preferred_element_type=F32)
    c = LANES // 2
    out_ref[0] = (outer[:c, :c] + outer[c:, c : 2 * c]) * scale
    out_ref[1] = (outer[:c, 2 * c : 3 * c] + outer[c:, 3 * c :]) * scale


def exchange(x, axis):
    return lax.all_to_all(x, axis, 0, 0, tiled=True)


def exchange_pairs(x, axis):
    n = x.shape[0] // 2
    return exchange(x.reshape(n, 2, LANES), axis).reshape(2 * n, LANES)


def exchange_tiles(x, axis):
    n = x.shape[0] // TILE
    return exchange(x.reshape(n, TILE, LANES), axis).reshape(TILE * n, LANES)


def local(field, cotangent, mode_blocks, spectral, w_in, b_in, w_out, b_out):
    rows, width = field.shape
    chans, hid = w_in.shape
    ncol = width // chans
    grid = lax.axis_size("grid")
    dp = lax.axis_size("dp")
    inv_cols = 1.0 / (ncol * dp)
    count = mode_blocks.shape[0] * BLK

    sources = (
        mode_blocks,
        field,
        spectral.reshape(2, chans, chans),
        w_in,
        w_out.T,
        b_in.reshape(1, hid),
        b_out.reshape(1, chans),
    )
    (
        modal,
        table,
        field_here,
        mix_weights,
        back_weights,
        w_in_two,
        w_out_two,
        b_in_two,
        b_out_two,
        zero_row,
        zero_own,
    ) = call(
        first_kernel,
        "first",
        [
            ((2 * count, width), BF16),
            ((2 * count, rows), BF16),
            ((rows, width), BF16),
            ((width, 2 * width), BF16),
            ((2 * width, width), BF16),
            ((width, 2 * hid), BF16),
            ((width, 2 * hid), BF16),
            ((1, 2 * hid), F32),
            ((1, width), F32),
            ((count, width), F32),
            ((TILE, width), F32),
        ],
        [HBM] * len(sources),
        [pltpu.SMEM(mode_blocks.shape, jnp.int32)]
        + [pltpu.VMEM(a.shape, a.dtype) for a in sources[2:7]]
        + [pltpu.VMEM((2 * count, width), F32), pltpu.SemaphoreType.DMA((len(sources),))],
    )(*(pltpu.with_memory_space_constraint(a, pltpu.HBM) for a in sources))
    mixed, modal_sum = call(
        mix_kernel, "mix", [((2 * grid, width), BF16), ((TILE, width), F32)], [VMEM] * 2
    )(exchange_pairs(modal, "grid"), mix_weights)
    piece = exchange_pairs(mixed, "grid")

    output, parts = call(
        functools.partial(cells_kernel, 256),
        "cells",
        [((rows, width), BF16, HBM), ((TILE * grid, width), BF16)],
        [VMEM] * 9,
        [
            pltpu.VMEM((2 * count, width), F32),
            pltpu.VMEM((rows, 2 * hid), BF16),
            pltpu.VMEM((rows, 2 * hid), BF16),
            pltpu.VMEM((rows, width), BF16),
            pltpu.VMEM((TILE * grid, width), F32),
            pltpu.SemaphoreType.DMA((rows // 256,)),
        ],
    )(
        piece,
        table,
        field_here,
        cotangent,
        w_in_two,
        b_in_two,
        w_out_two,
        b_out_two,
        zero_row,
    )
    share, grad_in = call(
        share_kernel, "share", [((2 * TILE * dp, width), F32), ((TILE, width), F32)], [VMEM] * 4
    )(exchange_tiles(parts, "grid"), modal_sum, back_weights, zero_own)
    shares = exchange(share, "dp")
    (own,) = call(
        functools.partial(total_kernel, inv_cols), "total", [((OWN * grid, width), BF16)], [VMEM] * 3
    )(shares, grad_in, zero_own)
    field_grad, spectral_grad, w_in_grad, w_out_grad, b_in_grad, b_out_grad = call(
        functools.partial(final_kernel, inv_cols),
        "final",
        [
            ((rows, width), BF16),
            ((2, chans, chans), F32),
            ((chans, hid), F32),
            ((chans, hid), F32),
            ((1, hid), F32),
            ((1, chans), F32),
        ],
        [VMEM] * 5,
        [pltpu.VMEM((OWN * grid, width), F32)],
    )(exchange_pairs(own, "grid"), shares, table, cotangent, zero_row)
    return (
        output,
        field_grad,
        spectral_grad.reshape(2, 1, chans, chans),
        w_in_grad,
        b_in_grad.reshape(hid),
        w_out_grad.T,
        b_out_grad.reshape(chans),
    )


def solution(mesh):
    in_specs = (
        P("grid", "dp"),
        P("grid", "dp"),
        P(),
        P(None, "grid", None, None),
        P(),
        P(),
        P(),
        P(),
    )
    out_specs = (P("grid", "dp"), P("grid", "dp"), P(None, "grid", None, None), P(), P(), P(), P())
    return jax.shard_map(local, mesh=mesh, in_specs=in_specs, out_specs=out_specs, check_vma=False)
```

```python
import functools
import math

import jax
import jax.numpy as jnp
from jax import lax
from jax.experimental import pallas as pl
from jax.experimental.pallas import tpu as pltpu
from jax.sharding import PartitionSpec as P

NX = 65536
BLK = 8
LANES = 128
TILE = 8
F32 = jnp.float32
BF16 = jnp.bfloat16
VMEM = pl.BlockSpec(memory_space=pltpu.VMEM)
HBM = pl.BlockSpec(memory_space=pltpu.HBM)
OWN = 6


def call(kernel, name, outs, specs, scratch=()):
    return pl.pallas_call(
        kernel,
        name=name,
        out_shape=[jax.ShapeDtypeStruct(o[0], o[1]) for o in outs],
        in_specs=specs,
        out_specs=[o[2] if len(o) > 2 else VMEM for o in outs],
        scratch_shapes=list(scratch),
        compiler_params=pltpu.CompilerParams(vmem_limit_bytes=48 << 20),
    )


def dot(a, b):
    return jnp.dot(a, b, preferred_element_type=F32)


def dot_on(a, b, over_a, over_b):
    return lax.dot_general(a, b, (((over_a,), (over_b,)), ((), ())), preferred_element_type=F32)


def row_id(shape):
    return lax.broadcasted_iota(jnp.int32, shape, 0)


def every(ref, start, count, step):
    return ref[pl.ds(start, count, stride=step), :]


def cos_sin(turn):
    quarter = NX // 4
    quad = (turn + quarter // 2) >> (quarter.bit_length() - 1)
    rest = (turn - quad * quarter).astype(F32) * (2.0 * math.pi / NX)
    sq = rest * rest
    sin = rest * (1.0 + sq * (-1 / 6 + sq * (1 / 120 + sq * (-1 / 5040 + sq * (1 / 362880)))))
    cos = 1.0 + sq * (
        -1 / 2 + sq * (1 / 24 + sq * (-1 / 720 + sq * (1 / 40320 + sq * (-1 / 3628800))))
    )
    odd = (quad & 1) == 1
    c = jnp.where(odd, sin, cos)
    s = jnp.where(odd, cos, sin)
    return jnp.where(((quad + 1) & 2) != 0, -c, c), jnp.where((quad & 2) != 0, -s, s)


def twice_diag(x):
    zero = jnp.zeros_like(x)
    return jnp.concatenate(
        [jnp.concatenate([x, zero], axis=1), jnp.concatenate([zero, x], axis=1)], axis=0
    )


def first_kernel(
    blocks_hbm,
    field_hbm,
    spectral_hbm,
    win_hbm,
    wout_hbm,
    bin_hbm,
    bout_hbm,
    cot_hbm,
    modal_ref,
    table_ref,
    field_ref,
    cot_ref,
    mix_ref,
    back_ref,
    win_two_ref,
    wout_two_ref,
    bin_two_ref,
    bout_two_ref,
    zero_row_ref,
    zero_own_ref,
    blocks_ref,
    s_ref,
    win_ref,
    wout_ref,
    bin_ref,
    bout_ref,
    wide_ref,
    sems,
):
    pairs = (
        (blocks_hbm, blocks_ref),
        (field_hbm, field_ref),
        (spectral_hbm, s_ref),
        (win_hbm, win_ref),
        (wout_hbm, wout_ref),
        (bin_hbm, bin_ref),
        (bout_hbm, bout_ref),
        (cot_hbm, cot_ref),
    )
    copies = [pltpu.make_async_copy(a, b, sems.at[i]) for i, (a, b) in enumerate(pairs)]
    for copy in copies:
        copy.start()
    win_two_ref[...] = jnp.zeros_like(win_two_ref)
    wout_two_ref[...] = jnp.zeros_like(wout_two_ref)
    copies[0].wait()
    kblocks = blocks_ref.shape[0]
    count = kblocks * BLK
    rows = field_ref.shape[0]
    index = lax.axis_index("grid")
    base = jnp.concatenate(
        [jnp.full((BLK, LANES), blocks_ref[b] * BLK, jnp.int32) for b in range(kblocks)], axis=0
    )
    modes = base + row_id((count, LANES)) % BLK
    lane = lax.broadcasted_iota(jnp.int32, (count, LANES), 1)
    scale = 1.0 / math.sqrt(NX)
    near_c, near_s = cos_sin((modes * lane) & (NX - 1))
    near_c, near_s = near_c * scale, near_s * scale
    far_c, far_s = cos_sin((modes * (index * rows + lane * LANES)) & (NX - 1))
    for a in range(rows // LANES):
        ca = jnp.broadcast_to(far_c[:, a : a + 1], (count, LANES))
        sa = jnp.broadcast_to(far_s[:, a : a + 1], (count, LANES))
        span = pl.ds(a * LANES, LANES)
        table_ref[:count, span] = (near_c * ca - near_s * sa).astype(BF16)
        table_ref[count:, span] = (-(near_s * ca + near_c * sa)).astype(BF16)
    copies[1].wait()
    modal = dot(table_ref[...], field_ref[...])
    wide_ref[pl.ds(0, count, stride=2), :] = modal[:count]
    wide_ref[pl.ds(1, count, stride=2), :] = modal[count:]
    modal_ref[...] = wide_ref[...].astype(BF16)
    zero_row_ref[...] = jnp.where(modes == 0, 1.0, 0.0)
    at = jnp.int32(0)
    for b in range(kblocks):
        at = jnp.where(blocks_ref[b] == 0, b * BLK, at)
    own = jnp.full((TILE, LANES), index, jnp.int32)
    zero_own_ref[...] = jnp.where(own == at, 1.0, 0.0)
    for copy in copies[2:]:
        copy.wait()
    s_re, s_im = twice_diag(s_ref[0]), twice_diag(s_ref[1])
    mix_ref[...] = jnp.concatenate([s_re, s_im], axis=1)
    back_ref[...] = jnp.concatenate([s_re, s_im], axis=0)
    chans, hid = win_ref.shape
    for two_ref, one_ref in ((win_two_ref, win_ref), (wout_two_ref, wout_ref)):
        two_ref[:chans, :hid] = one_ref[...]
        two_ref[chans:, hid:] = one_ref[...]
    bin_two_ref[...] = jnp.concatenate([bin_ref[...]] * 2, axis=1)
    bout_two_ref[...] = jnp.concatenate([bout_ref[...]] * 2, axis=1)


def complex_rows(x, weights, axis, sign):
    high = x.astype(BF16).astype(F32)
    rest = x - high
    mid = rest.astype(BF16).astype(F32)
    low = rest - mid
    row = row_id(x.shape)
    left = jnp.where(row < 2, high, jnp.where(row < 4, mid, jnp.where(row < 6, low, 0.0)))
    dims = (((1,), (axis,)), ((), ()))
    y = lax.dot_general(left.astype(BF16), weights, dims, preferred_element_type=F32)
    y = y + pltpu.roll(y, 4, 0)
    y = y + pltpu.roll(y, 2, 0)
    by_re = y[:, :LANES]
    by_im = pltpu.roll(y[:, LANES:], 1, 0)
    return by_re + jnp.where(row % 2 == 0, sign, -sign) * by_im


def mix_kernel(recv_ref, weights_ref, out_ref, sum_ref):
    x = jnp.sum(recv_ref[...].astype(F32).reshape(-1, TILE, LANES), axis=0)
    x = x + pltpu.roll(x, 4, 0)
    x = x + pltpu.roll(x, 2, 0)
    sum_ref[...] = x
    mixed = complex_rows(x, weights_ref[...], 0, -1.0)
    out_ref[...] = jnp.concatenate([mixed] * (out_ref.shape[0] // TILE), axis=0).astype(BF16)


def gelu_pair(pre):
    k = math.sqrt(2.0 / math.pi)
    inner = k + (0.044715 * k) * (pre * pre)
    share = 0.5 * jnp.tanh(pre * inner) + 0.5
    gate = pre * share
    return gate, share + gate * (1.0 - share) * (6.0 * inner - 4.0 * k)


def cells_kernel(
    chunk,
    piece_ref,
    table_ref,
    field_ref,
    cot_ref,
    win_ref,
    bin_ref,
    wout_t_ref,
    bout_ref,
    zero_row_ref,
    out_hbm,
    parts_ref,
    wide_ref,
    hidden_ref,
    gpre_ref,
    out_ref,
    sums_ref,
    out_sems,
):
    rows = field_ref.shape[0]
    count = table_ref.shape[0] // 2
    hid = bin_ref.shape[1] // 2
    chans = LANES // 2
    wide_ref[...] = 2.0 * piece_ref[...].astype(F32)
    mixed = jnp.concatenate([every(wide_ref, 0, count, 2), every(wide_ref, 1, count, 2)], axis=0)
    right = stack_parts(dot(mixed.astype(BF16), win_ref[...]))
    copies = []
    for i in range(rows // chunk):
        span = pl.ds(i * chunk, chunk)
        table = table_ref[:, span]
        pre = dot_on(jnp.concatenate([table, table], axis=0), right, 0, 0) + bin_ref[...]
        gate, slope = gelu_pair(pre)
        hidden = gate.astype(BF16)
        hidden_ref[span, :] = hidden
        gpre_ref[span, :] = (dot(cot_ref[span, :], wout_t_ref[...]) * slope).astype(BF16)
        out = dot_on(hidden, wout_t_ref[...], 1, 1) + bout_ref[...]
        out_ref[span, :] = (field_ref[span, :].astype(F32) + out).astype(BF16)
        copies.append(pltpu.make_async_copy(out_ref.at[span], out_hbm.at[span], out_sems.at[i]))
        copies[-1].start()
    ones = jnp.ones((2 * TILE, rows), BF16)
    t = dot(jnp.concatenate([table_ref[...], ones], axis=0), gpre_ref[...])
    by_out = dot_on(cot_ref[...], hidden_ref[...], 0, 0)
    sums_out = dot(ones, cot_ref[...])
    b_in = t[2 * count : 2 * count + 1]
    t_parts = stack_parts(t[: 2 * count])
    grad_modal = dot_on(t_parts, win_ref[...], 1, 1)
    grad_modal = 2.0 * (grad_modal[: 2 * count] + grad_modal[2 * count :])
    mixed_t = mixed.T.astype(BF16)
    by_in = dot(jnp.concatenate([mixed_t, mixed_t], axis=1), t_parts)
    g_in = by_in[:chans, :hid] + by_in[chans:, hid:]
    g_out = by_out[:chans, :hid] + by_out[chans:, hid:]
    b_in = b_in[:, :hid] + b_in[:, hid:]
    b_out = halves((sums_out + pltpu.roll(sums_out, chans, 1))[:1])
    for r, block in enumerate(
        (
            grad_modal[:count],
            jnp.where(zero_row_ref[...] > 0.0, b_out, grad_modal[count:]),
            g_in[:, :LANES],
            g_in[:, LANES:],
            g_out[:, :LANES],
            g_out[:, LANES:],
            jnp.broadcast_to(b_in[:, :LANES], (count, LANES)),
            jnp.broadcast_to(b_in[:, LANES:], (count, LANES)),
        )
    ):
        sums_ref[pl.ds(r, count, stride=TILE), :] = block
    parts_ref[...] = sums_ref[...].astype(BF16)
    for copy in copies:
        copy.wait()


def stack_parts(x):
    high, low = split(x)
    return jnp.concatenate([high, low], axis=0).astype(BF16)


def halves(x):
    high, low = split(x)
    lane = lax.broadcasted_iota(jnp.int32, x.shape, 1)
    return jnp.where(lane < LANES // 2, high, low)


def split(x):
    high = x.astype(BF16).astype(F32)
    return high, x - high


def share_kernel(recv_ref, modal_ref, weights_ref, zero_own_ref, share_ref, grad_in_ref):
    x = jnp.sum(recv_ref[...].astype(F32).reshape(-1, TILE, LANES), axis=0)
    row = row_id(x.shape)
    owner = zero_own_ref[...] > 0.0
    extra = jnp.where(owner & (row == 2), pltpu.roll(x, 1, 0), 0.0)
    x = jnp.where(owner & (row == 1), 0.0, x)
    both = jnp.concatenate([x, jnp.where(row < 2, modal_ref[...], extra)], axis=0)
    share_ref[...] = jnp.concatenate([both] * (share_ref.shape[0] // (2 * TILE)), axis=0)
    grad = jnp.concatenate([x[:2]] * (TILE // 2), axis=0)
    grad_in_ref[...] = complex_rows(grad, weights_ref[...], 1, 1.0)


def total_kernel(scale, shares_ref, grad_in_ref, zero_own_ref, out_ref):
    x = jnp.sum(shares_ref[...].reshape(-1, 2 * TILE, LANES), axis=0) * scale
    bias = x[TILE + 2 : TILE + 3]
    bias = halves(bias + pltpu.roll(bias, LANES // 2, 1))
    row = row_id((TILE, LANES))
    own = jnp.where(row < 2, grad_in_ref[...], x[:TILE])
    own = jnp.where((zero_own_ref[...] > 0.0) & (row == 1), bias, own)
    group = jnp.concatenate([own[:OWN]] * 4, axis=0)
    out_ref[...] = jnp.concatenate([group] * (out_ref.shape[0] // (4 * OWN)), axis=0).astype(BF16)


def final_kernel(
    scale,
    recv_ref,
    shares_ref,
    table_ref,
    cot_ref,
    zero_row_ref,
    fgrad_ref,
    spectral_ref,
    win_ref,
    wout_ref,
    bin_ref,
    bout_ref,
    wide_ref,
):
    count = table_ref.shape[0] // 2
    wide_ref[...] = recv_ref[...].astype(F32)
    rows = [every(wide_ref, r, count, OWN) for r in range(OWN)]
    grad_in = jnp.concatenate(rows[:2], axis=0).astype(BF16)
    back = dot_on(table_ref[...], grad_in, 0, 0)
    fgrad_ref[...] = (cot_ref[...].astype(F32) + back).astype(BF16)
    win_ref[:, :LANES] = rows[2]
    win_ref[:, LANES:] = rows[3]
    wout_ref[:, :LANES] = rows[4]
    wout_ref[:, LANES:] = rows[5]
    n = shares_ref.shape[0] // (2 * TILE)
    for r in range(2):
        b_in = jnp.sum(every(shares_ref, OWN + r, n, 2 * TILE), axis=0, keepdims=True)
        bin_ref[:, r * LANES : (r + 1) * LANES] = b_in * scale
    b_out = jnp.sum(jnp.where(zero_row_ref[...] > 0.0, rows[1], 0.0), axis=0, keepdims=True)
    bout_ref[...] = (b_out + pltpu.roll(b_out, LANES // 2, 1))[:, : bout_ref.shape[1]]
    spectral_sums(scale, shares_ref, spectral_ref)


def spectral_sums(scale, shares_ref, out_ref):
    n = shares_ref.shape[0] // (2 * TILE)
    d_re, d_im, u_re, u_im = (every(shares_ref, r, n, 2 * TILE) for r in (0, 1, TILE, TILE + 1))
    left_high, left_low = split(jnp.concatenate([u_re, u_im], axis=0))
    right_high, right_low = split(
        jnp.concatenate(
            [jnp.concatenate([d_re, d_im], axis=0), jnp.concatenate([d_im, -d_re], axis=0)], axis=1
        )
    )
    left = jnp.concatenate([left_high, left_high, left_low], axis=0).astype(BF16)
    right = jnp.concatenate([right_high, right_low, right_high], axis=0).astype(BF16)
    outer = lax.dot_general(left, right, (((0,), (0,)), ((), ())), preferred_element_type=F32)
    c = LANES // 2
    out_ref[0] = (outer[:c, :c] + outer[c:, c : 2 * c]) * scale
    out_ref[1] = (outer[:c, 2 * c : 3 * c] + outer[c:, 3 * c :]) * scale


def exchange(x, axis):
    return lax.all_to_all(x, axis, 0, 0, tiled=True)


def exchange_pairs(x, axis):
    n = x.shape[0] // 2
    return exchange(x.reshape(n, 2, LANES), axis).reshape(2 * n, LANES)


def exchange_tiles(x, axis):
    n = x.shape[0] // TILE
    return exchange(x.reshape(n, TILE, LANES), axis).reshape(TILE * n, LANES)


def local(field, cotangent, mode_blocks, spectral, w_in, b_in, w_out, b_out):
    rows, width = field.shape
    chans, hid = w_in.shape
    ncol = width // chans
    grid = lax.axis_size("grid")
    dp = lax.axis_size("dp")
    inv_cols = 1.0 / (ncol * dp)
    count = mode_blocks.shape[0] * BLK

    sources = (
        mode_blocks,
        field,
        spectral.reshape(2, chans, chans),
        w_in,
        w_out.T,
        b_in.reshape(1, hid),
        b_out.reshape(1, chans),
        cotangent,
    )
    (
        modal,
        table,
        field_here,
        cotangent_here,
        mix_weights,
        back_weights,
        w_in_two,
        w_out_two,
        b_in_two,
        b_out_two,
        zero_row,
        zero_own,
    ) = call(
        first_kernel,
        "first",
        [
            ((2 * count, width), BF16),
            ((2 * count, rows), BF16),
            ((rows, width), BF16),
            ((rows, width), BF16),
            ((width, 2 * width), BF16),
            ((2 * width, width), BF16),
            ((width, 2 * hid), BF16),
            ((width, 2 * hid), BF16),
            ((1, 2 * hid), F32),
            ((1, width), F32),
            ((count, width), F32),
            ((TILE, width), F32),
        ],
        [HBM] * len(sources),
        [pltpu.SMEM(mode_blocks.shape, jnp.int32)]
        + [pltpu.VMEM(a.shape, a.dtype) for a in sources[2:7]]
        + [pltpu.VMEM((2 * count, width), F32), pltpu.SemaphoreType.DMA((len(sources),))],
    )(*(pltpu.with_memory_space_constraint(a, pltpu.HBM) for a in sources))
    mixed, modal_sum = call(
        mix_kernel, "mix", [((2 * grid, width), BF16), ((TILE, width), F32)], [VMEM] * 2
    )(exchange_pairs(modal, "grid"), mix_weights)
    piece = exchange_pairs(mixed, "grid")

    output, parts = call(
        functools.partial(cells_kernel, 1024),
        "cells",
        [((rows, width), BF16, HBM), ((TILE * grid, width), BF16)],
        [VMEM] * 9,
        [
            pltpu.VMEM((2 * count, width), F32),
            pltpu.VMEM((rows, 2 * hid), BF16),
            pltpu.VMEM((rows, 2 * hid), BF16),
            pltpu.VMEM((rows, width), BF16),
            pltpu.VMEM((TILE * grid, width), F32),
            pltpu.SemaphoreType.DMA((rows // 1024,)),
        ],
    )(
        piece,
        table,
        field_here,
        cotangent_here,
        w_in_two,
        b_in_two,
        w_out_two,
        b_out_two,
        zero_row,
    )
    share, grad_in = call(
        share_kernel, "share", [((2 * TILE * dp, width), F32), ((TILE, width), F32)], [VMEM] * 4
    )(exchange_tiles(parts, "grid"), modal_sum, back_weights, zero_own)
    shares = exchange(share, "dp")
    (own,) = call(
        functools.partial(total_kernel, inv_cols), "total", [((OWN * grid, width), BF16)], [VMEM] * 3
    )(shares, grad_in, zero_own)
    field_grad, spectral_grad, w_in_grad, w_out_grad, b_in_grad, b_out_grad = call(
        functools.partial(final_kernel, inv_cols),
        "final",
        [
            ((rows, width), BF16),
            ((2, chans, chans), F32),
            ((chans, hid), F32),
            ((chans, hid), F32),
            ((1, hid), F32),
            ((1, chans), F32),
        ],
        [VMEM] * 5,
        [pltpu.VMEM((OWN * grid, width), F32)],
    )(exchange_pairs(own, "grid"), shares, table, cotangent_here, zero_row)
    return (
        output,
        field_grad,
        spectral_grad.reshape(2, 1, chans, chans),
        w_in_grad,
        b_in_grad.reshape(hid),
        w_out_grad.T,
        b_out_grad.reshape(chans),
    )


def solution(mesh):
    in_specs = (
        P("grid", "dp"),
        P("grid", "dp"),
        P(),
        P(None, "grid", None, None),
        P(),
        P(),
        P(),
        P(),
    )
    out_specs = (P("grid", "dp"), P("grid", "dp"), P(None, "grid", None, None), P(), P(), P(), P())
    return jax.shard_map(local, mesh=mesh, in_specs=in_specs, out_specs=out_specs, check_vma=False)
```
